256 devices in a mesh: section: 2 (over core), seq: 16 (over x, y), tensor: 8 (over z).
Axes of the slice: x: 4, y: 4, z: 8, core: 2. Of those that a mesh axis runs over, the one named last changes fastest.
Arguments:
- x_in: bfloat16 [2, 32768, 2048], P(None, 'seq', 'tensor'), may hold values from -6 to 6
- norm_gain: float32 [2, 2048], P('section', 'tensor'), may hold values from 0.5 to 1.5
- right_blocks: bfloat16 [2, 128, 256, 256], P('section', 'seq'), may hold values from -0.375 to 0.375
- left_blocks: bfloat16 [2, 256, 128, 128], P('section', 'seq'), may hold values from -0.5 to 0.5
- gate_first: bfloat16 [2, 32, 64, 64], P('section'), may hold values from -0.75 to 0.75
- gate_second: bfloat16 [2, 64, 32, 32], P('section'), may hold values from -1 to 1
- out_first: bfloat16 [2, 32, 64, 64], P('section'), may hold values from -0.75 to 0.75
- out_second: bfloat16 [2, 64, 32, 32], P('section'), may hold values from -1 to 1
- head: bfloat16 [2, 2048, 32768], P('section', None, ('seq', 'tensor')), may hold values from -0.375 to 0.375
- targets: int32 [2, 256], replicated, may hold values from 0 to 32767
Outputs:
- block_out: bfloat16 [2, 2, 32768, 2048], P('section', None, 'seq', 'tensor')
- aux_losses: float32 [2, 2, 256], P('section')
The draws below stay inside these ranges and needn't reach their ends.
All inputs are finite; a program needn't handle non-finite values.
Results may differ from the reference program's by a relative error of at most 0.011.
Values may be sent and summed in bfloat16 or wider, within the bound.
No kernel may reach another device: no remote copies, remote signals or barrier semaphores. Data moves between devices by JAX's collectives and lax.ppermute only.
A program may use at most 128 MiB of HBM per device.

```python
import jax
import jax.numpy as jnp
from jax import lax

C1 = 32
C2 = 64
D = 2048
B1 = 128
B2 = 256
L = 32768
V = 32768
STRIDE = 128
P_SIZE = 256
M = 2


def place_ends(values, own_key, smallest, top_value):
    place = [jax.random.randint(jax.random.fold_in(own_key, axis), (), 0, length) for axis, length in enumerate(values.shape)]
    main_axis = values.shape.index(max(values.shape))
    next_to = place[:main_axis] + [(place[main_axis] + 1) % values.shape[main_axis]] + place[main_axis + 1:]
    return values.at[tuple(place)].set(smallest).at[tuple(next_to)].set(top_value)


def block_levels(rng, dims, split, least, largest):
    loudness, own = 1.0, jax.random.fold_in(rng, 6)
    for position, blocks in split:
        heights = jnp.exp(jax.random.uniform(jax.random.fold_in(own, position), (blocks,), jnp.float32, least / len(split), largest / len(split)))
        loudness = loudness * jnp.repeat(heights, dims[position] // blocks).reshape([-1 if axis == position else 1 for axis in range(len(dims))])
    return loudness


def centred(key, shape, width, reach, shards=(), dtype=jnp.bfloat16):
    level = block_levels(key, shape, shards, -0.22, 0.18) if shards else 1.0
    entries = jax.random.normal(key, shape, jnp.float32) * width * level
    return jnp.minimum(jnp.maximum(entries, -reach), reach).astype(dtype)


def setup_inputs(seed: int = 0) -> dict:
    arg_keys = jax.random.split(jax.random.key(seed), 11)
    x_in = centred(arg_keys[0], (M, L, D), 1.0, 6.0, ((1, 16), (2, 8)))
    norm_gain = jnp.clip(0.5 + 1.0 * jax.random.uniform(arg_keys[1], (2, D), jnp.float32) ** block_levels(arg_keys[1], (2, D), ((0, 2), (1, 8)), -0.2, 0.2), 0.5, 1.5)
    right_blocks = centred(arg_keys[2], (2, B1, B2, B2), B2 ** -0.5, 0.375, ((0, 2), (1, 16)))
    left_blocks = centred(arg_keys[3], (2, B2, B1, B1), B1 ** -0.5, 0.5, ((0, 2), (1, 16)))
    gate_first = centred(arg_keys[4], (2, C1, C2, C2), C2 ** -0.5, 0.75, ((0, 2),))
    gate_second = centred(arg_keys[5], (2, C2, C1, C1), C1 ** -0.5, 1.0, ((0, 2),))
    out_first = centred(arg_keys[6], (2, C1, C2, C2), C2 ** -0.5, 0.75, ((0, 2),))
    out_second = centred(arg_keys[7], (2, C2, C1, C1), C1 ** -0.5, 1.0, ((0, 2),))
    head = centred(arg_keys[8], (2, D, V), (D // 9) ** -0.5, 0.375, ((0, 2), (2, 128)))
    targets = place_ends(jax.random.randint(arg_keys[9], (M, P_SIZE), 0, V), jax.random.fold_in(arg_keys[9], 1), 0, V - 1).astype(jnp.int32)
    return {"x_in": x_in, "norm_gain": norm_gain, "right_blocks": right_blocks, "left_blocks": left_blocks, "gate_first": gate_first, "gate_second": gate_second, "out_first": out_first, "out_second": out_second, "head": head, "targets": targets}


def channel_mix(values, first_factor, second_factor):
    token_count = values.shape[0]
    chan_view = values.reshape(token_count, C1, C2).astype(jnp.float32)
    inner_mix = jnp.einsum('rkl,trl->trk', first_factor.astype(jnp.float32), chan_view).astype(jnp.bfloat16)
    outer_mix = jnp.einsum('kir,trk->tik', second_factor.astype(jnp.float32), inner_mix.astype(jnp.float32)).astype(jnp.bfloat16)
    return outer_mix.reshape(token_count, C1 * C2)

def run_block(x_val, gain, right_local, left_local, gate_one, gate_two, out_one, out_two, head_local, labels):
    x_float = x_val.astype(jnp.float32)
    mean_square = lax.optimization_barrier(jnp.mean(x_float * x_float, axis=1))
    normed = (x_float * jax.lax.rsqrt(mean_square + 1e-05)[:, None] * gain[None, :]).astype(jnp.bfloat16)
    seq_view = normed.reshape(B1, B2, D).astype(jnp.float32)
    row_mix = jnp.einsum('pjq,pqc->pjc', right_local.astype(jnp.float32), seq_view).astype(jnp.bfloat16)
    seq_out = jnp.einsum('jip,pjc->ijc', left_local.astype(jnp.float32), row_mix.astype(jnp.float32)).astype(jnp.bfloat16)
    seq_out = seq_out.reshape(L, D)
    gate_pre = channel_mix(normed, gate_one, gate_two)
    gated_mix = (seq_out.astype(jnp.float32) * jax.nn.sigmoid(gate_pre.astype(jnp.float32))).astype(jnp.bfloat16)
    out_pre = channel_mix(gated_mix, out_one, out_two)
    result = (x_float + out_pre.astype(jnp.float32)).astype(jnp.bfloat16)
    scored = result[::STRIDE]
    logits = jnp.dot(scored, head_local, preferred_element_type=jnp.float32)
    log_total = jnp.log(lax.optimization_barrier(jnp.sum(jnp.exp(logits), axis=1)))
    target_logit = jnp.take_along_axis(logits, labels[:, None].astype(jnp.int32), axis=1)[:, 0]
    return (result, log_total - target_logit)

def reference(x_in, norm_gain, right_blocks, left_blocks, gate_first, gate_second, out_first, out_second, head, targets):
    outputs = [[], []]
    losses = [[], []]
    for micro_index in range(M):
        current = x_in[micro_index]
        for block_index in range(2):
            current, aux_loss = run_block(current, norm_gain[block_index], right_blocks[block_index], left_blocks[block_index], gate_first[block_index], gate_second[block_index], out_first[block_index], out_second[block_index], head[block_index], targets[micro_index])
            outputs[block_index].append(current)
            losses[block_index].append(aux_loss)
    block_out = jnp.stack([jnp.stack(outputs[0]), jnp.stack(outputs[1])])
    aux_losses = jnp.stack([jnp.stack(losses[0]), jnp.stack(losses[1])])
    return (block_out, aux_losses)
```

```python
import jax
import jax.numpy as jnp
from jax import lax
from jax.experimental import pallas as pl
from jax.experimental.pallas import tpu as pltpu
from jax.sharding import PartitionSpec as P

C1 = 32
C2 = 64
D = 2048
STRIDE = 128
EPS = 1e-05
BLK = 256
VMEM_LIMIT = 48 * 1024 * 1024


def params():
    return pltpu.CompilerParams(vmem_limit_bytes=VMEM_LIMIT)


def whole(shape):
    return pl.BlockSpec(shape, lambda *_: (0,) * len(shape))


def gather_by_exchange(block, axis):
    count = lax.axis_size(axis)
    copies = jnp.broadcast_to(block[None], (count,) + block.shape)
    return lax.all_to_all(copies, axis, split_axis=0, concat_axis=0, tiled=True)


def channel_map(first_t, second_rows, n_blk):
    def kernel(first_ref, second_ref, out_ref):
        first = first_ref[...].astype(jnp.float32)
        second = second_ref[...].astype(jnp.float32)
        out_ref[0] = (first * second[:, None, :]).astype(jnp.bfloat16).reshape(D, BLK)

    return pl.pallas_call(
        kernel,
        grid=(n_blk,),
        in_specs=[whole((C1, C2, BLK)), pl.BlockSpec((C1, BLK), lambda n: (0, n))],
        out_specs=pl.BlockSpec((1, D, BLK), lambda n: (n, 0, 0)),
        out_shape=jax.ShapeDtypeStruct((n_blk, D, BLK), jnp.bfloat16),
        compiler_params=params(),
    )(first_t, second_rows)


def left_map(left_rows, j_count):
    rows, p_count = left_rows.shape
    cols = p_count * j_count

    def kernel(left_ref, out_ref):
        lane = lax.broadcasted_iota(jnp.int32, (p_count, cols), 1) // j_count
        spread = (lane == lax.broadcasted_iota(jnp.int32, (p_count, cols), 0)).astype(jnp.bfloat16)
        wide = jnp.dot(left_ref[...], spread, preferred_element_type=jnp.float32)
        same = (lax.broadcasted_iota(jnp.int32, (BLK, cols), 0) % j_count) == (
            lax.broadcasted_iota(jnp.int32, (BLK, cols), 1) % j_count
        )
        out_ref[...] = jnp.where(same, wide, 0.0).astype(jnp.bfloat16)

    return pl.pallas_call(
        kernel,
        grid=(rows // BLK,),
        in_specs=[pl.BlockSpec((BLK, p_count), lambda n: (n, 0))],
        out_specs=pl.BlockSpec((BLK, cols), lambda n: (n, 0)),
        out_shape=jax.ShapeDtypeStruct((rows, cols), jnp.bfloat16),
        compiler_params=params(),
    )(left_rows)


def norm_and_right(x_ref, gain_ref, right_ref, normed_ref, mix_ref):
    n_blk, tokens, _ = x_ref.shape
    total = jnp.zeros((tokens, 1), jnp.float32)
    for n in range(n_blk):
        xf = x_ref[n].astype(jnp.float32)
        total = total + jnp.sum(xf * xf, axis=1, keepdims=True)
    scale = lax.rsqrt(total / D + EPS)
    groups, _, width, _ = mix_ref.shape
    for n in range(n_blk):
        normed = (x_ref[n].astype(jnp.float32) * scale * gain_ref[n]).astype(jnp.bfloat16)
        normed_ref[n] = normed
        mix = jnp.dot(right_ref[...], normed, preferred_element_type=jnp.float32)
        mix_ref[:, n] = mix.astype(jnp.bfloat16).reshape(groups, width, BLK)


def first_stage(x_tok, gain, right_row, groups):
    n_blk, tokens, _ = x_tok.shape
    return pl.pallas_call(
        norm_and_right,
        out_shape=(
            jax.ShapeDtypeStruct(x_tok.shape, jnp.bfloat16),
            jax.ShapeDtypeStruct((groups, n_blk, tokens // groups, BLK), jnp.bfloat16),
        ),
        compiler_params=params(),
    )(x_tok, gain, right_row)


def gate_stage(normed, gate_map):
    n_blk, tokens, _ = normed.shape

    def kernel(normed_ref, map_ref, out_ref):
        acc = jnp.zeros((tokens, BLK), jnp.float32)
        for z in range(n_blk):
            acc = acc + jnp.dot(
                normed_ref[z], map_ref[0, z * BLK : (z + 1) * BLK], preferred_element_type=jnp.float32
            )
        out_ref[0] = jax.nn.sigmoid(acc.astype(jnp.bfloat16).astype(jnp.float32))

    return pl.pallas_call(
        kernel,
        grid=(n_blk,),
        in_specs=[whole(normed.shape), pl.BlockSpec((1, D, BLK), lambda n: (n, 0, 0))],
        out_specs=pl.BlockSpec((1, tokens, BLK), lambda n: (n, 0, 0)),
        out_shape=jax.ShapeDtypeStruct(normed.shape, jnp.float32),
        compiler_params=params(),
    )(normed, gate_map)


def left_stage(left_dense, mix):
    rows, cols = left_dense.shape

    def kernel(left_ref, mix_ref, out_ref):
        out_ref[...] = jnp.dot(
            left_ref[...], mix_ref[...], preferred_element_type=jnp.float32
        ).astype(jnp.bfloat16)

    return pl.pallas_call(
        kernel,
        grid=(rows // BLK,),
        in_specs=[pl.BlockSpec((BLK, cols), lambda n: (n, 0)), whole(mix.shape)],
        out_specs=pl.BlockSpec((BLK, BLK), lambda n: (n, 0)),
        out_shape=jax.ShapeDtypeStruct((rows, BLK), jnp.bfloat16),
        compiler_params=params(),
    )(left_dense, mix)


def out_stage(seq_out, gate, x_tok, out_map, following=None):
    groups, n_blk, width, _ = seq_out.shape
    tokens = groups * width

    def kernel(seq_ref, gate_ref, x_ref, map_ref, *refs):
        if following is None:
            res_ref, gated_ref = refs
        else:
            gain_ref, right_ref, res_ref, normed_ref, mix_ref, gated_ref = refs
        n = pl.program_id(0)

        @pl.when(n == 0)
        def _():
            for z in range(n_blk):
                seq = seq_ref[:, z].reshape(tokens, BLK).astype(jnp.float32)
                gated_ref[z] = (seq * gate_ref[z]).astype(jnp.bfloat16)

        acc = jnp.zeros((tokens, BLK), jnp.float32)
        for z in range(n_blk):
            acc = acc + jnp.dot(
                gated_ref[z], map_ref[0, z * BLK : (z + 1) * BLK], preferred_element_type=jnp.float32
            )
        mixed = acc.astype(jnp.bfloat16).astype(jnp.float32)
        res_ref[n] = (x_ref[n].astype(jnp.float32) + mixed).astype(jnp.bfloat16)
        if following is not None:

            @pl.when(n == n_blk - 1)
            def _():
                norm_and_right(res_ref, gain_ref, right_ref, normed_ref, mix_ref)

    tok_shape = (n_blk, tokens, BLK)
    in_specs = [
        whole(seq_out.shape),
        whole(tok_shape),
        whole(tok_shape),
        pl.BlockSpec((1, D, BLK), lambda n: (n, 0, 0)),
    ]
    out_shape = [jax.ShapeDtypeStruct(tok_shape, jnp.bfloat16)]
    operands = [seq_out, gate, x_tok, out_map]
    if following is not None:
        gain, right_row = following
        operands += [gain, right_row]
        in_specs += [whole(gain.shape), whole(right_row.shape)]
        out_shape += [
            jax.ShapeDtypeStruct(tok_shape, jnp.bfloat16),
            jax.ShapeDtypeStruct(seq_out.shape, jnp.bfloat16),
        ]
    return pl.pallas_call(
        kernel,
        grid=(n_blk,),
        in_specs=in_specs,
        out_specs=[whole(s.shape) for s in out_shape],
        out_shape=out_shape,
        scratch_shapes=[pltpu.VMEM(tok_shape, jnp.bfloat16)],
        compiler_params=params(),
    )(*operands)


def body(
    x_in,
    norm_gain,
    right_blocks,
    left_blocks,
    gate_first,
    gate_second,
    out_first,
    out_second,
    head,
    targets,
):
    section = lax.axis_index("section")
    tensor_index = lax.axis_index("tensor")
    seq_count = lax.axis_size("seq")
    n_blk = lax.axis_size("tensor")
    everyone = ("seq", "tensor")
    swap = [(0, 1), (1, 0)]
    tokens = right_blocks.shape[2]
    j_dev = left_blocks.shape[1]
    p_count = left_blocks.shape[2]

    x_own = lax.dynamic_index_in_dim(x_in, section, 0, keepdims=False)
    x_tok = lax.all_to_all(
        x_own.reshape(n_blk, tokens, BLK), "tensor", split_axis=0, concat_axis=0, tiled=True
    )

    gains = gather_by_exchange(norm_gain, ("section", "tensor")).reshape(2, n_blk, 1, BLK)

    def spread_first(factor):
        return jnp.tile(jnp.transpose(factor[0], (0, 2, 1)), (1, 1, BLK // C2))

    def rows_second(factor):
        return jnp.transpose(factor[0], (2, 1, 0)).reshape(C1, D)

    own = (
        lax.dynamic_index_in_dim(right_blocks[0], tensor_index, 0, keepdims=False),
        jnp.transpose(left_blocks[0], (1, 0, 2)).reshape(p_count * j_dev, p_count),
        spread_first(gate_first),
        rows_second(gate_second),
        spread_first(out_first),
        rows_second(out_second),
    )
    other = tuple(lax.ppermute(w, "section", swap) for w in own)
    weights = []
    for b in range(2):
        right_row, left_rows, g1, g2, o1, o2 = (
            jnp.where(section == b, a, c) for a, c in zip(own, other)
        )
        weights.append(
            (
                right_row,
                left_map(left_rows, j_dev),
                channel_map(g1, g2, n_blk),
                channel_map(o1, o2, n_blk),
            )
        )

    head_local = head[0]
    vocab_dev = head_local.shape[1]
    vocab_offset = lax.axis_index(everyone) * vocab_dev

    normed, mix = first_stage(x_tok, gains[0], weights[0][0], seq_count)
    current = x_tok
    results, rows = [], []
    for b in range(2):
        _, left_dense, gate_map, out_map = weights[b]
        mix_cols = lax.all_to_all(
            mix.reshape(seq_count * n_blk, j_dev, BLK),
            everyone,
            split_axis=0,
            concat_axis=0,
            tiled=True,
        )
        gate = gate_stage(normed, gate_map)
        col_out = left_stage(left_dense, mix_cols.reshape(p_count * j_dev, BLK))
        seq_out = lax.all_to_all(
            col_out.reshape(p_count, j_dev, BLK), everyone, split_axis=0, concat_axis=0, tiled=True
        ).reshape(seq_count, n_blk, j_dev, BLK)
        if b == 0:
            current, normed, mix = out_stage(
                seq_out, gate, current, out_map, (gains[1], weights[1][0])
            )
        else:
            (current,) = out_stage(seq_out, gate, current, out_map)
        scored = jnp.transpose(current[:, ::STRIDE], (1, 0, 2)).reshape(-1, D)
        near = gather_by_exchange(scored, "tensor").reshape(-1, D)
        rows.append(gather_by_exchange(near, "seq").reshape(-1, D))
        results.append(
            lax.all_to_all(current, "tensor", split_axis=0, concat_axis=0, tiled=True).reshape(
                n_blk * tokens, BLK
            )
        )

    first = section == 0
    got_rows = lax.ppermute(jnp.where(first, rows[1], rows[0]), "section", swap)
    own_rows = jnp.where(first, rows[0], rows[1])
    scored_all = jnp.where(
        first, jnp.concatenate([own_rows, got_rows]), jnp.concatenate([got_rows, own_rows])
    )
    logits = jnp.dot(scored_all, head_local, preferred_element_type=jnp.float32)
    exp_sums = jnp.sum(jnp.exp(logits), axis=1)
    vocab_ids = jnp.arange(vocab_dev, dtype=jnp.int32)[None, :] + vocab_offset
    is_target = vocab_ids == targets.reshape(-1)[:, None]
    target_part = jnp.sum(jnp.where(is_target, logits, 0.0), axis=1)
    parts = jnp.stack([exp_sums, target_part]).reshape(-1, 128)
    totals = jnp.sum(gather_by_exchange(parts, everyone), axis=0).reshape(2, -1)
    aux_losses = (jnp.log(totals[0]) - totals[1]).reshape(1, 2, -1)

    got = lax.ppermute(jnp.where(first, results[1], results[0]), "section", swap)
    kept = jnp.where(first, results[0], results[1])
    block_out = jnp.where(first, jnp.stack([kept, got]), jnp.stack([got, kept]))[None]
    return (block_out, aux_losses)


def solution(mesh):
    in_specs = (
        P(None, "seq", "tensor"),
        P("section", "tensor"),
        P("section", "seq", None, None),
        P("section", "seq", None, None),
        P("section", None, None, None),
        P("section", None, None, None),
        P("section", None, None, None),
        P("section", None, None, None),
        P("section", None, ("seq", "tensor")),
        P(),
    )
    out_specs = (P("section", None, "seq", "tensor"), P("section", None, None))
    return jax.shard_map(body, mesh=mesh, in_specs=in_specs, out_specs=out_specs, check_vma=False)
```

```python
import jax
import jax.numpy as jnp
from jax import lax
from jax.experimental import pallas as pl
from jax.experimental.pallas import tpu as pltpu
from jax.sharding import PartitionSpec as P

C1 = 32
C2 = 64
D = 2048
STRIDE = 128
EPS = 1e-05
BLK = 256
EXTRA = 16
VMEM_LIMIT = 48 * 1024 * 1024
F32 = jnp.float32
BF16 = jnp.bfloat16


def params():
    return pltpu.CompilerParams(vmem_limit_bytes=VMEM_LIMIT)


def whole(shape):
    return pl.BlockSpec(shape, lambda *_: (0,) * len(shape))


def scalar_spec():
    return pl.BlockSpec(memory_space=pltpu.SMEM)


def shape_of(shape, dtype=BF16):
    return jax.ShapeDtypeStruct(shape, dtype)


def dot(a, b):
    return jnp.dot(a, b, preferred_element_type=F32)


def gather_by_exchange(block, axis):
    count = lax.axis_size(axis)
    copies = jnp.broadcast_to(block[None], (count,) + block.shape)
    return lax.all_to_all(copies, axis, split_axis=0, concat_axis=0, tiled=True)


def xor_route(axis, mask):
    return [(i, i ^ mask) for i in range(lax.axis_size(axis))]


def sum_over(block, axis, masks):
    got = [lax.ppermute(block, axis, xor_route(axis, mask)) for mask in masks]
    if len(got) == 1:
        return block + got[0]
    return (block + got[0]) + (got[1] + got[2])


def squares_by_lane(x_blocks):
    ones = jnp.ones((8, BLK), BF16)
    dims = (((1,), (1,)), ((), ()))
    total = None
    for x in x_blocks:
        xf = x.astype(F32)
        square = xf * xf
        high = square.astype(BF16)
        low = (square - high.astype(F32)).astype(BF16)
        part = lax.dot_general(ones, high, dims, preferred_element_type=F32) + lax.dot_general(
            ones, low, dims, preferred_element_type=F32
        )
        total = part if total is None else total + part
    return total


def split_stage(x_own, tensor_index):
    rows, tokens, _ = x_own.shape

    def kernel(z_ref, x_ref, squares_ref, *send_refs):
        z = z_ref[0]
        row = lax.broadcasted_iota(jnp.int32, (8, tokens), 0)
        squares = jnp.zeros((8, tokens), F32)
        for p in range(rows):
            squares = jnp.where(row == p, squares_by_lane([x_ref[p]]), squares)
        squares_ref[...] = squares
        for d in range(rows):
            send_refs[d][...] = x_ref[(z + d) % rows]

    outs = [shape_of((rows, tokens), F32)] + [shape_of((tokens, BLK))] * rows
    return pl.pallas_call(
        kernel,
        in_specs=[scalar_spec(), whole(x_own.shape)],
        out_shape=outs,
        compiler_params=params(),
    )(tensor_index, x_own)


def right_stage(x_chan, squares, gain_local, right, groups):
    rows = right.shape[0]
    tokens = right.shape[1]
    width = tokens // groups
    operands = [x_chan, gain_local, right] + ([] if squares is None else [squares])

    def kernel(x_ref, gain_ref, right_ref, *refs):
        out_ref = refs[-1]
        for p in range(rows):
            if squares is None:
                extra = x_ref[p, tokens:].astype(F32)
                total = extra[0:1] + extra[1:2] + extra[2:3]
            else:
                total = refs[0][p : p + 1]
            scale = lax.rsqrt(total / D + EPS)
            scaled = (right_ref[p].astype(F32) * scale).astype(BF16)
            mix = dot(scaled, x_ref[p, :tokens]) * gain_ref[...]
            out_ref[:, p] = mix.astype(BF16).reshape(groups, width, BLK)

    return pl.pallas_call(
        kernel,
        out_shape=shape_of((groups, rows, width, BLK)),
        compiler_params=params(),
    )(*operands)


def left_stage(left, mix):
    j_count, i_count, p_count = left.shape

    half = BLK // 2

    def kernel(left_ref, mix_ref, out_ref, wide_ref, acc_ref):
        for h in range(2):
            wide_ref[h] = mix_ref[:, h * half : (h + 1) * half].astype(F32)
        for j in range(j_count):
            column = jnp.concatenate(
                [wide_ref[h, pl.ds(j, p_count, stride=j_count), :] for h in range(2)], axis=1
            ).astype(BF16)
            mixed = dot(left_ref[j], column)
            for h in range(2):
                acc_ref[h, pl.ds(j, i_count, stride=j_count), :] = mixed[:, h * half : (h + 1) * half]
        for h in range(2):
            out_ref[:, h * half : (h + 1) * half] = acc_ref[h].astype(BF16)

    return pl.pallas_call(
        kernel,
        out_shape=shape_of((i_count * j_count, BLK)),
        scratch_shapes=[
            pltpu.VMEM((2, p_count * j_count, half), F32),
            pltpu.VMEM((2, i_count * j_count, half), F32),
        ],
        compiler_params=params(),
    )(left, mix)


def channel_map(first, second_rows, n_blk):
    def kernel(first_ref, second_ref, out_ref, spread_ref):
        @pl.when(pl.program_id(0) == 0)
        def _():
            lane = lax.broadcasted_iota(jnp.int32, (C2, BLK), 1) % C2
            pick = (lane == lax.broadcasted_iota(jnp.int32, (C2, BLK), 0)).astype(BF16)
            for r in range(C1):
                spread_ref[r] = lax.dot_general(
                    first_ref[r], pick, (((0,), (0,)), ((), ())), preferred_element_type=F32
                ).astype(BF16)

        for r in range(C1):
            row = second_ref[r : r + 1].astype(F32)
            out_ref[0, r * C2 : (r + 1) * C2] = (spread_ref[r].astype(F32) * row).astype(BF16)

    return pl.pallas_call(
        kernel,
        grid=(n_blk,),
        in_specs=[whole((C1, C2, C2)), pl.BlockSpec((C1, BLK), lambda n: (0, n))],
        out_specs=pl.BlockSpec((1, D, BLK), lambda n: (n, 0, 0)),
        out_shape=shape_of((n_blk, D, BLK)),
        scratch_shapes=[pltpu.VMEM((C1, C2, BLK), BF16)],
        compiler_params=params(),
    )(first, second_rows)


def normalize(x_blocks, gain_ref, tokens, store):
    total = jnp.zeros((tokens, 1), F32)
    for x in x_blocks:
        xf = x.astype(F32)
        total = total + jnp.sum(xf * xf, axis=1, keepdims=True)
    scale = lax.rsqrt(total / D + EPS)
    for n, x in enumerate(x_blocks):
        store(n, (x.astype(F32) * scale * gain_ref[n]).astype(BF16))


def token_stage(received, gain, tensor_index):
    n_blk = len(received)
    tokens = received[0].shape[0]

    def kernel(z_ref, gain_ref, *refs):
        x_ref, normed_ref = refs[n_blk:]
        for d in range(n_blk):
            x_ref[(z_ref[0] + n_blk - d) % n_blk] = refs[d][...]

        def store(n, value):
            normed_ref[:, n * BLK : (n + 1) * BLK] = value

        normalize([x_ref[n] for n in range(n_blk)], gain_ref, tokens, store)

    return pl.pallas_call(
        kernel,
        in_specs=[scalar_spec(), whole(gain.shape)] + [whole((tokens, BLK))] * n_blk,
        out_shape=(shape_of((n_blk, tokens, BLK)), shape_of((tokens, D))),
        compiler_params=params(),
    )(tensor_index, gain, *received)


def gate_stage(normed, gate_map):
    tokens = normed.shape[0]
    n_blk = gate_map.shape[0]

    def kernel(normed_ref, map_ref, out_ref):
        pre = dot(normed_ref[...], map_ref[0]).astype(BF16)
        out_ref[0] = jax.nn.sigmoid(pre.astype(F32))

    return pl.pallas_call(
        kernel,
        grid=(n_blk,),
        in_specs=[whole(normed.shape), pl.BlockSpec((1, D, BLK), lambda n: (n, 0, 0))],
        out_specs=pl.BlockSpec((1, tokens, BLK), lambda n: (n, 0, 0)),
        out_shape=shape_of((n_blk, tokens, BLK), F32),
        compiler_params=params(),
    )(normed, gate_map)


def out_stage(seq_out, gate, x_tok, out_map, gain=None):
    groups, n_blk, width, _ = seq_out.shape
    tokens = groups * width
    extra = 0 if gain is None else EXTRA

    def kernel(seq_ref, gate_ref, x_ref, map_ref, *refs):
        if gain is None:
            res_ref, gated_ref = refs
        else:
            gain_ref, res_ref, normed_ref, gated_ref = refs
        n = pl.program_id(0)

        @pl.when(n == 0)
        def _():
            for z in range(n_blk):
                seq = seq_ref[:, z].reshape(tokens, BLK).astype(F32)
                gated_ref[:, z * BLK : (z + 1) * BLK] = (seq * gate_ref[z]).astype(BF16)

        mixed = dot(gated_ref[...], map_ref[0]).astype(BF16).astype(F32)
        res_ref[n, :tokens] = (x_ref[n].astype(F32) + mixed).astype(BF16)
        if gain is not None:

            @pl.when(n == n_blk - 1)
            def _():
                blocks = [res_ref[z, :tokens] for z in range(n_blk)]

                def store(z, value):
                    normed_ref[:, z * BLK : (z + 1) * BLK] = value

                normalize(blocks, gain_ref, tokens, store)
                total = squares_by_lane(blocks)
                total = jnp.concatenate([total, total], axis=0)
                high = total.astype(BF16).astype(F32)
                mid = (total - high).astype(BF16).astype(F32)
                row = lax.broadcasted_iota(jnp.int32, (EXTRA, tokens), 0)
                rest = jnp.where(row == 1, mid, jnp.where(row == 2, total - high - mid, 0.0))
                packed = jnp.where(row == 0, high, rest).astype(BF16)
                for z in range(n_blk):
                    res_ref[z, tokens:] = packed

    tok_shape = (n_blk, tokens, BLK)
    in_specs = [
        whole(seq_out.shape),
        whole(tok_shape),
        whole(x_tok.shape),
        pl.BlockSpec((1, D, BLK), lambda n: (n, 0, 0)),
    ]
    out_shape = [shape_of((n_blk, tokens + extra, BLK))]
    operands = [seq_out, gate, x_tok, out_map]
    if gain is not None:
        operands.append(gain)
        in_specs.append(whole(gain.shape))
        out_shape.append(shape_of((tokens, D)))
    if x_tok.shape != tok_shape:
        in_specs[2] = whole(x_tok.shape)

        def wrapped(seq_ref, gate_ref, x_ref, *refs):
            kernel(seq_ref, gate_ref, x_ref.at[:, :tokens], *refs)
    else:
        wrapped = kernel
    return pl.pallas_call(
        wrapped,
        grid=(n_blk,),
        in_specs=in_specs,
        out_specs=[whole(s.shape) for s in out_shape],
        out_shape=out_shape,
        scratch_shapes=[pltpu.VMEM((tokens, D), BF16)],
        compiler_params=params(),
    )(*operands)


def body(
    x_in,
    norm_gain,
    right_blocks,
    left_blocks,
    gate_first,
    gate_second,
    out_first,
    out_second,
    head,
    targets,
):
    section = lax.axis_index("section")
    first = section == 0
    tensor_index = lax.axis_index("tensor")
    z_scalar = tensor_index.astype(jnp.int32).reshape(1)
    seq_count = lax.axis_size("seq")
    n_blk = lax.axis_size("tensor")
    everyone = ("seq", "tensor")
    swap = [(0, 1), (1, 0)]
    rows_dev, tokens = right_blocks.shape[1], right_blocks.shape[2]
    j_dev = left_blocks.shape[1]
    p_count = left_blocks.shape[2]

    def by_block(own):
        other = lax.ppermute(own, "section", swap)
        return jnp.where(first, own, other), jnp.where(first, other, own)

    x_own = lax.dynamic_index_in_dim(x_in, section, 0, keepdims=False).reshape(
        rows_dev, tokens, BLK
    )
    squares, *sends = split_stage(x_own, z_scalar)
    gain_local = by_block(norm_gain)
    gain_pair = jnp.concatenate(gain_local, axis=0)
    shared = jnp.concatenate([squares, gain_pair, jnp.zeros((6, BLK), F32)], axis=0)
    shared = gather_by_exchange(shared, "tensor")
    squares = jnp.sum(shared[:, :rows_dev], axis=0)
    gains = [shared[:, rows_dev + b][:, None, :] for b in range(2)]
    rights = by_block(right_blocks[0])
    lefts = by_block(left_blocks[0])

    received = [sends[0]] + [
        lax.ppermute(sends[d], "tensor", [(i, (i + d) % n_blk) for i in range(n_blk)])
        for d in range(1, n_blk)
    ]

    def rows_second(factor):
        return jnp.transpose(factor[0], (2, 1, 0)).reshape(C1, D)

    gate_maps = [
        channel_map(a, c, n_blk)
        for a, c in zip(by_block(gate_first[0]), by_block(rows_second(gate_second)))
    ]
    out_maps = [
        channel_map(a, c, n_blk)
        for a, c in zip(by_block(out_first[0]), by_block(rows_second(out_second)))
    ]

    head_local = head[0]
    vocab_dev = head_local.shape[1]
    vocab_offset = lax.axis_index(everyone) * vocab_dev

    def sequence_mix(x_chan, squares, b):
        mix = right_stage(x_chan, squares, gain_local[b], rights[b], seq_count)
        cols = lax.all_to_all(mix, "seq", split_axis=0, concat_axis=0, tiled=True)
        col_out = left_stage(lefts[b], cols.reshape(p_count * j_dev, BLK))
        seq_out = lax.all_to_all(
            col_out.reshape(p_count, j_dev, BLK), everyone, split_axis=0, concat_axis=0, tiled=True
        )
        return seq_out.reshape(seq_count, n_blk, j_dev, BLK)

    def scored_rows(result):
        return jnp.transpose(result[:, :tokens:STRIDE], (1, 0, 2)).reshape(-1, D)

    def to_channels(result):
        return lax.all_to_all(result, "tensor", split_axis=0, concat_axis=0, tiled=True)

    seq_out = sequence_mix(x_own, squares, 0)
    x_tok, normed = token_stage(received, gains[0], z_scalar)
    gate = gate_stage(normed, gate_maps[0])
    packed, normed = out_stage(seq_out, gate, x_tok, out_maps[0], gains[1])
    rows_one = scored_rows(packed)
    chan_one = to_channels(packed)

    gate = gate_stage(normed, gate_maps[1])
    seq_out = sequence_mix(chan_one, None, 1)
    (result,) = out_stage(seq_out, gate, packed, out_maps[1])
    rows_two = scored_rows(result)

    kept = jnp.where(first, rows_one, rows_two)
    got = lax.ppermute(jnp.where(first, rows_two, rows_one), "section", swap)
    pair = jnp.where(first, jnp.concatenate([kept, got]), jnp.concatenate([got, kept]))
    near = gather_by_exchange(pair, "tensor").reshape(-1, D)
    scored = gather_by_exchange(near, "seq").reshape(-1, D)
    scored, result = lax.optimization_barrier((scored, result))
    chan_two = to_channels(result)

    logits = jnp.dot(scored, head_local, preferred_element_type=F32)
    exp_sums = jnp.sum(jnp.exp(logits), axis=1)
    vocab_ids = jnp.arange(vocab_dev, dtype=jnp.int32)[None, :] + vocab_offset
    labels = jnp.transpose(targets.reshape(2, p_count, -1), (1, 0, 2)).reshape(-1)
    is_target = vocab_ids == labels[:, None]
    target_part = jnp.sum(jnp.where(is_target, logits, 0.0), axis=1)
    total = jnp.stack([exp_sums, target_part]).reshape(-1, 128)
    total = sum_over(total, "seq", (1, 2, 3))
    total = sum_over(total, "seq", (4, 8, 12))
    total = sum_over(total, "tensor", (2, 4, 6))
    total = sum_over(total, "tensor", (1,)).reshape(2, -1)
    losses = jnp.log(total[0]) - total[1]
    aux_losses = jnp.transpose(losses.reshape(p_count, 2, -1), (1, 0, 2)).reshape(1, 2, -1)

    chan_one = chan_one[:, :tokens].reshape(rows_dev * tokens, BLK)
    chan_two = chan_two.reshape(rows_dev * tokens, BLK)
    got_one = lax.ppermute(chan_one, "section", [(1, 0)])
    got_two = lax.ppermute(chan_two, "section", [(0, 1)])
    block_out = jnp.stack(
        [jnp.where(first, chan_one, got_two), jnp.where(first, got_one, chan_two)]
    )[None]
    return (block_out, aux_losses)


def solution(mesh):
    in_specs = (
        P(None, "seq", "tensor"),
        P("section", "tensor"),
        P("section", "seq", None, None),
        P("section", "seq", None, None),
        P("section", None, None, None),
        P("section", None, None, None),
        P("section", None, None, None),
        P("section", None, None, None),
        P("section", None, ("seq", "tensor")),
        P(),
    )
    out_specs = (P("section", None, "seq", "tensor"), P("section", None, None))
    return jax.shard_map(body, mesh=mesh, in_specs=in_specs, out_specs=out_specs, check_vma=False)
```

```python
import jax
import jax.numpy as jnp
from jax import lax
from jax.experimental import pallas as pl
from jax.experimental.pallas import tpu as pltpu
from jax.sharding import PartitionSpec as P

C1 = 32
C2 = 64
D = 2048
STRIDE = 128
EPS = 1e-05
BLK = 256
EXTRA = 16
VMEM_LIMIT = 48 * 1024 * 1024
F32 = jnp.float32
BF16 = jnp.bfloat16


def params():
    return pltpu.CompilerParams(vmem_limit_bytes=VMEM_LIMIT)


def whole(shape):
    return pl.BlockSpec(shape, lambda *_: (0,) * len(shape))


def scalar_spec():
    return pl.BlockSpec(memory_space=pltpu.SMEM)


def shape_of(shape, dtype=BF16):
    return jax.ShapeDtypeStruct(shape, dtype)


def dot(a, b):
    return jnp.dot(a, b, preferred_element_type=F32)


def gather_by_exchange(block, axis):
    count = lax.axis_size(axis)
    copies = jnp.broadcast_to(block[None], (count,) + block.shape)
    return lax.all_to_all(copies, axis, split_axis=0, concat_axis=0, tiled=True)


def squares_by_lane(x_blocks):
    ones = jnp.ones((8, BLK), BF16)
    dims = (((1,), (1,)), ((), ()))
    total = None
    for x in x_blocks:
        xf = x.astype(F32)
        square = xf * xf
        high = square.astype(BF16)
        low = (square - high.astype(F32)).astype(BF16)
        part = lax.dot_general(ones, high, dims, preferred_element_type=F32) + lax.dot_general(
            ones, low, dims, preferred_element_type=F32
        )
        total = part if total is None else total + part
    return total


def split_stage(x_own, tensor_index):
    rows, tokens, _ = x_own.shape

    def kernel(z_ref, x_ref, squares_ref, *send_refs):
        z = z_ref[0]
        row = lax.broadcasted_iota(jnp.int32, (8, tokens), 0)
        squares = jnp.zeros((8, tokens), F32)
        for p in range(rows):
            squares = jnp.where(row == p, squares_by_lane([x_ref[p]]), squares)
        squares_ref[...] = squares
        for d in range(rows):
            send_refs[d][...] = x_ref[(z + d) % rows]

    outs = [shape_of((rows, tokens), F32)] + [shape_of((tokens, BLK))] * rows
    return pl.pallas_call(
        kernel,
        in_specs=[scalar_spec(), whole(x_own.shape)],
        out_shape=outs,
        compiler_params=params(),
    )(tensor_index, x_own)


def right_stage(x_chan, squares, gain_local, right, groups):
    rows = right.shape[0]
    tokens = right.shape[1]
    width = tokens // groups
    operands = [x_chan, gain_local, right] + ([] if squares is None else [squares])

    def kernel(x_ref, gain_ref, right_ref, *refs):
        out_ref = refs[-1]
        for p in range(rows):
            if squares is None:
                extra = x_ref[p, tokens:].astype(F32)
                total = extra[0:1] + extra[1:2] + extra[2:3]
            else:
                total = refs[0][p : p + 1]
            scale = lax.rsqrt(total / D + EPS)
            scaled = (right_ref[p].astype(F32) * scale).astype(BF16)
            mix = dot(scaled, x_ref[p, :tokens]) * gain_ref[...]
            out_ref[:, p] = mix.astype(BF16).reshape(groups, width, BLK)

    return pl.pallas_call(
        kernel,
        out_shape=shape_of((groups, rows, width, BLK)),
        compiler_params=params(),
    )(*operands)


def left_stage(left, mix):
    j_count, i_count, p_count = left.shape

    half = BLK // 2

    def kernel(left_ref, mix_ref, out_ref, wide_ref, acc_ref):
        for h in range(2):
            wide_ref[h] = mix_ref[:, h * half : (h + 1) * half].astype(F32)
        for j in range(j_count):
            column = jnp.concatenate(
                [wide_ref[h, pl.ds(j, p_count, stride=j_count), :] for h in range(2)], axis=1
            ).astype(BF16)
            mixed = dot(left_ref[j], column)
            for h in range(2):
                acc_ref[h, pl.ds(j, i_count, stride=j_count), :] = mixed[:, h * half : (h + 1) * half]
        for h in range(2):
            out_ref[:, h * half : (h + 1) * half] = acc_ref[h].astype(BF16)

    return pl.pallas_call(
        kernel,
        out_shape=shape_of((i_count * j_count, BLK)),
        scratch_shapes=[
            pltpu.VMEM((2, p_count * j_count, half), F32),
            pltpu.VMEM((2, i_count * j_count, half), F32),
        ],
        compiler_params=params(),
    )(left, mix)


def channel_map(first, second_rows, n_blk):
    def kernel(first_ref, second_ref, out_ref, spread_ref):
        @pl.when(pl.program_id(0) == 0)
        def _():
            lane = lax.broadcasted_iota(jnp.int32, (C2, BLK), 1) % C2
            pick = (lane == lax.broadcasted_iota(jnp.int32, (C2, BLK), 0)).astype(BF16)

            @pl.loop(0, C1)
            def _(r):
                spread_ref[r] = lax.dot_general(
                    first_ref[r], pick, (((0,), (0,)), ((), ())), preferred_element_type=F32
                ).astype(BF16)

        for r in range(C1):
            row = second_ref[r : r + 1]
            out_ref[0, r * C2 : (r + 1) * C2] = spread_ref[r] * row

    return pl.pallas_call(
        kernel,
        grid=(n_blk,),
        in_specs=[whole((C1, C2, C2)), pl.BlockSpec((C1, BLK), lambda n: (0, n))],
        out_specs=pl.BlockSpec((1, D, BLK), lambda n: (n, 0, 0)),
        out_shape=shape_of((n_blk, D, BLK)),
        scratch_shapes=[pltpu.VMEM((C1, C2, BLK), BF16)],
        compiler_params=params(),
    )(first, second_rows)


def normalize(x_blocks, gain_ref, tokens, store):
    total = jnp.zeros((tokens, 1), F32)
    for x in x_blocks:
        xf = x.astype(F32)
        total = total + jnp.sum(xf * xf, axis=1, keepdims=True)
    scale = lax.rsqrt(total / D + EPS)
    for n, x in enumerate(x_blocks):
        store(n, (x.astype(F32) * scale * gain_ref[n]).astype(BF16))


def token_stage(received, gain, tensor_index):
    n_blk = len(received)
    tokens = received[0].shape[0]

    def kernel(z_ref, gain_ref, *refs):
        x_ref, normed_ref = refs[n_blk:]
        for d in range(n_blk):
            x_ref[(z_ref[0] + n_blk - d) % n_blk] = refs[d][...]

        def store(n, value):
            normed_ref[:, n * BLK : (n + 1) * BLK] = value

        normalize([x_ref[n] for n in range(n_blk)], gain_ref, tokens, store)

    return pl.pallas_call(
        kernel,
        in_specs=[scalar_spec(), whole(gain.shape)] + [whole((tokens, BLK))] * n_blk,
        out_shape=(shape_of((n_blk, tokens, BLK)), shape_of((tokens, D))),
        compiler_params=params(),
    )(tensor_index, gain, *received)


def gate_stage(normed, gate_map):
    tokens = normed.shape[0]
    n_blk = gate_map.shape[0]

    def kernel(normed_ref, map_ref, out_ref):
        pre = dot(normed_ref[...], map_ref[0]).astype(BF16)
        out_ref[0] = jax.nn.sigmoid(pre.astype(F32))

    return pl.pallas_call(
        kernel,
        grid=(n_blk,),
        in_specs=[whole(normed.shape), pl.BlockSpec((1, D, BLK), lambda n: (n, 0, 0))],
        out_specs=pl.BlockSpec((1, tokens, BLK), lambda n: (n, 0, 0)),
        out_shape=shape_of((n_blk, tokens, BLK), F32),
        compiler_params=params(),
    )(normed, gate_map)


def out_stage(seq_out, gate, x_tok, out_map, gain=None, tensor_index=None):
    groups, n_blk, width, _ = seq_out.shape
    tokens = groups * width

    def kernel(seq_ref, gate_ref, x_ref, map_ref, *refs):
        n = pl.program_id(0)
        if gain is not None:
            gain_ref, res_ref, normed_ref, gated_ref = refs
        else:
            z_ref, *send_refs, rows_ref, res_ref, gated_ref = refs

        @pl.when(n == 0)
        def _():
            for z in range(n_blk):
                seq = seq_ref[:, z].reshape(tokens, BLK).astype(F32)
                gated_ref[:, z * BLK : (z + 1) * BLK] = (seq * gate_ref[z]).astype(BF16)

        mixed = dot(gated_ref[...], map_ref[0]).astype(BF16).astype(F32)
        res_ref[n, :tokens] = (x_ref[n, :tokens].astype(F32) + mixed).astype(BF16)

        @pl.when(n == n_blk - 1)
        def _():
            if gain is None:
                for d in range(n_blk):
                    send_refs[d][...] = res_ref[(z_ref[0] + d) % n_blk]
                for z in range(n_blk):
                    for q in range(tokens // STRIDE):
                        rows_ref[q : q + 1, z * BLK : (z + 1) * BLK] = res_ref[
                            z, q * STRIDE : q * STRIDE + 1
                        ]
                return
            blocks = [res_ref[z, :tokens] for z in range(n_blk)]

            def store(z, value):
                normed_ref[:, z * BLK : (z + 1) * BLK] = value

            normalize(blocks, gain_ref, tokens, store)
            total = squares_by_lane(blocks)
            total = jnp.concatenate([total, total], axis=0)
            high = total.astype(BF16).astype(F32)
            mid = (total - high).astype(BF16).astype(F32)
            row = lax.broadcasted_iota(jnp.int32, (EXTRA, tokens), 0)
            rest = jnp.where(row == 1, mid, jnp.where(row == 2, total - high - mid, 0.0))
            packed = jnp.where(row == 0, high, rest).astype(BF16)
            for z in range(n_blk):
                res_ref[z, tokens:] = packed

    in_specs = [
        whole(seq_out.shape),
        whole(gate.shape),
        whole(x_tok.shape),
        pl.BlockSpec((1, D, BLK), lambda n: (n, 0, 0)),
    ]
    operands = [seq_out, gate, x_tok, out_map]
    scratch = [pltpu.VMEM((tokens, D), BF16)]
    if gain is not None:
        operands.append(gain)
        in_specs.append(whole(gain.shape))
        out_shape = [shape_of((n_blk, tokens + EXTRA, BLK)), shape_of((tokens, D))]
    else:
        operands.append(tensor_index)
        in_specs.append(scalar_spec())
        out_shape = [shape_of((tokens, BLK))] * n_blk + [shape_of((tokens // STRIDE, D))]
        scratch = [pltpu.VMEM((n_blk, tokens, BLK), BF16)] + scratch
    return pl.pallas_call(
        kernel,
        grid=(n_blk,),
        in_specs=in_specs,
        out_specs=[whole(s.shape) for s in out_shape],
        out_shape=out_shape,
        scratch_shapes=scratch,
        compiler_params=params(),
    )(*operands)


def place_stage(received, tensor_index):
    n_blk = len(received)
    tokens = received[0].shape[0]

    def kernel(z_ref, *refs):
        for d in range(n_blk):
            refs[n_blk][(z_ref[0] + n_blk - d) % n_blk] = refs[d][...]

    return pl.pallas_call(
        kernel,
        in_specs=[scalar_spec()] + [whole((tokens, BLK))] * n_blk,
        out_shape=shape_of((n_blk, tokens, BLK)),
        compiler_params=params(),
    )(tensor_index, *received)


def body(
    x_in,
    norm_gain,
    right_blocks,
    left_blocks,
    gate_first,
    gate_second,
    out_first,
    out_second,
    head,
    targets,
):
    section = lax.axis_index("section")
    first = section == 0
    tensor_index = lax.axis_index("tensor")
    z_scalar = tensor_index.astype(jnp.int32).reshape(1)
    seq_count = lax.axis_size("seq")
    n_blk = lax.axis_size("tensor")
    everyone = ("seq", "tensor")
    swap = [(0, 1), (1, 0)]
    rows_dev, tokens = right_blocks.shape[1], right_blocks.shape[2]
    j_dev = left_blocks.shape[1]
    p_count = left_blocks.shape[2]

    def by_block(own):
        other = lax.ppermute(own, "section", swap)
        return jnp.where(first, own, other), jnp.where(first, other, own)

    def by_distance(blocks):
        return [blocks[0]] + [
            lax.ppermute(blocks[d], "tensor", [(i, (i + d) % n_blk) for i in range(n_blk)])
            for d in range(1, n_blk)
        ]

    def rows_second(factor):
        return jnp.transpose(factor[0], (2, 1, 0)).reshape(C1, D)

    tie = lax.optimization_barrier

    x_own = lax.dynamic_index_in_dim(x_in, section, 0, keepdims=False).reshape(
        rows_dev, tokens, BLK
    )
    squares, *sends = split_stage(x_own, z_scalar)
    rights = by_block(right_blocks[0])
    gain_local = by_block(norm_gain)
    shared = jnp.concatenate([squares, *gain_local, jnp.zeros((6, BLK), F32)], axis=0)

    shared, gate_own, out_own, second_own = tie(
        (shared, gate_first[0], out_first[0], (gate_second, out_second))
    )
    gate_one, gate_two = by_block(gate_own)
    out_one, out_two = by_block(out_own)
    gate_sec = by_block(rows_second(second_own[0]))
    out_sec = by_block(rows_second(second_own[1]))
    shared = gather_by_exchange(shared, "tensor")
    gate_map_one = channel_map(gate_one, gate_sec[0], n_blk)
    squares = jnp.sum(shared[:, :rows_dev], axis=0)
    gains = [shared[:, rows_dev + b][:, None, :] for b in range(2)]

    def mix_right(x_chan, squares, b):
        return right_stage(x_chan, squares, gain_local[b], rights[b], seq_count)

    def exchange_seq(mix):
        return lax.all_to_all(mix, "seq", split_axis=0, concat_axis=0, tiled=True)

    def mix_left(cols, b):
        out = left_stage(lefts[b], cols.reshape(p_count * j_dev, BLK))
        return out.reshape(p_count, j_dev, BLK)

    def exchange_all(cols):
        out = lax.all_to_all(cols, everyone, split_axis=0, concat_axis=0, tiled=True)
        return out.reshape(seq_count, n_blk, j_dev, BLK)

    mix = mix_right(x_own, squares, 0)
    mix, left_own, gate_map_one, out_one = tie((mix, left_blocks[0], gate_map_one, out_one))
    cols = exchange_seq(mix)
    lefts = by_block(left_own)
    received = by_distance(sends)
    out_map_one = channel_map(out_one, out_sec[0], n_blk)

    cols = mix_left(cols, 0)
    cols, received, out_map_one, gate_two, out_two, head_own = tie(
        (cols, received, out_map_one, gate_two, out_two, head[0])
    )
    seq_out = exchange_all(cols)
    x_tok, normed = token_stage(received, gains[0], z_scalar)
    gate = gate_stage(normed, gate_map_one)
    gate_map_two = channel_map(gate_two, gate_sec[1], n_blk)
    out_map_two = channel_map(out_two, out_sec[1], n_blk)
    heads = by_block(head_own)
    packed, normed = out_stage(seq_out, gate, x_tok, out_map_one, gain=gains[1])

    rows_one = jnp.transpose(packed[:, :tokens:STRIDE], (1, 0, 2)).reshape(-1, D)
    chan_one = lax.all_to_all(packed, "tensor", split_axis=0, concat_axis=0, tiled=True)
    gate = gate_stage(normed, gate_map_two)
    cols = exchange_seq(mix_right(chan_one, None, 1))
    seq_out = exchange_all(mix_left(cols, 1))
    *sends, rows_two = out_stage(seq_out, gate, packed, out_map_two, tensor_index=z_scalar)

    pair = jnp.concatenate([rows_one, rows_two], axis=0)
    near = gather_by_exchange(pair, "tensor").reshape(-1, D)
    received = by_distance(sends)
    scored = gather_by_exchange(near, "seq")
    scored, received = tie((scored, received))
    scored = scored.reshape(-1, D)

    vocab_dev = head.shape[2]
    vocab_offset = lax.axis_index(everyone) * vocab_dev
    vocab_ids = jnp.arange(vocab_dev, dtype=jnp.int32)[None, :] + vocab_offset
    labels = jnp.where(first, targets[0], targets[1]).reshape(p_count, 1, -1)
    labels = jnp.broadcast_to(labels, (p_count, 2, labels.shape[2]))
    row_shape = labels.shape
    is_target = vocab_ids == labels.reshape(-1)[:, None]
    parts = []
    for b in range(2):
        logits = jnp.dot(scored, heads[b], preferred_element_type=F32)
        exp_sums = jnp.sum(jnp.exp(logits), axis=1)
        target_part = jnp.sum(jnp.where(is_target, logits, 0.0), axis=1)
        parts.append(jnp.stack([exp_sums, target_part]))
    row_block = lax.broadcasted_iota(jnp.int32, row_shape, 1).reshape(1, -1)
    parts = jnp.where(row_block == 0, parts[0], parts[1]).reshape(-1, 128)
    totals = jnp.sum(gather_by_exchange(parts, everyone), axis=0).reshape(2, -1)
    losses = (jnp.log(totals[0]) - totals[1]).reshape(row_shape)
    losses = [losses[:, b].reshape(-1) for b in range(2)]
    kept = jnp.where(first, losses[0], losses[1])
    got = lax.ppermute(jnp.where(first, losses[1], losses[0]), "section", swap)
    aux_losses = jnp.where(first, jnp.stack([kept, got]), jnp.stack([got, kept]))[None]

    chan_one = chan_one[:, :tokens].reshape(rows_dev * tokens, BLK)
    chan_two = place_stage(received, z_scalar).reshape(rows_dev * tokens, BLK)
    got_one = lax.ppermute(chan_one, "section", [(1, 0)])
    got_two = lax.ppermute(chan_two, "section", [(0, 1)])
    block_out = jnp.stack(
        [jnp.where(first, chan_one, got_two), jnp.where(first, got_one, chan_two)]
    )[None]
    return (block_out, aux_losses)


def solution(mesh):
    in_specs = (
        P(None, "seq", "tensor"),
        P("section", "tensor"),
        P("section", "seq", None, None),
        P("section", "seq", None, None),
        P("section", None, None, None),
        P("section", None, None, None),
        P("section", None, None, None),
        P("section", None, None, None),
        P("section", None, ("seq", "tensor")),
        P(),
    )
    out_specs = (P("section", None, "seq", "tensor"), P("section", None, None))
    return jax.shard_map(body, mesh=mesh, in_specs=in_specs, out_specs=out_specs, check_vma=False)
```

```python
import jax
import jax.numpy as jnp
from jax import lax
from jax.experimental import pallas as pl
from jax.experimental.pallas import tpu as pltpu
from jax.sharding import PartitionSpec as P

C1 = 32
C2 = 64
D = 2048
STRIDE = 128
EPS = 1e-05
BLK = 256
EXTRA = 16
VMEM_LIMIT = 48 * 1024 * 1024
F32 = jnp.float32
BF16 = jnp.bfloat16


def params():
    return pltpu.CompilerParams(vmem_limit_bytes=VMEM_LIMIT)


def whole(shape):
    return pl.BlockSpec(shape, lambda *_: (0,) * len(shape))


def scalar_spec():
    return pl.BlockSpec(memory_space=pltpu.SMEM)


def shape_of(shape, dtype=BF16):
    return jax.ShapeDtypeStruct(shape, dtype)


def dot(a, b):
    return jnp.dot(a, b, preferred_element_type=F32)


def gather_by_exchange(block, axis):
    count = lax.axis_size(axis)
    copies = jnp.broadcast_to(block[None], (count,) + block.shape)
    return lax.all_to_all(copies, axis, split_axis=0, concat_axis=0, tiled=True)


def squares_by_lane(x_blocks):
    ones = jnp.ones((8, BLK), BF16)
    dims = (((1,), (1,)), ((), ()))
    total = None
    for x in x_blocks:
        xf = x.astype(F32)
        square = xf * xf
        high = square.astype(BF16)
        low = (square - high.astype(F32)).astype(BF16)
        part = lax.dot_general(ones, high, dims, preferred_element_type=F32) + lax.dot_general(
            ones, low, dims, preferred_element_type=F32
        )
        total = part if total is None else total + part
    return total


def split_stage(x_own, tensor_index):
    rows, tokens, _ = x_own.shape

    def kernel(z_ref, x_ref, squares_ref, *send_refs):
        z = z_ref[0]
        row = lax.broadcasted_iota(jnp.int32, (8, tokens), 0)
        squares = jnp.zeros((8, tokens), F32)
        for p in range(rows):
            squares = jnp.where(row == p, squares_by_lane([x_ref[p]]), squares)
        squares_ref[...] = squares
        for d in range(rows):
            send_refs[d][...] = x_ref[(z + d) % rows]

    outs = [shape_of((rows, tokens), F32)] + [shape_of((tokens, BLK))] * rows
    return pl.pallas_call(
        kernel,
        in_specs=[scalar_spec(), whole(x_own.shape)],
        out_shape=outs,
        compiler_params=params(),
    )(tensor_index, x_own)


def right_stage(x_chan, squares, gain_local, right, groups):
    rows = right.shape[0]
    tokens = right.shape[1]
    width = tokens // groups
    operands = [x_chan, gain_local, right] + ([] if squares is None else [squares])

    def kernel(x_ref, gain_ref, right_ref, *refs):
        out_ref = refs[-1]
        for p in range(rows):
            if squares is None:
                extra = x_ref[p, tokens : tokens + EXTRA].astype(F32)
                total = extra[0:1] + extra[1:2] + extra[2:3]
            else:
                total = refs[0][p : p + 1]
            scale = lax.rsqrt(total / D + EPS)
            scaled = (right_ref[p].astype(F32) * scale).astype(BF16)
            mix = dot(scaled, x_ref[p, :tokens]) * gain_ref[...]
            out_ref[:, p] = mix.astype(BF16).reshape(groups, width, BLK)

    return pl.pallas_call(
        kernel,
        out_shape=shape_of((groups, rows, width, BLK)),
        compiler_params=params(),
    )(*operands)


def left_stage(left, mix):
    j_count, i_count, p_count = left.shape

    half = BLK // 2

    def kernel(left_ref, mix_ref, out_ref, wide_ref, acc_ref):
        for h in range(2):
            wide_ref[h] = mix_ref[:, h * half : (h + 1) * half].astype(F32)
        for j in range(j_count):
            column = jnp.concatenate(
                [wide_ref[h, pl.ds(j, p_count, stride=j_count), :] for h in range(2)], axis=1
            ).astype(BF16)
            mixed = dot(left_ref[j], column)
            for h in range(2):
                acc_ref[h, pl.ds(j, i_count, stride=j_count), :] = mixed[:, h * half : (h + 1) * half]
        for h in range(2):
            out_ref[:, h * half : (h + 1) * half] = acc_ref[h].astype(BF16)

    return pl.pallas_call(
        kernel,
        out_shape=shape_of((i_count * j_count, BLK)),
        scratch_shapes=[
            pltpu.VMEM((2, p_count * j_count, half), F32),
            pltpu.VMEM((2, i_count * j_count, half), F32),
        ],
        compiler_params=params(),
    )(left, mix)


def channel_map(first, second_rows, n_blk):
    def kernel(first_ref, second_ref, out_ref, spread_ref):
        @pl.when(pl.program_id(0) == 0)
        def _():
            lane = lax.broadcasted_iota(jnp.int32, (C2, BLK), 1) % C2
            pick = (lane == lax.broadcasted_iota(jnp.int32, (C2, BLK), 0)).astype(BF16)

            @pl.loop(0, C1)
            def _(r):
                spread_ref[r] = lax.dot_general(
                    first_ref[r], pick, (((0,), (0,)), ((), ())), preferred_element_type=F32
                ).astype(BF16)

        for r in range(C1):
            row = second_ref[r : r + 1].astype(F32)
            out_ref[0, r * C2 : (r + 1) * C2] = (spread_ref[r].astype(F32) * row).astype(BF16)

    return pl.pallas_call(
        kernel,
        grid=(n_blk,),
        in_specs=[whole((C1, C2, C2)), pl.BlockSpec((C1, BLK), lambda n: (0, n))],
        out_specs=pl.BlockSpec((1, D, BLK), lambda n: (n, 0, 0)),
        out_shape=shape_of((n_blk, D, BLK)),
        scratch_shapes=[pltpu.VMEM((C1, C2, BLK), BF16)],
        compiler_params=params(),
    )(first, second_rows)


def normalize(x_blocks, gain_ref, tokens, store):
    total = jnp.zeros((tokens, 1), F32)
    for x in x_blocks:
        xf = x.astype(F32)
        total = total + jnp.sum(xf * xf, axis=1, keepdims=True)
    scale = lax.rsqrt(total / D + EPS)
    for n, x in enumerate(x_blocks):
        store(n, (x.astype(F32) * scale * gain_ref[n]).astype(BF16))


def token_stage(received, gain, tensor_index):
    n_blk = len(received)
    tokens = received[0].shape[0]

    def kernel(z_ref, gain_ref, *refs):
        x_ref, normed_ref = refs[n_blk:]
        for d in range(n_blk):
            x_ref[(z_ref[0] + n_blk - d) % n_blk] = refs[d][...]

        def store(n, value):
            normed_ref[:, n * BLK : (n + 1) * BLK] = value

        normalize([x_ref[n] for n in range(n_blk)], gain_ref, tokens, store)

    return pl.pallas_call(
        kernel,
        in_specs=[scalar_spec(), whole(gain.shape)] + [whole((tokens, BLK))] * n_blk,
        out_shape=(shape_of((n_blk, tokens, BLK)), shape_of((tokens, D))),
        compiler_params=params(),
    )(tensor_index, gain, *received)


def gate_stage(normed, gate_map):
    tokens = normed.shape[0]
    n_blk = gate_map.shape[0]

    def kernel(normed_ref, map_ref, out_ref):
        pre = dot(normed_ref[...], map_ref[0]).astype(BF16)
        out_ref[0] = jax.nn.sigmoid(pre.astype(F32))

    return pl.pallas_call(
        kernel,
        grid=(n_blk,),
        in_specs=[whole(normed.shape), pl.BlockSpec((1, D, BLK), lambda n: (n, 0, 0))],
        out_specs=pl.BlockSpec((1, tokens, BLK), lambda n: (n, 0, 0)),
        out_shape=shape_of((n_blk, tokens, BLK), F32),
        compiler_params=params(),
    )(normed, gate_map)


def out_stage(seq_out, gate, x_tok, out_map, gain=None):
    groups, n_blk, width, _ = seq_out.shape
    tokens = groups * width
    height = tokens + EXTRA * (1 if gain is None else 2)

    def kernel(seq_ref, gate_ref, x_ref, map_ref, *refs):
        n = pl.program_id(0)
        if gain is None:
            res_ref, gated_ref = refs
        else:
            gain_ref, res_ref, normed_ref, gated_ref = refs

        @pl.when(n == 0)
        def _():
            for z in range(n_blk):
                seq = seq_ref[:, z].reshape(tokens, BLK).astype(F32)
                gated_ref[:, z * BLK : (z + 1) * BLK] = (seq * gate_ref[z]).astype(BF16)

        mixed = dot(gated_ref[...], map_ref[0]).astype(BF16).astype(F32)
        res_ref[n, :tokens] = (x_ref[n, :tokens].astype(F32) + mixed).astype(BF16)

        @pl.when(n == n_blk - 1)
        def _():
            blocks = [res_ref[z, :tokens] for z in range(n_blk)]
            place = lax.broadcasted_iota(jnp.int32, (EXTRA, BLK), 0)
            scored = jnp.zeros((EXTRA, BLK), F32)
            for z in range(n_blk):
                for q in range(tokens // STRIDE):
                    row = blocks[z][q * STRIDE : q * STRIDE + 1].astype(F32)
                    scored = jnp.where(place == q * n_blk + z, row, scored)
            for z in range(n_blk):
                res_ref[z, height - EXTRA :] = scored.astype(BF16)
            if gain is None:
                return

            def store(z, value):
                normed_ref[:, z * BLK : (z + 1) * BLK] = value

            normalize(blocks, gain_ref, tokens, store)
            total = squares_by_lane(blocks)
            total = jnp.concatenate([total, total], axis=0)
            high = total.astype(BF16).astype(F32)
            mid = (total - high).astype(BF16).astype(F32)
            row = lax.broadcasted_iota(jnp.int32, (EXTRA, tokens), 0)
            rest = jnp.where(row == 1, mid, jnp.where(row == 2, total - high - mid, 0.0))
            packed = jnp.where(row == 0, high, rest).astype(BF16)
            for z in range(n_blk):
                res_ref[z, tokens : tokens + EXTRA] = packed

    in_specs = [
        whole(seq_out.shape),
        whole(gate.shape),
        whole(x_tok.shape),
        pl.BlockSpec((1, D, BLK), lambda n: (n, 0, 0)),
    ]
    operands = [seq_out, gate, x_tok, out_map]
    out_shape = [shape_of((n_blk, height, BLK))]
    if gain is not None:
        operands.append(gain)
        in_specs.append(whole(gain.shape))
        out_shape.append(shape_of((tokens, D)))
    return pl.pallas_call(
        kernel,
        grid=(n_blk,),
        in_specs=in_specs,
        out_specs=[whole(s.shape) for s in out_shape],
        out_shape=out_shape,
        scratch_shapes=[pltpu.VMEM((tokens, D), BF16)],
        compiler_params=params(),
    )(*operands)


def score_stage(row_sets, heads, labels, first_column, column_step):
    n_blk = row_sets[0].shape[0]
    per_ring = 2 * n_blk
    count = len(row_sets) * per_ring
    groups, _, width = heads.shape

    def kernel(first_ref, head_ref, label_ref, *refs):
        out_ref, rows_ref, exp_ref, target_ref = refs[-4:]
        g = pl.program_id(0)

        @pl.when(g == 0)
        def _():
            exp_ref[...] = jnp.zeros_like(exp_ref)
            target_ref[...] = jnp.zeros_like(target_ref)
            for m in range(len(row_sets)):
                for z in range(n_blk):
                    lines = refs[m][z].astype(F32)
                    for q in range(2):
                        at = m * per_ring + z * 2 + q
                        for n in range(n_blk):
                            line = q * n_blk + n
                            rows_ref[at : at + 1, n * BLK : (n + 1) * BLK] = lines[line : line + 1]

        logits = dot(rows_ref[...].astype(BF16), head_ref[0])
        column = lax.broadcasted_iota(jnp.int32, (count, width), 1) + (first_ref[0] + g * column_step)
        exp_ref[...] += jnp.sum(jnp.exp(logits), axis=1, keepdims=True)
        target_ref[...] += jnp.sum(
            jnp.where(column == label_ref[...], logits, 0.0), axis=1, keepdims=True
        )

        @pl.when(g == groups - 1)
        def _():
            row = lax.broadcasted_iota(jnp.int32, (count, 128), 0)
            lane = lax.broadcasted_iota(jnp.int32, (count, 128), 1)
            spread = jnp.where(lane == row, exp_ref[...], 0.0)
            spread = spread + jnp.where(lane == row + count, target_ref[...], 0.0)
            out_ref[...] = jnp.sum(spread, axis=0, keepdims=True)

    return pl.pallas_call(
        kernel,
        grid=(groups,),
        in_specs=[
            scalar_spec(),
            pl.BlockSpec((1, D, width), lambda g: (g, 0, 0)),
            whole(labels.shape),
        ]
        + [whole(r.shape) for r in row_sets],
        out_specs=whole((1, 128)),
        out_shape=shape_of((1, 128), F32),
        scratch_shapes=[
            pltpu.VMEM((count, D), F32),
            pltpu.VMEM((count, 1), F32),
            pltpu.VMEM((count, 1), F32),
        ],
        compiler_params=params(),
    )(first_column, heads, labels, *row_sets)


def loss_stage(parts, groups, count):
    def kernel(parts_ref, out_ref):
        total = jnp.sum(parts_ref[...].reshape(groups, -1, 128), axis=1)
        losses = jnp.log(total[:, :count]) - total[:, count : 2 * count]
        for m in range(2):
            out_ref[m] = losses[:, m * count // 2 : (m + 1) * count // 2]

    return pl.pallas_call(
        kernel,
        out_shape=shape_of((2, groups, count // 2), F32),
        compiler_params=params(),
    )(parts)


def body(
    x_in,
    norm_gain,
    right_blocks,
    left_blocks,
    gate_first,
    gate_second,
    out_first,
    out_second,
    head,
    targets,
):
    section = lax.axis_index("section")
    first = section == 0
    tensor_index = lax.axis_index("tensor")
    z_scalar = tensor_index.astype(jnp.int32).reshape(1)
    seq_count = lax.axis_size("seq")
    n_blk = lax.axis_size("tensor")
    everyone = ("seq", "tensor")
    swap = [(0, 1), (1, 0)]
    rows_dev, tokens = right_blocks.shape[1], right_blocks.shape[2]
    j_dev = left_blocks.shape[1]
    p_count = left_blocks.shape[2]

    def by_block(own):
        other = lax.ppermute(own, "section", swap)
        return jnp.where(first, own, other), jnp.where(first, other, own)

    def by_distance(blocks):
        return [blocks[0]] + [
            lax.ppermute(blocks[d], "tensor", [(i, (i + d) % n_blk) for i in range(n_blk)])
            for d in range(1, n_blk)
        ]

    def rows_second(factor):
        return jnp.transpose(factor[0], (2, 1, 0)).reshape(C1, D)

    tie = lax.optimization_barrier

    x_own = lax.dynamic_index_in_dim(x_in, section, 0, keepdims=False).reshape(
        rows_dev, tokens, BLK
    )
    squares, *sends = split_stage(x_own, z_scalar)
    rights = by_block(right_blocks[0])
    gain_local = by_block(norm_gain)
    shared = jnp.concatenate([squares, *gain_local, jnp.zeros((6, BLK), F32)], axis=0)

    shared, head_own = tie((shared, head[0]))
    heads = lax.all_gather(head_own, "seq", axis=0)

    shared = gather_by_exchange(shared, "tensor")
    squares = jnp.sum(shared[:, :rows_dev], axis=0)
    gains = [shared[:, rows_dev + b][:, None, :] for b in range(2)]
    lefts = by_block(left_blocks[0])
    received = by_distance(sends)

    def exchange_seq(mix):
        return lax.all_to_all(mix, "seq", split_axis=0, concat_axis=0, tiled=True)

    def mix_left(cols, b):
        out = left_stage(lefts[b], cols.reshape(p_count * j_dev, BLK))
        return out.reshape(p_count, j_dev, BLK)

    def exchange_all(cols):
        out = lax.all_to_all(cols, everyone, split_axis=0, concat_axis=0, tiled=True)
        return out.reshape(seq_count, n_blk, j_dev, BLK)

    mix = right_stage(x_own, squares, gain_local[0], rights[0], seq_count)
    near = [1, 2, n_blk - 2, n_blk - 1]
    mix, near_blocks, gate_own, out_own, gate_sec_own, out_sec_own = tie(
        (mix, [received[d] for d in near], gate_first[0], out_first[0], gate_second, out_second)
    )
    for d, block in zip(near, near_blocks):
        received[d] = block
    cols = exchange_seq(mix)
    gate_firsts = by_block(gate_own)
    out_firsts = by_block(out_own)
    gate_seconds = by_block(rows_second(gate_sec_own))
    out_seconds = by_block(rows_second(out_sec_own))

    cols = mix_left(cols, 0)
    cols, received, gate_firsts, out_firsts, gate_seconds, out_seconds = tie(
        (cols, received, gate_firsts, out_firsts, gate_seconds, out_seconds)
    )
    seq_out = exchange_all(cols)
    x_tok, normed = token_stage(received, gains[0], z_scalar)
    gate = gate_stage(normed, channel_map(gate_firsts[0], gate_seconds[0], n_blk))
    out_map = channel_map(out_firsts[0], out_seconds[0], n_blk)
    packed, normed = out_stage(seq_out, gate, x_tok, out_map, gain=gains[1])

    packed, normed, gate_two, out_two, gate_sec, out_sec = tie(
        (packed, normed, gate_firsts[1], out_firsts[1], gate_seconds[1], out_seconds[1])
    )
    chan_one = lax.all_to_all(packed, "tensor", split_axis=0, concat_axis=0, tiled=True)
    gate = gate_stage(normed, channel_map(gate_two, gate_sec, n_blk))
    out_map = channel_map(out_two, out_sec, n_blk)
    mix = right_stage(chan_one, None, gain_local[1], rights[1], seq_count)
    mix, gate, out_map = tie((mix, gate, out_map))
    seq_out = exchange_all(mix_left(exchange_seq(mix), 1))
    seq_out, heads = tie((seq_out, heads))
    (packed_two,) = out_stage(seq_out, gate, packed, out_map)
    chan_two = lax.all_to_all(packed_two, "tensor", split_axis=0, concat_axis=0, tiled=True)

    rows_one, rows_two = chan_one[:, -EXTRA:], chan_two[:, -EXTRA:]
    kept = jnp.where(first, rows_one, rows_two)
    got = lax.ppermute(jnp.where(first, rows_two, rows_one), "section", swap)
    vocab_dev = head.shape[2]
    labels = lax.dynamic_index_in_dim(
        targets.reshape(2, seq_count, -1), lax.axis_index("seq"), 1, keepdims=False
    )
    labels = jnp.where(first, labels, labels[::-1]).reshape(-1, 1)
    parts = score_stage((kept, got), heads, labels, z_scalar * vocab_dev, n_blk * vocab_dev)
    parts = gather_by_exchange(parts, everyone).reshape(-1, 128)
    losses = loss_stage(parts, seq_count, labels.shape[0])
    aux_losses = jnp.where(first, losses, losses[::-1]).reshape(1, 2, -1)

    chan_one = chan_one[:, :tokens].reshape(rows_dev * tokens, BLK)
    chan_two = chan_two[:, :tokens].reshape(rows_dev * tokens, BLK)
    got_one = lax.ppermute(chan_one, "section", [(1, 0)])
    got_two = lax.ppermute(chan_two, "section", [(0, 1)])
    block_out = jnp.stack(
        [jnp.where(first, chan_one, got_two), jnp.where(first, got_one, chan_two)]
    )[None]
    return (block_out, aux_losses)


def solution(mesh):
    in_specs = (
        P(None, "seq", "tensor"),
        P("section", "tensor"),
        P("section", "seq", None, None),
        P("section", "seq", None, None),
        P("section", None, None, None),
        P("section", None, None, None),
        P("section", None, None, None),
        P("section", None, None, None),
        P("section", None, ("seq", "tensor")),
        P(),
    )
    out_specs = (P("section", None, "seq", "tensor"), P("section", None, None))
    return jax.shard_map(body, mesh=mesh, in_specs=in_specs, out_specs=out_specs, check_vma=False)
```

```python
import jax
import jax.numpy as jnp
from jax import lax
from jax.experimental import pallas as pl
from jax.experimental.pallas import tpu as pltpu
from jax.sharding import PartitionSpec as P

C1 = 32
C2 = 64
D = 2048
STRIDE = 128
EPS = 1e-05
BLK = 256
EXTRA = 16
PER = BLK // C2
VMEM_LIMIT = 48 * 1024 * 1024
F32 = jnp.float32
BF16 = jnp.bfloat16


def params():
    return pltpu.CompilerParams(vmem_limit_bytes=VMEM_LIMIT)


def whole(shape):
    return pl.BlockSpec(shape, lambda *_: (0,) * len(shape))


def scalar_spec():
    return pl.BlockSpec(memory_space=pltpu.SMEM)


def shape_of(shape, dtype=BF16):
    return jax.ShapeDtypeStruct(shape, dtype)


def dot(a, b):
    return jnp.dot(a, b, preferred_element_type=F32)


def gather_by_exchange(block, axis):
    count = lax.axis_size(axis)
    copies = jnp.broadcast_to(block[None], (count,) + block.shape)
    return lax.all_to_all(copies, axis, split_axis=0, concat_axis=0, tiled=True)


def squares_by_lane(x_blocks):
    ones = jnp.ones((8, BLK), BF16)
    dims = (((1,), (1,)), ((), ()))
    total = None
    for x in x_blocks:
        xf = x.astype(F32)
        square = xf * xf
        high = square.astype(BF16)
        low = (square - high.astype(F32)).astype(BF16)
        part = lax.dot_general(ones, high, dims, preferred_element_type=F32) + lax.dot_general(
            ones, low, dims, preferred_element_type=F32
        )
        total = part if total is None else total + part
    return total


def split3(value):
    high = value.astype(BF16).astype(F32)
    mid = (value - high).astype(BF16).astype(F32)
    return high, mid, value - high - mid


def pack_stage(x_own, gains):
    rows, tokens, _ = x_own.shape

    def kernel(x_ref, gain_a_ref, gain_b_ref, out_ref):
        row = lax.broadcasted_iota(jnp.int32, (rows, tokens), 0)
        squares = jnp.zeros((rows, tokens), F32)
        for p in range(rows):
            squares = jnp.where(row == p, squares_by_lane([x_ref[p]]), squares)
        gain_rows = jnp.zeros((rows, BLK), F32)
        for b, gain_ref in enumerate((gain_a_ref, gain_b_ref)):
            for part, value in enumerate(split3(gain_ref[...])):
                gain_rows = jnp.where(row == b * 3 + part, value, gain_rows)
        planes = jnp.concatenate([*split3(squares), gain_rows], axis=0).astype(BF16)
        for p in range(rows):
            out_ref[p, :tokens] = x_ref[p]
            out_ref[p, tokens:] = planes

    return pl.pallas_call(
        kernel,
        out_shape=shape_of((rows, tokens + 4 * rows, BLK)),
        compiler_params=params(),
    )(x_own, *gains)


def right_stage(x_chan, gain_local, right, groups, shared=None):
    rows = right.shape[0]
    tokens = right.shape[1]
    width = tokens // groups
    operands = [x_chan, gain_local, right] + ([] if shared is None else [shared])

    def kernel(x_ref, gain_ref, right_ref, *refs):
        out_ref = refs[-1]
        if shared is not None:
            squares = jnp.zeros((rows, tokens), F32)
            for z in range(shared.shape[0]):
                planes = refs[0][z, tokens:].astype(F32)
                for part in range(3):
                    squares = squares + planes[part * rows : (part + 1) * rows]
        for p in range(rows):
            if shared is None:
                extra = x_ref[p, tokens : tokens + EXTRA].astype(F32)
                total = extra[0:1] + extra[1:2] + extra[2:3]
            else:
                total = squares[p : p + 1]
            scale = lax.rsqrt(total / D + EPS)
            scaled = (right_ref[p].astype(F32) * scale).astype(BF16)
            mix = dot(scaled, x_ref[p, :tokens]) * gain_ref[...]
            out_ref[:, p] = mix.astype(BF16).reshape(groups, width, BLK)

    return pl.pallas_call(
        kernel,
        out_shape=shape_of((groups, rows, width, BLK)),
        compiler_params=params(),
    )(*operands)


def left_stage(left, mix):
    j_count, i_count, p_count = left.shape

    half = BLK // 2

    def kernel(left_ref, mix_ref, out_ref, wide_ref, acc_ref):
        for h in range(2):
            wide_ref[h] = mix_ref[:, h * half : (h + 1) * half].astype(F32)
        for j in range(j_count):
            column = jnp.concatenate(
                [wide_ref[h, pl.ds(j, p_count, stride=j_count), :] for h in range(2)], axis=1
            ).astype(BF16)
            mixed = dot(left_ref[j], column)
            for h in range(2):
                acc_ref[h, pl.ds(j, i_count, stride=j_count), :] = mixed[:, h * half : (h + 1) * half]
        for h in range(2):
            out_ref[:, h * half : (h + 1) * half] = acc_ref[h].astype(BF16)

    return pl.pallas_call(
        kernel,
        out_shape=shape_of((i_count * j_count, BLK)),
        scratch_shapes=[
            pltpu.VMEM((2, p_count * j_count, half), F32),
            pltpu.VMEM((2, i_count * j_count, half), F32),
        ],
        compiler_params=params(),
    )(left, mix)


def channel_map(first, second_rows, n_blk):
    def kernel(first_ref, second_ref, out_ref, spread_ref):
        @pl.when(pl.program_id(0) == 0)
        def _():
            lane = lax.broadcasted_iota(jnp.int32, (BLK, PER * BLK), 1)
            wanted = (lane // BLK) * C2 + lane % C2
            pick = (wanted == lax.broadcasted_iota(jnp.int32, (BLK, PER * BLK), 0)).astype(BF16)
            for g in range(C1 // PER):
                spread = lax.dot_general(
                    first_ref[g * PER : (g + 1) * PER].reshape(BLK, C2),
                    pick,
                    (((0,), (0,)), ((), ())),
                    preferred_element_type=F32,
                ).astype(BF16)
                for r in range(PER):
                    spread_ref[g * PER + r] = spread[:, r * BLK : (r + 1) * BLK]

        for r in range(C1):
            row = second_ref[r : r + 1].astype(F32)
            out_ref[0, r * C2 : (r + 1) * C2] = (spread_ref[r].astype(F32) * row).astype(BF16)

    return pl.pallas_call(
        kernel,
        grid=(n_blk,),
        in_specs=[whole((C1, C2, C2)), pl.BlockSpec((C1, BLK), lambda n: (0, n))],
        out_specs=pl.BlockSpec((1, D, BLK), lambda n: (n, 0, 0)),
        out_shape=shape_of((n_blk, D, BLK)),
        scratch_shapes=[pltpu.VMEM((C1, C2, BLK), BF16)],
        compiler_params=params(),
    )(first, second_rows)


def normalize(x_blocks, gain_ref, tokens, store):
    total = jnp.zeros((tokens, 1), F32)
    for x in x_blocks:
        xf = x.astype(F32)
        total = total + jnp.sum(xf * xf, axis=1, keepdims=True)
    scale = lax.rsqrt(total / D + EPS)
    for n, x in enumerate(x_blocks):
        store(n, (x.astype(F32) * scale * gain_ref[n]).astype(BF16))


def token_stage(x_tok, gain, tokens):
    n_blk = x_tok.shape[0]

    def kernel(gain_ref, x_ref, normed_ref):
        def store(n, value):
            normed_ref[:, n * BLK : (n + 1) * BLK] = value

        normalize([x_ref[n, :tokens] for n in range(n_blk)], gain_ref, tokens, store)

    return pl.pallas_call(
        kernel,
        out_shape=shape_of((tokens, D)),
        compiler_params=params(),
    )(gain, x_tok)


def gate_stage(normed, gate_map):
    tokens = normed.shape[0]
    n_blk = gate_map.shape[0]

    def kernel(normed_ref, map_ref, out_ref):
        pre = dot(normed_ref[...], map_ref[0]).astype(BF16)
        out_ref[0] = jax.nn.sigmoid(pre.astype(F32))

    return pl.pallas_call(
        kernel,
        grid=(n_blk,),
        in_specs=[whole(normed.shape), pl.BlockSpec((1, D, BLK), lambda n: (n, 0, 0))],
        out_specs=pl.BlockSpec((1, tokens, BLK), lambda n: (n, 0, 0)),
        out_shape=shape_of((n_blk, tokens, BLK), F32),
        compiler_params=params(),
    )(normed, gate_map)


def out_stage(seq_out, gate, x_tok, out_map, gain=None):
    groups, n_blk, width, _ = seq_out.shape
    tokens = groups * width
    height = tokens + EXTRA * (1 if gain is None else 2)

    def kernel(seq_ref, gate_ref, x_ref, map_ref, *refs):
        n = pl.program_id(0)
        if gain is None:
            res_ref, gated_ref = refs
        else:
            gain_ref, res_ref, normed_ref, gated_ref = refs

        @pl.when(n == 0)
        def _():
            for z in range(n_blk):
                seq = seq_ref[:, z].reshape(tokens, BLK).astype(F32)
                gated_ref[:, z * BLK : (z + 1) * BLK] = (seq * gate_ref[z]).astype(BF16)

        mixed = dot(gated_ref[...], map_ref[0]).astype(BF16).astype(F32)
        res_ref[n, :tokens] = (x_ref[n, :tokens].astype(F32) + mixed).astype(BF16)

        @pl.when(n == n_blk - 1)
        def _():
            blocks = [res_ref[z, :tokens] for z in range(n_blk)]
            place = lax.broadcasted_iota(jnp.int32, (EXTRA, BLK), 0)
            scored = jnp.zeros((EXTRA, BLK), F32)
            for z in range(n_blk):
                for q in range(tokens // STRIDE):
                    row = blocks[z][q * STRIDE : q * STRIDE + 1].astype(F32)
                    scored = jnp.where(place == q * n_blk + z, row, scored)
            for z in range(n_blk):
                res_ref[z, height - EXTRA :] = scored.astype(BF16)
            if gain is None:
                return

            def store(z, value):
                normed_ref[:, z * BLK : (z + 1) * BLK] = value

            normalize(blocks, gain_ref, tokens, store)
            total = squares_by_lane(blocks)
            total = jnp.concatenate([total, total], axis=0)
            high, mid, low = split3(total)
            row = lax.broadcasted_iota(jnp.int32, (EXTRA, tokens), 0)
            rest = jnp.where(row == 1, mid, jnp.where(row == 2, low, 0.0))
            packed = jnp.where(row == 0, high, rest).astype(BF16)
            for z in range(n_blk):
                res_ref[z, tokens : tokens + EXTRA] = packed

    in_specs = [
        whole(seq_out.shape),
        whole(gate.shape),
        whole(x_tok.shape),
        pl.BlockSpec((1, D, BLK), lambda n: (n, 0, 0)),
    ]
    operands = [seq_out, gate, x_tok, out_map]
    out_shape = [shape_of((n_blk, height, BLK))]
    if gain is not None:
        operands.append(gain)
        in_specs.append(whole(gain.shape))
        out_shape.append(shape_of((tokens, D)))
    return pl.pallas_call(
        kernel,
        grid=(n_blk,),
        in_specs=in_specs,
        out_specs=[whole(s.shape) for s in out_shape],
        out_shape=out_shape,
        scratch_shapes=[pltpu.VMEM((tokens, D), BF16)],
        compiler_params=params(),
    )(*operands)


def score_stage(row_sets, heads, labels, first_column, column_step):
    n_blk = row_sets[0].shape[0]
    per_ring = 2 * n_blk
    count = len(row_sets) * per_ring
    groups, _, width = heads.shape
    per_step = 2

    def kernel(first_ref, head_ref, label_ref, *refs):
        out_ref, rows_ref, exp_ref, target_ref = refs[-4:]
        g = pl.program_id(0)

        @pl.when(g == 0)
        def _():
            exp_ref[...] = jnp.zeros_like(exp_ref)
            target_ref[...] = jnp.zeros_like(target_ref)
            for m in range(len(row_sets)):
                for z in range(n_blk):
                    lines = refs[m][z].astype(F32)
                    for q in range(2):
                        at = m * per_ring + z * 2 + q
                        for n in range(n_blk):
                            line = q * n_blk + n
                            rows_ref[at : at + 1, n * BLK : (n + 1) * BLK] = lines[line : line + 1]

        for part in range(per_step):
            logits = dot(rows_ref[...].astype(BF16), head_ref[part])
            start = first_ref[0] + (g * per_step + part) * column_step
            column = lax.broadcasted_iota(jnp.int32, (count, width), 1) + start
            exp_ref[...] += jnp.sum(jnp.exp(logits), axis=1, keepdims=True)
            target_ref[...] += jnp.sum(
                jnp.where(column == label_ref[...], logits, 0.0), axis=1, keepdims=True
            )

        @pl.when(g == groups // per_step - 1)
        def _():
            row = lax.broadcasted_iota(jnp.int32, (count, 128), 0)
            lane = lax.broadcasted_iota(jnp.int32, (count, 128), 1)
            spread = jnp.where(lane == row, exp_ref[...], 0.0)
            spread = spread + jnp.where(lane == row + count, target_ref[...], 0.0)
            out_ref[...] = jnp.sum(spread, axis=0, keepdims=True)

    return pl.pallas_call(
        kernel,
        grid=(groups // per_step,),
        in_specs=[
            scalar_spec(),
            pl.BlockSpec((per_step, D, width), lambda g: (g, 0, 0)),
            whole(labels.shape),
        ]
        + [whole(r.shape) for r in row_sets],
        out_specs=whole((1, 128)),
        out_shape=shape_of((1, 128), F32),
        scratch_shapes=[
            pltpu.VMEM((count, D), F32),
            pltpu.VMEM((count, 1), F32),
            pltpu.VMEM((count, 1), F32),
        ],
        compiler_params=params(),
    )(first_column, heads, labels, *row_sets)


def loss_stage(parts, groups, count):
    def kernel(parts_ref, out_ref):
        total = jnp.sum(parts_ref[...].reshape(groups, -1, 128), axis=1)
        losses = jnp.log(total[:, :count]) - total[:, count : 2 * count]
        for m in range(2):
            out_ref[m] = losses[:, m * count // 2 : (m + 1) * count // 2]

    return pl.pallas_call(
        kernel,
        out_shape=shape_of((2, groups, count // 2), F32),
        compiler_params=params(),
    )(parts)


def body(
    x_in,
    norm_gain,
    right_blocks,
    left_blocks,
    gate_first,
    gate_second,
    out_first,
    out_second,
    head,
    targets,
):
    section = lax.axis_index("section")
    first = section == 0
    tensor_index = lax.axis_index("tensor")
    z_scalar = tensor_index.astype(jnp.int32).reshape(1)
    seq_count = lax.axis_size("seq")
    n_blk = lax.axis_size("tensor")
    everyone = ("seq", "tensor")
    swap = [(0, 1), (1, 0)]
    rows_dev, tokens = right_blocks.shape[1], right_blocks.shape[2]
    j_dev = left_blocks.shape[1]
    p_count = left_blocks.shape[2]

    def by_block(own):
        other = lax.ppermute(own, "section", swap)
        return jnp.where(first, own, other), jnp.where(first, other, own)

    def rows_second(factor):
        return jnp.transpose(factor[0], (2, 1, 0)).reshape(C1, D)

    tie = lax.optimization_barrier

    x_own = lax.dynamic_index_in_dim(x_in, section, 0, keepdims=False).reshape(
        rows_dev, tokens, BLK
    )
    gain_local = by_block(norm_gain)

    packed = pack_stage(x_own, gain_local)
    packed, *own = tie(
        (
            packed,
            right_blocks[0],
            left_blocks[0],
            gate_first[0],
            out_first[0],
            gate_second,
            out_second,
        )
    )
    rights, lefts, gate_firsts, out_firsts = (by_block(w) for w in own[:4])
    gate_seconds, out_seconds = (by_block(rows_second(w)) for w in own[4:])
    x_tok = lax.all_to_all(packed, "tensor", split_axis=0, concat_axis=0, tiled=True)
    gain_rows = x_tok[:, tokens + 3 * rows_dev :][:, :6].astype(F32)
    gain_rows = jnp.sum(gain_rows.reshape(n_blk, 2, 3, BLK), axis=2)
    gains = [gain_rows[:, b : b + 1] for b in range(2)]

    def exchange_seq(mix):
        return lax.all_to_all(mix, "seq", split_axis=0, concat_axis=0, tiled=True)

    def mix_left(cols, b):
        out = left_stage(lefts[b], cols.reshape(p_count * j_dev, BLK))
        return out.reshape(p_count, j_dev, BLK)

    def exchange_all(cols):
        out = lax.all_to_all(cols, everyone, split_axis=0, concat_axis=0, tiled=True)
        return out.reshape(seq_count, n_blk, j_dev, BLK)

    mix = right_stage(x_own, gain_local[0], rights[0], seq_count, shared=x_tok)
    mix, head_own, lefts, gate_firsts, out_firsts, gate_seconds, out_seconds = tie(
        (mix, head[0], lefts, gate_firsts, out_firsts, gate_seconds, out_seconds)
    )
    heads = lax.all_gather(head_own, "seq", axis=0)
    cols = exchange_seq(mix)

    cols = mix_left(cols, 0)
    cols, gate_firsts, out_firsts, gate_seconds, out_seconds = tie(
        (cols, gate_firsts, out_firsts, gate_seconds, out_seconds)
    )
    seq_out = exchange_all(cols)
    normed = token_stage(x_tok, gains[0], tokens)
    gate = gate_stage(normed, channel_map(gate_firsts[0], gate_seconds[0], n_blk))
    out_map = channel_map(out_firsts[0], out_seconds[0], n_blk)
    packed, normed = out_stage(seq_out, gate, x_tok, out_map, gain=gains[1])

    packed, normed, gate_two, out_two, gate_sec, out_sec = tie(
        (packed, normed, gate_firsts[1], out_firsts[1], gate_seconds[1], out_seconds[1])
    )
    chan_one = lax.all_to_all(packed, "tensor", split_axis=0, concat_axis=0, tiled=True)
    gate = gate_stage(normed, channel_map(gate_two, gate_sec, n_blk))
    out_map = channel_map(out_two, out_sec, n_blk)
    mix = right_stage(chan_one, gain_local[1], rights[1], seq_count)
    mix, gate, out_map = tie((mix, gate, out_map))
    seq_out = exchange_all(mix_left(exchange_seq(mix), 1))
    seq_out, heads = tie((seq_out, heads))
    (packed_two,) = out_stage(seq_out, gate, packed, out_map)
    chan_two = lax.all_to_all(packed_two, "tensor", split_axis=0, concat_axis=0, tiled=True)

    rows_one, rows_two = chan_one[:, -EXTRA:], chan_two[:, -EXTRA:]
    kept = jnp.where(first, rows_one, rows_two)
    got = lax.ppermute(jnp.where(first, rows_two, rows_one), "section", swap)
    vocab_dev = head.shape[2]
    labels = lax.dynamic_index_in_dim(
        targets.reshape(2, seq_count, -1), lax.axis_index("seq"), 1, keepdims=False
    )
    labels = jnp.where(first, labels, labels[::-1]).reshape(-1, 1)
    parts = score_stage((kept, got), heads, labels, z_scalar * vocab_dev, n_blk * vocab_dev)
    parts = gather_by_exchange(parts, everyone).reshape(-1, 128)
    losses = loss_stage(parts, seq_count, labels.shape[0])
    aux_losses = jnp.where(first, losses, losses[::-1]).reshape(1, 2, -1)

    chan_one = chan_one[:, :tokens].reshape(rows_dev * tokens, BLK)
    chan_two = chan_two[:, :tokens].reshape(rows_dev * tokens, BLK)
    got_one = lax.ppermute(chan_one, "section", [(1, 0)])
    got_two = lax.ppermute(chan_two, "section", [(0, 1)])
    block_out = jnp.stack(
        [jnp.where(first, chan_one, got_two), jnp.where(first, got_one, chan_two)]
    )[None]
    return (block_out, aux_losses)


def solution(mesh):
    in_specs = (
        P(None, "seq", "tensor"),
        P("section", "tensor"),
        P("section", "seq", None, None),
        P("section", "seq", None, None),
        P("section", None, None, None),
        P("section", None, None, None),
        P("section", None, None, None),
        P("section", None, None, None),
        P("section", None, ("seq", "tensor")),
        P(),
    )
    out_specs = (P("section", None, "seq", "tensor"), P("section", None, None))
    return jax.shard_map(body, mesh=mesh, in_specs=in_specs, out_specs=out_specs, check_vma=False)
```

```python
import jax
import jax.numpy as jnp
from jax import lax
from jax.experimental import pallas as pl
from jax.experimental.pallas import tpu as pltpu
from jax.sharding import PartitionSpec as P

C1 = 32
C2 = 64
D = 2048
STRIDE = 128
EPS = 1e-05
BLK = 256
EXTRA = 16
PER = BLK // C2
VMEM_LIMIT = 48 * 1024 * 1024
F32 = jnp.float32
BF16 = jnp.bfloat16


def params():
    return pltpu.CompilerParams(vmem_limit_bytes=VMEM_LIMIT)


def whole(shape):
    return pl.BlockSpec(shape, lambda *_: (0,) * len(shape))


def scalar_spec():
    return pl.BlockSpec(memory_space=pltpu.SMEM)


def shape_of(shape, dtype=BF16):
    return jax.ShapeDtypeStruct(shape, dtype)


def dot(a, b):
    return jnp.dot(a, b, preferred_element_type=F32)


def gather_by_exchange(block, axis):
    count = lax.axis_size(axis)
    copies = jnp.broadcast_to(block[None], (count,) + block.shape)
    return lax.all_to_all(copies, axis, split_axis=0, concat_axis=0, tiled=True)


def squares_by_lane(x_blocks):
    ones = jnp.ones((8, BLK), BF16)
    dims = (((1,), (1,)), ((), ()))
    total = None
    for x in x_blocks:
        xf = x.astype(F32)
        square = xf * xf
        high = square.astype(BF16)
        low = (square - high.astype(F32)).astype(BF16)
        part = lax.dot_general(ones, high, dims, preferred_element_type=F32) + lax.dot_general(
            ones, low, dims, preferred_element_type=F32
        )
        total = part if total is None else total + part
    return total


def split3(value):
    high = value.astype(BF16).astype(F32)
    mid = (value - high).astype(BF16).astype(F32)
    return high, mid, value - high - mid


def pack_stage(x_own, gains):
    rows, tokens, _ = x_own.shape

    def kernel(x_ref, gain_a_ref, gain_b_ref, out_ref):
        row = lax.broadcasted_iota(jnp.int32, (rows, tokens), 0)
        squares = jnp.zeros((rows, tokens), F32)
        for p in range(rows):
            squares = jnp.where(row == p, squares_by_lane([x_ref[p]]), squares)
        gain_rows = jnp.zeros((rows, BLK), F32)
        for b, gain_ref in enumerate((gain_a_ref, gain_b_ref)):
            for part, value in enumerate(split3(gain_ref[...])):
                gain_rows = jnp.where(row == b * 3 + part, value, gain_rows)
        planes = jnp.concatenate([*split3(squares), gain_rows], axis=0).astype(BF16)
        for p in range(rows):
            out_ref[p, :tokens] = x_ref[p]
            out_ref[p, tokens:] = planes

    return pl.pallas_call(
        kernel,
        out_shape=shape_of((rows, tokens + 4 * rows, BLK)),
        compiler_params=params(),
    )(x_own, *gains)


def right_stage(x_chan, gain_local, right, groups, shared=None):
    rows = right.shape[0]
    tokens = right.shape[1]
    width = tokens // groups
    operands = [x_chan, gain_local, right] + ([] if shared is None else [shared])

    def kernel(x_ref, gain_ref, right_ref, *refs):
        out_ref = refs[-1]
        if shared is not None:
            squares = jnp.zeros((rows, tokens), F32)
            for z in range(shared.shape[0]):
                planes = refs[0][z, tokens:].astype(F32)
                for part in range(3):
                    squares = squares + planes[part * rows : (part + 1) * rows]
        for p in range(rows):
            if shared is None:
                extra = x_ref[p, tokens : tokens + EXTRA].astype(F32)
                total = extra[0:1] + extra[1:2] + extra[2:3]
            else:
                total = squares[p : p + 1]
            scale = lax.rsqrt(total / D + EPS)
            scaled = (right_ref[p].astype(F32) * scale).astype(BF16)
            mix = dot(scaled, x_ref[p, :tokens]) * gain_ref[...]
            out_ref[:, p] = mix.astype(BF16).reshape(groups, width, BLK)

    return pl.pallas_call(
        kernel,
        out_shape=shape_of((groups, rows, width, BLK)),
        compiler_params=params(),
    )(*operands)


def left_stage(left, mix):
    j_count, i_count, p_count = left.shape

    half = BLK // 2

    def kernel(left_ref, mix_ref, out_ref, wide_ref, acc_ref):
        for h in range(2):
            wide_ref[h] = mix_ref[:, h * half : (h + 1) * half].astype(F32)
        for j in range(j_count):
            column = jnp.concatenate(
                [wide_ref[h, pl.ds(j, p_count, stride=j_count), :] for h in range(2)], axis=1
            ).astype(BF16)
            mixed = dot(left_ref[j], column)
            for h in range(2):
                acc_ref[h, pl.ds(j, i_count, stride=j_count), :] = mixed[:, h * half : (h + 1) * half]
        for h in range(2):
            out_ref[:, h * half : (h + 1) * half] = acc_ref[h].astype(BF16)

    return pl.pallas_call(
        kernel,
        out_shape=shape_of((i_count * j_count, BLK)),
        scratch_shapes=[
            pltpu.VMEM((2, p_count * j_count, half), F32),
            pltpu.VMEM((2, i_count * j_count, half), F32),
        ],
        compiler_params=params(),
    )(left, mix)


def channel_map(first, second_rows, n_blk):
    def kernel(first_ref, second_ref, out_ref, spread_ref):
        @pl.when(pl.program_id(0) == 0)
        def _():
            lane = lax.broadcasted_iota(jnp.int32, (BLK, PER * BLK), 1)
            wanted = (lane // BLK) * C2 + lane % C2
            pick = (wanted == lax.broadcasted_iota(jnp.int32, (BLK, PER * BLK), 0)).astype(BF16)
            for g in range(C1 // PER):
                spread = lax.dot_general(
                    first_ref[g * PER : (g + 1) * PER].reshape(BLK, C2),
                    pick,
                    (((0,), (0,)), ((), ())),
                    preferred_element_type=F32,
                ).astype(BF16)
                for r in range(PER):
                    spread_ref[g * PER + r] = spread[:, r * BLK : (r + 1) * BLK]

        for r in range(C1):
            row = second_ref[r : r + 1].astype(F32)
            out_ref[0, r * C2 : (r + 1) * C2] = (spread_ref[r].astype(F32) * row).astype(BF16)

    return pl.pallas_call(
        kernel,
        grid=(n_blk,),
        in_specs=[whole((C1, C2, C2)), pl.BlockSpec((C1, BLK), lambda n: (0, n))],
        out_specs=pl.BlockSpec((1, D, BLK), lambda n: (n, 0, 0)),
        out_shape=shape_of((n_blk, D, BLK)),
        scratch_shapes=[pltpu.VMEM((C1, C2, BLK), BF16)],
        compiler_params=params(),
    )(first, second_rows)


def normalize(x_blocks, gain_ref, tokens, store):
    total = jnp.zeros((tokens, 1), F32)
    for x in x_blocks:
        xf = x.astype(F32)
        total = total + jnp.sum(xf * xf, axis=1, keepdims=True)
    scale = lax.rsqrt(total / D + EPS)
    for n, x in enumerate(x_blocks):
        store(n, (x.astype(F32) * scale * gain_ref[n]).astype(BF16))


def token_stage(x_tok, gain, tokens):
    n_blk = x_tok.shape[0]

    def kernel(gain_ref, x_ref, normed_ref):
        def store(n, value):
            normed_ref[:, n * BLK : (n + 1) * BLK] = value

        normalize([x_ref[n, :tokens] for n in range(n_blk)], gain_ref, tokens, store)

    return pl.pallas_call(
        kernel,
        out_shape=shape_of((tokens, D)),
        compiler_params=params(),
    )(gain, x_tok)


def gate_stage(normed, gate_map):
    tokens = normed.shape[0]
    n_blk = gate_map.shape[0]

    def kernel(normed_ref, map_ref, out_ref):
        pre = dot(normed_ref[...], map_ref[0]).astype(BF16)
        out_ref[0] = jax.nn.sigmoid(pre.astype(F32))

    return pl.pallas_call(
        kernel,
        grid=(n_blk,),
        in_specs=[whole(normed.shape), pl.BlockSpec((1, D, BLK), lambda n: (n, 0, 0))],
        out_specs=pl.BlockSpec((1, tokens, BLK), lambda n: (n, 0, 0)),
        out_shape=shape_of((n_blk, tokens, BLK), F32),
        compiler_params=params(),
    )(normed, gate_map)


def out_stage(seq_out, gate, x_tok, out_map, gain=None):
    groups, n_blk, width, _ = seq_out.shape
    tokens = groups * width
    height = tokens + EXTRA * (1 if gain is None else 2)

    def kernel(seq_ref, gate_ref, x_ref, map_ref, *refs):
        n = pl.program_id(0)
        if gain is None:
            res_ref, gated_ref = refs
        else:
            gain_ref, res_ref, normed_ref, gated_ref = refs

        @pl.when(n == 0)
        def _():
            for z in range(n_blk):
                seq = seq_ref[:, z].reshape(tokens, BLK).astype(F32)
                gated_ref[:, z * BLK : (z + 1) * BLK] = (seq * gate_ref[z]).astype(BF16)

        mixed = dot(gated_ref[...], map_ref[0]).astype(BF16).astype(F32)
        res_ref[n, :tokens] = (x_ref[n, :tokens].astype(F32) + mixed).astype(BF16)

        @pl.when(n == n_blk - 1)
        def _():
            blocks = [res_ref[z, :tokens] for z in range(n_blk)]
            place = lax.broadcasted_iota(jnp.int32, (EXTRA, BLK), 0)
            scored = jnp.zeros((EXTRA, BLK), F32)
            for z in range(n_blk):
                for q in range(tokens // STRIDE):
                    row = blocks[z][q * STRIDE : q * STRIDE + 1].astype(F32)
                    scored = jnp.where(place == q * n_blk + z, row, scored)
            for z in range(n_blk):
                res_ref[z, height - EXTRA :] = scored.astype(BF16)
            if gain is None:
                return

            def store(z, value):
                normed_ref[:, z * BLK : (z + 1) * BLK] = value

            normalize(blocks, gain_ref, tokens, store)
            total = squares_by_lane(blocks)
            total = jnp.concatenate([total, total], axis=0)
            high, mid, low = split3(total)
            row = lax.broadcasted_iota(jnp.int32, (EXTRA, tokens), 0)
            rest = jnp.where(row == 1, mid, jnp.where(row == 2, low, 0.0))
            packed = jnp.where(row == 0, high, rest).astype(BF16)
            for z in range(n_blk):
                res_ref[z, tokens : tokens + EXTRA] = packed

    in_specs = [
        whole(seq_out.shape),
        whole(gate.shape),
        whole(x_tok.shape),
        pl.BlockSpec((1, D, BLK), lambda n: (n, 0, 0)),
    ]
    operands = [seq_out, gate, x_tok, out_map]
    out_shape = [shape_of((n_blk, height, BLK))]
    if gain is not None:
        operands.append(gain)
        in_specs.append(whole(gain.shape))
        out_shape.append(shape_of((tokens, D)))
    return pl.pallas_call(
        kernel,
        grid=(n_blk,),
        in_specs=in_specs,
        out_specs=[whole(s.shape) for s in out_shape],
        out_shape=out_shape,
        scratch_shapes=[pltpu.VMEM((tokens, D), BF16)],
        compiler_params=params(),
    )(*operands)


def score_stage(row_sets, heads, labels, places):
    x_count = len(row_sets)
    pairs = row_sets[0].shape[0]
    n_blk = pairs // 2
    per_set = 2 * pairs
    count = x_count * per_set
    width = heads[0].shape[1]

    def kernel(place_ref, label_ref, *refs):
        out_ref, rows_ref = refs[-2:]
        head_refs = refs[x_count : x_count + len(heads)]
        for d in range(x_count):
            first_row = place_ref[d] * per_set
            for z in range(0, pairs, 4):
                lines = [refs[d][z + k].astype(F32) for k in range(4)]
                group = [lines[k][q * n_blk : (q + 1) * n_blk] for k in range(4) for q in range(2)]
                at = pl.multiple_of(first_row + 2 * z, 8)
                for n in range(n_blk):
                    block = jnp.concatenate([g[n : n + 1] for g in group], axis=0)
                    rows_ref[pl.ds(at, 8), n * BLK : (n + 1) * BLK] = block
        rows = rows_ref[...].astype(BF16)
        exp_sum = jnp.zeros((count, 1), F32)
        target = jnp.zeros((count, 1), F32)
        for d, head_ref in enumerate(head_refs):
            logits = dot(rows, head_ref[...])
            column = lax.broadcasted_iota(jnp.int32, (count, width), 1) + place_ref[x_count + d]
            exp_sum = exp_sum + jnp.sum(jnp.exp(logits), axis=1, keepdims=True)
            target = target + jnp.sum(
                jnp.where(column == label_ref[...], logits, 0.0), axis=1, keepdims=True
            )
        row = lax.broadcasted_iota(jnp.int32, (count, count), 0)
        lane = lax.broadcasted_iota(jnp.int32, (count, count), 1)
        out_ref[0:1] = jnp.sum(jnp.where(lane == row, exp_sum, 0.0), axis=0, keepdims=True)
        out_ref[1:2] = jnp.sum(jnp.where(lane == row, target, 0.0), axis=0, keepdims=True)

    return pl.pallas_call(
        kernel,
        in_specs=[scalar_spec(), whole(labels.shape)]
        + [whole(r.shape) for r in row_sets]
        + [whole(h.shape) for h in heads],
        out_shape=shape_of((2, count), F32),
        scratch_shapes=[pltpu.VMEM((count, D), F32)],
        compiler_params=params(),
    )(places, labels, *row_sets, *heads)


def loss_stage(parts, x_count, y_count):
    count = parts.shape[-1]
    ring = count // (2 * x_count)

    def kernel(parts_ref, out_ref):
        by_place = parts_ref[...].reshape(x_count, y_count, -1, 2, count)
        total = jnp.sum(jnp.sum(by_place, axis=2), axis=0)
        losses = jnp.log(total[:, 0]) - total[:, 1]
        for m in range(2):
            for x in range(x_count):
                at = (x * 2 + m) * ring
                out_ref[m, x] = losses[:, at : at + ring]

    return pl.pallas_call(
        kernel,
        out_shape=shape_of((2, x_count, y_count, ring), F32),
        compiler_params=params(),
    )(parts)


def body(
    x_in,
    norm_gain,
    right_blocks,
    left_blocks,
    gate_first,
    gate_second,
    out_first,
    out_second,
    head,
    targets,
):
    section = lax.axis_index("section")
    first = section == 0
    tensor_index = lax.axis_index("tensor")
    z_scalar = tensor_index.astype(jnp.int32).reshape(1)
    seq_count = lax.axis_size("seq")
    y_count = 4
    x_count = seq_count // y_count
    n_blk = lax.axis_size("tensor")
    everyone = ("seq", "tensor")
    swap = [(0, 1), (1, 0)]
    rows_dev, tokens = right_blocks.shape[1], right_blocks.shape[2]
    j_dev = left_blocks.shape[1]
    p_count = left_blocks.shape[2]

    def by_block(own):
        other = lax.ppermute(own, "section", swap)
        return jnp.where(first, own, other), jnp.where(first, other, own)

    def along_y(block, distance):
        route = [(i, i - i % y_count + (i + distance) % y_count) for i in range(seq_count)]
        return lax.ppermute(block, "seq", route)

    def along_x(block, distance):
        route = [(i, (i + distance * y_count) % seq_count) for i in range(seq_count)]
        return lax.ppermute(block, "seq", route)

    def rows_second(factor):
        return jnp.transpose(factor[0], (2, 1, 0)).reshape(C1, D)

    tie = lax.optimization_barrier

    x_own = lax.dynamic_index_in_dim(x_in, section, 0, keepdims=False).reshape(
        rows_dev, tokens, BLK
    )
    gain_local = by_block(norm_gain)

    packed = pack_stage(x_own, gain_local)
    packed, *own = tie(
        (
            packed,
            right_blocks[0],
            left_blocks[0],
            gate_first[0],
            out_first[0],
            gate_second,
            out_second,
            head[0],
        )
    )
    rights, lefts, gate_firsts, out_firsts = (by_block(w) for w in own[:4])
    gate_seconds, out_seconds = (by_block(rows_second(w)) for w in own[4:6])
    heads = [own[6], along_y(own[6], 1), None, along_y(own[6], 3)]
    x_tok = lax.all_to_all(packed, "tensor", split_axis=0, concat_axis=0, tiled=True)
    gain_rows = x_tok[:, tokens + 3 * rows_dev :][:, :6].astype(F32)
    gain_rows = jnp.sum(gain_rows.reshape(n_blk, 2, 3, BLK), axis=2)
    gains = [gain_rows[:, b : b + 1] for b in range(2)]

    def exchange_seq(mix):
        return lax.all_to_all(mix, "seq", split_axis=0, concat_axis=0, tiled=True)

    def mix_left(cols, b):
        out = left_stage(lefts[b], cols.reshape(p_count * j_dev, BLK))
        return out.reshape(p_count, j_dev, BLK)

    def exchange_all(cols):
        out = lax.all_to_all(cols, everyone, split_axis=0, concat_axis=0, tiled=True)
        return out.reshape(seq_count, n_blk, j_dev, BLK)

    mix = right_stage(x_own, gain_local[0], rights[0], seq_count, shared=x_tok)
    mix, heads[1], heads[3], lefts, gate_firsts, out_firsts, gate_seconds, out_seconds = tie(
        (mix, heads[1], heads[3], lefts, gate_firsts, out_firsts, gate_seconds, out_seconds)
    )
    cols = exchange_seq(mix)

    cols = mix_left(cols, 0)
    cols, gate_firsts, out_firsts, gate_seconds, out_seconds = tie(
        (cols, gate_firsts, out_firsts, gate_seconds, out_seconds)
    )
    seq_out = exchange_all(cols)
    normed = token_stage(x_tok, gains[0], tokens)
    gate = gate_stage(normed, channel_map(gate_firsts[0], gate_seconds[0], n_blk))
    out_map = channel_map(out_firsts[0], out_seconds[0], n_blk)
    packed, normed = out_stage(seq_out, gate, x_tok, out_map, gain=gains[1])

    packed, normed, heads[0], gate_two, out_two, gate_sec, out_sec = tie(
        (packed, normed, heads[0], gate_firsts[1], out_firsts[1], gate_seconds[1], out_seconds[1])
    )
    heads[2] = along_y(heads[0], 2)
    chan_one = lax.all_to_all(packed, "tensor", split_axis=0, concat_axis=0, tiled=True)
    gate = gate_stage(normed, channel_map(gate_two, gate_sec, n_blk))
    out_map = channel_map(out_two, out_sec, n_blk)
    mix = right_stage(chan_one, gain_local[1], rights[1], seq_count)
    mix, gate, out_map, heads[2] = tie((mix, gate, out_map, heads[2]))
    seq_out = exchange_all(mix_left(exchange_seq(mix), 1))
    (packed_two,) = out_stage(seq_out, gate, packed, out_map)
    chan_two = lax.all_to_all(packed_two, "tensor", split_axis=0, concat_axis=0, tiled=True)

    rows_one, rows_two = chan_one[:, -EXTRA:], chan_two[:, -EXTRA:]
    kept = jnp.where(first, rows_one, rows_two)
    got = lax.ppermute(jnp.where(first, rows_two, rows_one), "section", swap)
    rows = jnp.concatenate([kept, got], axis=0)
    row_sets = [rows] + [along_x(rows, d) for d in range(1, x_count)]
    seq_index = lax.axis_index("seq").astype(jnp.int32)
    x_index, y_index = seq_index // y_count, seq_index % y_count
    vocab_dev = head.shape[2]
    labels = targets.reshape(2, x_count, y_count, -1)
    labels = lax.dynamic_index_in_dim(labels, y_index, 2, keepdims=False)
    labels = jnp.transpose(jnp.where(first, labels, labels[::-1]), (1, 0, 2)).reshape(-1, 1)
    places = [(x_index + x_count - d) % x_count for d in range(x_count)]
    for d in range(y_count):
        source = x_index * y_count + (y_index + y_count - d) % y_count
        places.append((source * n_blk + z_scalar[0]) * vocab_dev)
    parts = score_stage(row_sets, heads, labels, jnp.stack(places))
    losses = loss_stage(gather_by_exchange(parts, everyone), x_count, y_count)
    aux_losses = jnp.where(first, losses, losses[::-1]).reshape(1, 2, -1)

    chan_one = chan_one[:, :tokens].reshape(rows_dev * tokens, BLK)
    chan_two = chan_two[:, :tokens].reshape(rows_dev * tokens, BLK)
    got_one = lax.ppermute(chan_one, "section", [(1, 0)])
    got_two = lax.ppermute(chan_two, "section", [(0, 1)])
    block_out = jnp.stack(
        [jnp.where(first, chan_one, got_two), jnp.where(first, got_one, chan_two)]
    )[None]
    return (block_out, aux_losses)


def solution(mesh):
    in_specs = (
        P(None, "seq", "tensor"),
        P("section", "tensor"),
        P("section", "seq", None, None),
        P("section", "seq", None, None),
        P("section", None, None, None),
        P("section", None, None, None),
        P("section", None, None, None),
        P("section", None, None, None),
        P("section", None, ("seq", "tensor")),
        P(),
    )
    out_specs = (P("section", None, "seq", "tensor"), P("section", None, None))
    return jax.shard_map(body, mesh=mesh, in_specs=in_specs, out_specs=out_specs, check_vma=False)
```

```python
import jax
import jax.numpy as jnp
from jax import lax
from jax.experimental import pallas as pl
from jax.experimental.pallas import tpu as pltpu
from jax.sharding import PartitionSpec as P

C1 = 32
C2 = 64
D = 2048
STRIDE = 128
EPS = 1e-05
BLK = 256
EXTRA = 16
PER = BLK // C2
VMEM_LIMIT = 48 * 1024 * 1024
F32 = jnp.float32
BF16 = jnp.bfloat16


def params():
    return pltpu.CompilerParams(vmem_limit_bytes=VMEM_LIMIT)


def whole(shape):
    return pl.BlockSpec(shape, lambda *_: (0,) * len(shape))


def scalar_spec():
    return pl.BlockSpec(memory_space=pltpu.SMEM)


def shape_of(shape, dtype=BF16):
    return jax.ShapeDtypeStruct(shape, dtype)


def dot(a, b):
    return jnp.dot(a, b, preferred_element_type=F32)


def gather_by_exchange(block, axis):
    count = lax.axis_size(axis)
    copies = jnp.broadcast_to(block[None], (count,) + block.shape)
    return lax.all_to_all(copies, axis, split_axis=0, concat_axis=0, tiled=True)


def squares_by_lane(x_blocks):
    ones = jnp.ones((8, BLK), BF16)
    dims = (((1,), (1,)), ((), ()))
    total = None
    for x in x_blocks:
        xf = x.astype(F32)
        square = xf * xf
        high = square.astype(BF16)
        low = (square - high.astype(F32)).astype(BF16)
        part = lax.dot_general(ones, high, dims, preferred_element_type=F32) + lax.dot_general(
            ones, low, dims, preferred_element_type=F32
        )
        total = part if total is None else total + part
    return total


def split3(value):
    high = value.astype(BF16).astype(F32)
    mid = (value - high).astype(BF16).astype(F32)
    return high, mid, value - high - mid


def pack_stage(x_own, gains):
    rows, tokens, _ = x_own.shape

    def kernel(x_ref, gain_a_ref, gain_b_ref, out_ref):
        row = lax.broadcasted_iota(jnp.int32, (rows, tokens), 0)
        squares = jnp.zeros((rows, tokens), F32)
        for p in range(rows):
            squares = jnp.where(row == p, squares_by_lane([x_ref[p]]), squares)
        gain_rows = jnp.zeros((rows, BLK), F32)
        for b, gain_ref in enumerate((gain_a_ref, gain_b_ref)):
            for part, value in enumerate(split3(gain_ref[...])):
                gain_rows = jnp.where(row == b * 3 + part, value, gain_rows)
        planes = jnp.concatenate([*split3(squares), gain_rows], axis=0).astype(BF16)
        for p in range(rows):
            out_ref[p, :tokens] = x_ref[p]
            out_ref[p, tokens:] = planes

    return pl.pallas_call(
        kernel,
        out_shape=shape_of((rows, tokens + 4 * rows, BLK)),
        compiler_params=params(),
    )(x_own, *gains)


def right_stage(x_chan, gain_local, right, groups, shared=None):
    rows = right.shape[0]
    tokens = right.shape[1]
    width = tokens // groups
    operands = [x_chan, gain_local, right] + ([] if shared is None else [shared])

    def kernel(x_ref, gain_ref, right_ref, *refs):
        out_ref = refs[-1]
        if shared is not None:
            squares = jnp.zeros((rows, tokens), F32)
            for z in range(shared.shape[0]):
                planes = refs[0][z, tokens:].astype(F32)
                for part in range(3):
                    squares = squares + planes[part * rows : (part + 1) * rows]
        for p in range(rows):
            if shared is None:
                extra = x_ref[p, tokens : tokens + EXTRA].astype(F32)
                total = extra[0:1] + extra[1:2] + extra[2:3]
            else:
                total = squares[p : p + 1]
            scale = lax.rsqrt(total / D + EPS)
            scaled = (right_ref[p].astype(F32) * scale).astype(BF16)
            mix = dot(scaled, x_ref[p, :tokens]) * gain_ref[...]
            out_ref[:, p] = mix.astype(BF16).reshape(groups, width, BLK)

    return pl.pallas_call(
        kernel,
        out_shape=shape_of((groups, rows, width, BLK)),
        compiler_params=params(),
    )(*operands)


def left_stage(left, mix):
    j_count, i_count, p_count = left.shape

    half = BLK // 2

    def kernel(left_ref, mix_ref, out_ref, wide_ref, acc_ref):
        for h in range(2):
            wide_ref[h] = mix_ref[:, h * half : (h + 1) * half].astype(F32)
        for j in range(j_count):
            column = jnp.concatenate(
                [wide_ref[h, pl.ds(j, p_count, stride=j_count), :] for h in range(2)], axis=1
            ).astype(BF16)
            mixed = dot(left_ref[j], column)
            for h in range(2):
                acc_ref[h, pl.ds(j, i_count, stride=j_count), :] = mixed[:, h * half : (h + 1) * half]
        for h in range(2):
            out_ref[:, h * half : (h + 1) * half] = acc_ref[h].astype(BF16)

    return pl.pallas_call(
        kernel,
        out_shape=shape_of((i_count * j_count, BLK)),
        scratch_shapes=[
            pltpu.VMEM((2, p_count * j_count, half), F32),
            pltpu.VMEM((2, i_count * j_count, half), F32),
        ],
        compiler_params=params(),
    )(left, mix)


def channel_map(first, second_rows, n_blk):
    def kernel(first_ref, second_ref, out_ref, spread_ref):
        @pl.when(pl.program_id(0) == 0)
        def _():
            lane = lax.broadcasted_iota(jnp.int32, (BLK, PER * BLK), 1)
            wanted = (lane // BLK) * C2 + lane % C2
            pick = (wanted == lax.broadcasted_iota(jnp.int32, (BLK, PER * BLK), 0)).astype(BF16)
            for g in range(C1 // PER):
                spread = lax.dot_general(
                    first_ref[g * PER : (g + 1) * PER].reshape(BLK, C2),
                    pick,
                    (((0,), (0,)), ((), ())),
                    preferred_element_type=F32,
                ).astype(BF16)
                for r in range(PER):
                    spread_ref[g * PER + r] = spread[:, r * BLK : (r + 1) * BLK]

        for r in range(C1):
            row = second_ref[r : r + 1].astype(F32)
            out_ref[0, r * C2 : (r + 1) * C2] = (spread_ref[r].astype(F32) * row).astype(BF16)

    return pl.pallas_call(
        kernel,
        grid=(n_blk,),
        in_specs=[whole((C1, C2, C2)), pl.BlockSpec((C1, BLK), lambda n: (0, n))],
        out_specs=pl.BlockSpec((1, D, BLK), lambda n: (n, 0, 0)),
        out_shape=shape_of((n_blk, D, BLK)),
        scratch_shapes=[pltpu.VMEM((C1, C2, BLK), BF16)],
        compiler_params=params(),
    )(first, second_rows)


def normalize(x_blocks, gain_ref, tokens, store):
    total = jnp.zeros((tokens, 1), F32)
    for x in x_blocks:
        xf = x.astype(F32)
        total = total + jnp.sum(xf * xf, axis=1, keepdims=True)
    scale = lax.rsqrt(total / D + EPS)
    for n, x in enumerate(x_blocks):
        store(n, (x.astype(F32) * scale * gain_ref[n]).astype(BF16))


def token_stage(x_tok, gain, tokens):
    n_blk = x_tok.shape[0]

    def kernel(gain_ref, x_ref, normed_ref):
        def store(n, value):
            normed_ref[:, n * BLK : (n + 1) * BLK] = value

        normalize([x_ref[n, :tokens] for n in range(n_blk)], gain_ref, tokens, store)

    return pl.pallas_call(
        kernel,
        out_shape=shape_of((tokens, D)),
        compiler_params=params(),
    )(gain, x_tok)


def gate_stage(normed, gate_map):
    tokens = normed.shape[0]
    n_blk = gate_map.shape[0]

    def kernel(normed_ref, map_ref, out_ref):
        pre = dot(normed_ref[...], map_ref[0]).astype(BF16)
        out_ref[0] = jax.nn.sigmoid(pre.astype(F32))

    return pl.pallas_call(
        kernel,
        grid=(n_blk,),
        in_specs=[whole(normed.shape), pl.BlockSpec((1, D, BLK), lambda n: (n, 0, 0))],
        out_specs=pl.BlockSpec((1, tokens, BLK), lambda n: (n, 0, 0)),
        out_shape=shape_of((n_blk, tokens, BLK), F32),
        compiler_params=params(),
    )(normed, gate_map)


def out_stage(seq_out, gate, x_tok, out_map, gain=None):
    groups, n_blk, width, _ = seq_out.shape
    tokens = groups * width
    height = tokens + (0 if gain is None else EXTRA)

    def kernel(seq_ref, gate_ref, x_ref, map_ref, *refs):
        n = pl.program_id(0)
        if gain is None:
            rows_ref, res_ref, gated_ref = refs
        else:
            gain_ref, rows_ref, res_ref, normed_ref, gated_ref = refs

        @pl.when(n == 0)
        def _():
            for z in range(n_blk):
                seq = seq_ref[:, z].reshape(tokens, BLK).astype(F32)
                gated_ref[:, z * BLK : (z + 1) * BLK] = (seq * gate_ref[z]).astype(BF16)

        mixed = dot(gated_ref[...], map_ref[0]).astype(BF16).astype(F32)
        res_ref[n, :tokens] = (x_ref[n, :tokens].astype(F32) + mixed).astype(BF16)

        @pl.when(n == n_blk - 1)
        def _():
            blocks = [res_ref[z, :tokens] for z in range(n_blk)]
            for z in range(n_blk):
                for q in range(tokens // STRIDE):
                    rows_ref[q : q + 1, z * BLK : (z + 1) * BLK] = blocks[z][
                        q * STRIDE : q * STRIDE + 1
                    ]
            if gain is None:
                return

            def store(z, value):
                normed_ref[:, z * BLK : (z + 1) * BLK] = value

            normalize(blocks, gain_ref, tokens, store)
            total = squares_by_lane(blocks)
            total = jnp.concatenate([total, total], axis=0)
            high, mid, low = split3(total)
            row = lax.broadcasted_iota(jnp.int32, (EXTRA, tokens), 0)
            rest = jnp.where(row == 1, mid, jnp.where(row == 2, low, 0.0))
            packed = jnp.where(row == 0, high, rest).astype(BF16)
            for z in range(n_blk):
                res_ref[z, tokens : tokens + EXTRA] = packed

    in_specs = [
        whole(seq_out.shape),
        whole(gate.shape),
        whole(x_tok.shape),
        pl.BlockSpec((1, D, BLK), lambda n: (n, 0, 0)),
    ]
    operands = [seq_out, gate, x_tok, out_map]
    out_shape = [shape_of((tokens // STRIDE, D)), shape_of((n_blk, height, BLK))]
    if gain is not None:
        operands.append(gain)
        in_specs.append(whole(gain.shape))
        out_shape.append(shape_of((tokens, D)))
    return pl.pallas_call(
        kernel,
        grid=(n_blk,),
        in_specs=in_specs,
        out_specs=[whole(s.shape) for s in out_shape],
        out_shape=out_shape,
        scratch_shapes=[pltpu.VMEM((tokens, D), BF16)],
        compiler_params=params(),
    )(*operands)


def score_stage(row_sets, heads, labels, places):
    x_count = len(row_sets)
    per_set = row_sets[0].shape[0]
    count = x_count * per_set
    width = heads[0].shape[1]

    def kernel(place_ref, label_ref, *refs):
        out_ref, rows_ref = refs[-2:]
        head_refs = refs[x_count : x_count + len(heads)]
        for d in range(x_count):
            rows_ref[place_ref[d]] = refs[d][...]
        rows = rows_ref[...].reshape(count, D)
        exp_sum = jnp.zeros((count, 1), F32)
        target = jnp.zeros((count, 1), F32)
        for d, head_ref in enumerate(head_refs):
            logits = dot(rows, head_ref[...])
            column = lax.broadcasted_iota(jnp.int32, (count, width), 1) + place_ref[x_count + d]
            exp_sum = exp_sum + jnp.sum(jnp.exp(logits), axis=1, keepdims=True)
            target = target + jnp.sum(
                jnp.where(column == label_ref[...], logits, 0.0), axis=1, keepdims=True
            )
        row = lax.broadcasted_iota(jnp.int32, (count, count), 0)
        lane = lax.broadcasted_iota(jnp.int32, (count, count), 1)
        out_ref[0:1] = jnp.sum(jnp.where(lane == row, exp_sum, 0.0), axis=0, keepdims=True)
        out_ref[1:2] = jnp.sum(jnp.where(lane == row, target, 0.0), axis=0, keepdims=True)

    return pl.pallas_call(
        kernel,
        in_specs=[scalar_spec(), whole(labels.shape)]
        + [whole(r.shape) for r in row_sets]
        + [whole(h.shape) for h in heads],
        out_shape=shape_of((2, count), F32),
        scratch_shapes=[pltpu.VMEM((x_count, per_set, D), BF16)],
        compiler_params=params(),
    )(places, labels, *row_sets, *heads)


def loss_stage(parts, x_count, y_count):
    count = parts.shape[-1]
    ring = count // (2 * x_count)

    def kernel(parts_ref, out_ref):
        by_place = parts_ref[...].reshape(x_count, y_count, -1, 2, count)
        total = jnp.sum(jnp.sum(by_place, axis=2), axis=0)
        losses = jnp.log(total[:, 0]) - total[:, 1]
        for m in range(2):
            for x in range(x_count):
                at = (x * 2 + m) * ring
                out_ref[m, x] = losses[:, at : at + ring]

    return pl.pallas_call(
        kernel,
        out_shape=shape_of((2, x_count, y_count, ring), F32),
        compiler_params=params(),
    )(parts)


def result_stage(section, chan_one, got_one, got_two, chan_two, tokens):
    rows = chan_one.shape[0]

    def kernel(section_ref, *refs):
        out_ref = refs[-1]

        @pl.when(section_ref[0] == 0)
        def _():
            out_ref[0] = refs[0][...]
            out_ref[1] = refs[1][...]

        @pl.when(section_ref[0] != 0)
        def _():
            out_ref[0] = refs[2][...]
            out_ref[1] = refs[3][...]

    return pl.pallas_call(
        kernel,
        grid=(rows,),
        in_specs=[scalar_spec()] + [pl.BlockSpec((1, tokens, BLK), lambda p: (p, 0, 0))] * 4,
        out_specs=pl.BlockSpec((2, 1, tokens, BLK), lambda p: (0, p, 0, 0)),
        out_shape=shape_of((2, rows, tokens, BLK)),
        compiler_params=params(),
    )(section, chan_one, got_one, got_two, chan_two)


def body(
    x_in,
    norm_gain,
    right_blocks,
    left_blocks,
    gate_first,
    gate_second,
    out_first,
    out_second,
    head,
    targets,
):
    section = lax.axis_index("section")
    first = section == 0
    tensor_index = lax.axis_index("tensor")
    z_scalar = tensor_index.astype(jnp.int32).reshape(1)
    seq_count = lax.axis_size("seq")
    y_count = 4
    x_count = seq_count // y_count
    n_blk = lax.axis_size("tensor")
    everyone = ("seq", "tensor")
    swap = [(0, 1), (1, 0)]
    rows_dev, tokens = right_blocks.shape[1], right_blocks.shape[2]
    j_dev = left_blocks.shape[1]
    p_count = left_blocks.shape[2]

    def by_block(own):
        other = lax.ppermute(own, "section", swap)
        return jnp.where(first, own, other), jnp.where(first, other, own)

    def along_y(block, distance):
        route = [(i, i - i % y_count + (i + distance) % y_count) for i in range(seq_count)]
        return lax.ppermute(block, "seq", route)

    def along_x(block, distance):
        route = [(i, (i + distance * y_count) % seq_count) for i in range(seq_count)]
        return lax.ppermute(block, "seq", route)

    def rows_second(factor):
        return jnp.transpose(factor[0], (2, 1, 0)).reshape(C1, D)

    tie = lax.optimization_barrier

    x_own = lax.dynamic_index_in_dim(x_in, section, 0, keepdims=False).reshape(
        rows_dev, tokens, BLK
    )
    gain_local = by_block(norm_gain)

    packed = pack_stage(x_own, gain_local)
    packed, *own = tie(
        (
            packed,
            right_blocks[0],
            left_blocks[0],
            gate_first[0],
            out_first[0],
            gate_second,
            out_second,
            head[0],
        )
    )
    rights, lefts, gate_firsts, out_firsts = (by_block(w) for w in own[:4])
    gate_seconds, out_seconds = (by_block(rows_second(w)) for w in own[4:6])
    lefts, head_own = tie((lefts, own[6]))
    heads = [head_own, along_y(head_own, 1), None, along_y(head_own, 3)]
    x_tok = lax.all_to_all(packed, "tensor", split_axis=0, concat_axis=0, tiled=True)
    gain_rows = x_tok[:, tokens + 3 * rows_dev :][:, :6].astype(F32)
    gain_rows = jnp.sum(gain_rows.reshape(n_blk, 2, 3, BLK), axis=2)
    gains = [gain_rows[:, b : b + 1] for b in range(2)]

    def exchange_seq(mix):
        return lax.all_to_all(mix, "seq", split_axis=0, concat_axis=0, tiled=True)

    def mix_left(cols, b):
        out = left_stage(lefts[b], cols.reshape(p_count * j_dev, BLK))
        return out.reshape(p_count, j_dev, BLK)

    def exchange_all(cols):
        out = lax.all_to_all(cols, everyone, split_axis=0, concat_axis=0, tiled=True)
        return out.reshape(seq_count, n_blk, j_dev, BLK)

    mix = right_stage(x_own, gain_local[0], rights[0], seq_count, shared=x_tok)
    mix, heads[1], heads[3], lefts, gate_firsts, out_firsts, gate_seconds, out_seconds = tie(
        (mix, heads[1], heads[3], lefts, gate_firsts, out_firsts, gate_seconds, out_seconds)
    )
    cols = exchange_seq(mix)

    cols = mix_left(cols, 0)
    cols, gate_firsts, out_firsts, gate_seconds, out_seconds = tie(
        (cols, gate_firsts, out_firsts, gate_seconds, out_seconds)
    )
    seq_out = exchange_all(cols)
    normed = token_stage(x_tok, gains[0], tokens)
    gate = gate_stage(normed, channel_map(gate_firsts[0], gate_seconds[0], n_blk))
    out_map = channel_map(out_firsts[0], out_seconds[0], n_blk)
    rows_one, packed, normed = out_stage(seq_out, gate, x_tok, out_map, gain=gains[1])

    packed, normed, heads[0], gate_two, out_two, gate_sec, out_sec = tie(
        (packed, normed, heads[0], gate_firsts[1], out_firsts[1], gate_seconds[1], out_seconds[1])
    )
    heads[2] = along_y(heads[0], 2)
    chan_one = lax.all_to_all(packed, "tensor", split_axis=0, concat_axis=0, tiled=True)
    gate = gate_stage(normed, channel_map(gate_two, gate_sec, n_blk))
    out_map = channel_map(out_two, out_sec, n_blk)
    mix = right_stage(chan_one, gain_local[1], rights[1], seq_count)
    mix, gate, out_map, heads[2] = tie((mix, gate, out_map, heads[2]))
    seq_out = exchange_all(mix_left(exchange_seq(mix), 1))
    rows_two, result = out_stage(seq_out, gate, packed, out_map)

    pair = jnp.stack([rows_one, rows_two])[:, None]
    pair = jnp.broadcast_to(pair, (2, n_blk) + rows_two.shape).reshape((-1,) + rows_two.shape)
    rows = lax.all_to_all(pair, ("section", "tensor"), split_axis=0, concat_axis=0, tiled=True)
    rows, result = tie((rows, result))
    chan_two = lax.all_to_all(result, "tensor", split_axis=0, concat_axis=0, tiled=True)

    rows = rows.reshape(-1, D)
    row_sets = [rows] + [along_x(rows, d) for d in range(1, x_count)]
    seq_index = lax.axis_index("seq").astype(jnp.int32)
    x_index, y_index = seq_index // y_count, seq_index % y_count
    vocab_dev = head.shape[2]
    labels = targets.reshape(2, x_count, y_count, -1)
    labels = lax.dynamic_index_in_dim(labels, y_index, 2, keepdims=False)
    labels = jnp.transpose(labels, (1, 0, 2)).reshape(-1, 1)
    places = [(x_index + x_count - d) % x_count for d in range(x_count)]
    for d in range(y_count):
        source = x_index * y_count + (y_index + y_count - d) % y_count
        places.append((source * n_blk + z_scalar[0]) * vocab_dev)
    parts = score_stage(row_sets, heads, labels, jnp.stack(places))
    parts, chan_two = tie((parts, chan_two))
    sums = gather_by_exchange(parts, everyone)

    got_one = lax.ppermute(chan_one, "section", [(1, 0)])
    got_two = lax.ppermute(chan_two, "section", [(0, 1)])
    scalar = section.astype(jnp.int32).reshape(1)
    block_out = result_stage(scalar, chan_one, got_one, got_two, chan_two, tokens)
    sums, block_out = tie((sums, block_out))
    aux_losses = loss_stage(sums, x_count, y_count).reshape(1, 2, -1)
    block_out = block_out.reshape(1, 2, rows_dev * tokens, BLK)
    return (block_out, aux_losses)


def solution(mesh):
    in_specs = (
        P(None, "seq", "tensor"),
        P("section", "tensor"),
        P("section", "seq", None, None),
        P("section", "seq", None, None),
        P("section", None, None, None),
        P("section", None, None, None),
        P("section", None, None, None),
        P("section", None, None, None),
        P("section", None, ("seq", "tensor")),
        P(),
    )
    out_specs = (P("section", None, "seq", "tensor"), P("section", None, None))
    return jax.shard_map(body, mesh=mesh, in_specs=in_specs, out_specs=out_specs, check_vma=False)
```

```python
import jax
import jax.numpy as jnp
from jax import lax
from jax.experimental import pallas as pl
from jax.experimental.pallas import tpu as pltpu
from jax.sharding import PartitionSpec as P

C1 = 32
C2 = 64
D = 2048
STRIDE = 128
EPS = 1e-05
BLK = 256
EXTRA = 16
PER = BLK // C2
VMEM_LIMIT = 48 * 1024 * 1024
F32 = jnp.float32
BF16 = jnp.bfloat16


def params():
    return pltpu.CompilerParams(vmem_limit_bytes=VMEM_LIMIT)


def whole(shape):
    return pl.BlockSpec(shape, lambda *_: (0,) * len(shape))


def scalar_spec():
    return pl.BlockSpec(memory_space=pltpu.SMEM)


def shape_of(shape, dtype=BF16):
    return jax.ShapeDtypeStruct(shape, dtype)


def dot(a, b):
    return jnp.dot(a, b, preferred_element_type=F32)


def gather_by_exchange(block, axis):
    count = lax.axis_size(axis)
    copies = jnp.broadcast_to(block[None], (count,) + block.shape)
    return lax.all_to_all(copies, axis, split_axis=0, concat_axis=0, tiled=True)


def squares_by_lane(x_blocks):
    ones = jnp.ones((8, BLK), BF16)
    dims = (((1,), (1,)), ((), ()))
    total = None
    for x in x_blocks:
        xf = x.astype(F32)
        square = xf * xf
        high = square.astype(BF16)
        low = (square - high.astype(F32)).astype(BF16)
        part = lax.dot_general(ones, high, dims, preferred_element_type=F32) + lax.dot_general(
            ones, low, dims, preferred_element_type=F32
        )
        total = part if total is None else total + part
    return total


def split3(value):
    high = value.astype(BF16).astype(F32)
    mid = (value - high).astype(BF16).astype(F32)
    return high, mid, value - high - mid


def split_stage(x_own, gains, tensor_index):
    rows, tokens, _ = x_own.shape

    def kernel(z_ref, gain_a_ref, gain_b_ref, x_ref, shared_ref, *send_refs):
        row = lax.broadcasted_iota(jnp.int32, (rows, tokens), 0)
        squares = jnp.zeros((rows, tokens), F32)
        for p in range(rows):
            squares = jnp.where(row == p, squares_by_lane([x_ref[p]]), squares)
        shared_ref[:rows] = squares
        shared_ref[rows:] = jnp.where(row == 0, gain_a_ref[...], gain_b_ref[...])
        for d in range(rows):
            send_refs[d][...] = x_ref[(z_ref[0] + d) % rows]

    outs = [shape_of((2 * rows, tokens), F32)] + [shape_of((tokens, BLK))] * rows
    return pl.pallas_call(
        kernel,
        in_specs=[scalar_spec()] + [whole((1, BLK))] * 2 + [whole(x_own.shape)],
        out_shape=outs,
        compiler_params=params(),
    )(tensor_index, *gains, x_own)


def right_stage(x_chan, gain_local, right, groups, shared=None):
    rows = right.shape[0]
    tokens = right.shape[1]
    width = tokens // groups
    operands = [x_chan, gain_local, right] + ([] if shared is None else [shared])

    def kernel(x_ref, gain_ref, right_ref, *refs):
        out_ref = refs[-1]
        if shared is not None:
            squares = refs[0][0, :rows]
            for z in range(1, shared.shape[0]):
                squares = squares + refs[0][z, :rows]
        for p in range(rows):
            if shared is None:
                extra = x_ref[p, tokens : tokens + EXTRA].astype(F32)
                total = extra[0:1] + extra[1:2] + extra[2:3]
            else:
                total = squares[p : p + 1]
            scale = lax.rsqrt(total / D + EPS)
            scaled = (right_ref[p].astype(F32) * scale).astype(BF16)
            mix = dot(scaled, x_ref[p, :tokens]) * gain_ref[...]
            out_ref[:, p] = mix.astype(BF16).reshape(groups, width, BLK)

    return pl.pallas_call(
        kernel,
        out_shape=shape_of((groups, rows, width, BLK)),
        compiler_params=params(),
    )(*operands)


def left_stage(left, mix):
    j_count, i_count, p_count = left.shape

    half = BLK // 2

    def kernel(left_ref, mix_ref, out_ref, wide_ref, acc_ref):
        for h in range(2):
            wide_ref[h] = mix_ref[:, h * half : (h + 1) * half].astype(F32)
        for j in range(j_count):
            column = jnp.concatenate(
                [wide_ref[h, pl.ds(j, p_count, stride=j_count), :] for h in range(2)], axis=1
            ).astype(BF16)
            mixed = dot(left_ref[j], column)
            for h in range(2):
                acc_ref[h, pl.ds(j, i_count, stride=j_count), :] = mixed[:, h * half : (h + 1) * half]
        for h in range(2):
            out_ref[:, h * half : (h + 1) * half] = acc_ref[h].astype(BF16)

    return pl.pallas_call(
        kernel,
        out_shape=shape_of((i_count * j_count, BLK)),
        scratch_shapes=[
            pltpu.VMEM((2, p_count * j_count, half), F32),
            pltpu.VMEM((2, i_count * j_count, half), F32),
        ],
        compiler_params=params(),
    )(left, mix)


def channel_map(first, second_rows, n_blk):
    def kernel(first_ref, second_ref, out_ref, spread_ref):
        @pl.when(pl.program_id(0) == 0)
        def _():
            lane = lax.broadcasted_iota(jnp.int32, (BLK, PER * BLK), 1)
            wanted = (lane // BLK) * C2 + lane % C2
            pick = (wanted == lax.broadcasted_iota(jnp.int32, (BLK, PER * BLK), 0)).astype(BF16)
            for g in range(C1 // PER):
                spread = lax.dot_general(
                    first_ref[g * PER : (g + 1) * PER].reshape(BLK, C2),
                    pick,
                    (((0,), (0,)), ((), ())),
                    preferred_element_type=F32,
                ).astype(BF16)
                for r in range(PER):
                    spread_ref[g * PER + r] = spread[:, r * BLK : (r + 1) * BLK]

        for r in range(C1):
            row = second_ref[r : r + 1].astype(F32)
            out_ref[0, r * C2 : (r + 1) * C2] = (spread_ref[r].astype(F32) * row).astype(BF16)

    return pl.pallas_call(
        kernel,
        grid=(n_blk,),
        in_specs=[whole((C1, C2, C2)), pl.BlockSpec((C1, BLK), lambda n: (0, n))],
        out_specs=pl.BlockSpec((1, D, BLK), lambda n: (n, 0, 0)),
        out_shape=shape_of((n_blk, D, BLK)),
        scratch_shapes=[pltpu.VMEM((C1, C2, BLK), BF16)],
        compiler_params=params(),
    )(first, second_rows)


def normalize(x_blocks, gain_ref, tokens, store):
    total = jnp.zeros((tokens, 1), F32)
    for x in x_blocks:
        xf = x.astype(F32)
        total = total + jnp.sum(xf * xf, axis=1, keepdims=True)
    scale = lax.rsqrt(total / D + EPS)
    for n, x in enumerate(x_blocks):
        store(n, (x.astype(F32) * scale * gain_ref[n]).astype(BF16))


def token_stage(received, gain, tensor_index):
    n_blk = len(received)
    tokens = received[0].shape[0]

    def kernel(z_ref, gain_ref, *refs):
        x_ref, normed_ref = refs[n_blk:]
        for d in range(n_blk):
            x_ref[(z_ref[0] + n_blk - d) % n_blk] = refs[d][...]

        def store(n, value):
            normed_ref[:, n * BLK : (n + 1) * BLK] = value

        normalize([x_ref[n] for n in range(n_blk)], gain_ref, tokens, store)

    return pl.pallas_call(
        kernel,
        in_specs=[scalar_spec(), whole(gain.shape)] + [whole((tokens, BLK))] * n_blk,
        out_shape=(shape_of((n_blk, tokens, BLK)), shape_of((tokens, D))),
        compiler_params=params(),
    )(tensor_index, gain, *received)


def gate_stage(normed, gate_map):
    tokens = normed.shape[0]
    n_blk = gate_map.shape[0]

    def kernel(normed_ref, map_ref, out_ref):
        pre = dot(normed_ref[...], map_ref[0]).astype(BF16)
        out_ref[0] = jax.nn.sigmoid(pre.astype(F32))

    return pl.pallas_call(
        kernel,
        grid=(n_blk,),
        in_specs=[whole(normed.shape), pl.BlockSpec((1, D, BLK), lambda n: (n, 0, 0))],
        out_specs=pl.BlockSpec((1, tokens, BLK), lambda n: (n, 0, 0)),
        out_shape=shape_of((n_blk, tokens, BLK), F32),
        compiler_params=params(),
    )(normed, gate_map)


def out_stage(seq_out, gate, x_tok, out_map, gain=None):
    groups, n_blk, width, _ = seq_out.shape
    tokens = groups * width
    height = tokens + (0 if gain is None else EXTRA)

    def kernel(seq_ref, gate_ref, x_ref, map_ref, *refs):
        n = pl.program_id(0)
        if gain is None:
            rows_ref, res_ref, gated_ref = refs
        else:
            gain_ref, rows_ref, res_ref, normed_ref, gated_ref = refs

        @pl.when(n == 0)
        def _():
            for z in range(n_blk):
                seq = seq_ref[:, z].reshape(tokens, BLK).astype(F32)
                gated_ref[:, z * BLK : (z + 1) * BLK] = (seq * gate_ref[z]).astype(BF16)

        mixed = dot(gated_ref[...], map_ref[0]).astype(BF16).astype(F32)
        res_ref[n, :tokens] = (x_ref[n, :tokens].astype(F32) + mixed).astype(BF16)

        @pl.when(n == n_blk - 1)
        def _():
            blocks = [res_ref[z, :tokens] for z in range(n_blk)]
            for z in range(n_blk):
                for q in range(tokens // STRIDE):
                    rows_ref[q : q + 1, z * BLK : (z + 1) * BLK] = blocks[z][
                        q * STRIDE : q * STRIDE + 1
                    ]
            if gain is None:
                return

            def store(z, value):
                normed_ref[:, z * BLK : (z + 1) * BLK] = value

            normalize(blocks, gain_ref, tokens, store)
            total = squares_by_lane(blocks)
            total = jnp.concatenate([total, total], axis=0)
            high, mid, low = split3(total)
            row = lax.broadcasted_iota(jnp.int32, (EXTRA, tokens), 0)
            rest = jnp.where(row == 1, mid, jnp.where(row == 2, low, 0.0))
            packed = jnp.where(row == 0, high, rest).astype(BF16)
            for z in range(n_blk):
                res_ref[z, tokens : tokens + EXTRA] = packed

    in_specs = [
        whole(seq_out.shape),
        whole(gate.shape),
        whole(x_tok.shape),
        pl.BlockSpec((1, D, BLK), lambda n: (n, 0, 0)),
    ]
    operands = [seq_out, gate, x_tok, out_map]
    out_shape = [shape_of((tokens // STRIDE, D)), shape_of((n_blk, height, BLK))]
    if gain is not None:
        operands.append(gain)
        in_specs.append(whole(gain.shape))
        out_shape.append(shape_of((tokens, D)))
    return pl.pallas_call(
        kernel,
        grid=(n_blk,),
        in_specs=in_specs,
        out_specs=[whole(s.shape) for s in out_shape],
        out_shape=out_shape,
        scratch_shapes=[pltpu.VMEM((tokens, D), BF16)],
        compiler_params=params(),
    )(*operands)


def score_stage(row_sets, heads, labels, places):
    x_count = len(row_sets)
    per_set = row_sets[0].shape[0]
    count = x_count * per_set
    width = heads[0].shape[1]

    def kernel(place_ref, label_ref, *refs):
        out_ref, rows_ref = refs[-2:]
        head_refs = refs[x_count : x_count + len(heads)]
        for d in range(x_count):
            rows_ref[place_ref[d]] = refs[d][...]
        rows = rows_ref[...].reshape(count, D)
        exp_sum = jnp.zeros((count, 1), F32)
        target = jnp.zeros((count, 1), F32)
        for d, head_ref in enumerate(head_refs):
            logits = dot(rows, head_ref[...])
            column = lax.broadcasted_iota(jnp.int32, (count, width), 1) + place_ref[x_count + d]
            exp_sum = exp_sum + jnp.sum(jnp.exp(logits), axis=1, keepdims=True)
            target = target + jnp.sum(
                jnp.where(column == label_ref[...], logits, 0.0), axis=1, keepdims=True
            )
        row = lax.broadcasted_iota(jnp.int32, (count, count), 0)
        lane = lax.broadcasted_iota(jnp.int32, (count, count), 1)
        out_ref[0:1] = jnp.sum(jnp.where(lane == row, exp_sum, 0.0), axis=0, keepdims=True)
        out_ref[1:2] = jnp.sum(jnp.where(lane == row, target, 0.0), axis=0, keepdims=True)

    return pl.pallas_call(
        kernel,
        in_specs=[scalar_spec(), whole(labels.shape)]
        + [whole(r.shape) for r in row_sets]
        + [whole(h.shape) for h in heads],
        out_shape=shape_of((2, count), F32),
        scratch_shapes=[pltpu.VMEM((x_count, per_set, D), BF16)],
        compiler_params=params(),
    )(places, labels, *row_sets, *heads)


def loss_stage(parts, x_count, y_count):
    count = parts.shape[-1]
    ring = count // (2 * x_count)

    def kernel(parts_ref, out_ref):
        by_place = parts_ref[...].reshape(x_count, y_count, -1, 2, count)
        total = jnp.sum(jnp.sum(by_place, axis=2), axis=0)
        losses = jnp.log(total[:, 0]) - total[:, 1]
        for m in range(2):
            for x in range(x_count):
                at = (x * 2 + m) * ring
                out_ref[m, x] = losses[:, at : at + ring]

    return pl.pallas_call(
        kernel,
        out_shape=shape_of((2, x_count, y_count, ring), F32),
        compiler_params=params(),
    )(parts)


def result_stage(section, chan_one, got_one, got_two, chan_two, tokens):
    rows = chan_one.shape[0]

    def kernel(section_ref, *refs):
        out_ref = refs[-1]

        @pl.when(section_ref[0] == 0)
        def _():
            out_ref[0] = refs[0][...]
            out_ref[1] = refs[1][...]

        @pl.when(section_ref[0] != 0)
        def _():
            out_ref[0] = refs[2][...]
            out_ref[1] = refs[3][...]

    return pl.pallas_call(
        kernel,
        grid=(rows,),
        in_specs=[scalar_spec()] + [pl.BlockSpec((1, tokens, BLK), lambda p: (p, 0, 0))] * 4,
        out_specs=pl.BlockSpec((2, 1, tokens, BLK), lambda p: (0, p, 0, 0)),
        out_shape=shape_of((2, rows, tokens, BLK)),
        compiler_params=params(),
    )(section, chan_one, got_one, got_two, chan_two)


def body(
    x_in,
    norm_gain,
    right_blocks,
    left_blocks,
    gate_first,
    gate_second,
    out_first,
    out_second,
    head,
    targets,
):
    section = lax.axis_index("section")
    first = section == 0
    tensor_index = lax.axis_index("tensor")
    z_scalar = tensor_index.astype(jnp.int32).reshape(1)
    seq_count = lax.axis_size("seq")
    y_count = 4
    x_count = seq_count // y_count
    n_blk = lax.axis_size("tensor")
    everyone = ("seq", "tensor")
    swap = [(0, 1), (1, 0)]
    rows_dev, tokens = right_blocks.shape[1], right_blocks.shape[2]
    j_dev = left_blocks.shape[1]
    p_count = left_blocks.shape[2]

    def by_block(own):
        other = lax.ppermute(own, "section", swap)
        return jnp.where(first, own, other), jnp.where(first, other, own)

    def along_y(block, distance):
        route = [(i, i - i % y_count + (i + distance) % y_count) for i in range(seq_count)]
        return lax.ppermute(block, "seq", route)

    def along_z(block, distance):
        return lax.ppermute(block, "tensor", [(i, (i + distance) % n_blk) for i in range(n_blk)])

    def along_x(block, distance):
        route = [(i, (i + distance * y_count) % seq_count) for i in range(seq_count)]
        return lax.ppermute(block, "seq", route)

    def rows_second(factor):
        return jnp.transpose(factor[0], (2, 1, 0)).reshape(C1, D)

    tie = lax.optimization_barrier

    x_own = lax.dynamic_index_in_dim(x_in, section, 0, keepdims=False).reshape(
        rows_dev, tokens, BLK
    )
    gain_local = by_block(norm_gain)

    shared, *sends = split_stage(x_own, gain_local, z_scalar)
    shared, right_own, left_own = tie((shared, right_blocks[0], left_blocks[0]))
    rights = by_block(right_own)
    near = [1, 2, n_blk - 2, n_blk - 1]
    received = [sends[0]] + [None] * (n_blk - 1)
    for d in near:
        received[d] = along_z(sends[d], d)
    shared = gather_by_exchange(shared, "tensor")
    gains = [shared[:, rows_dev + b][:, None] for b in range(2)]

    def exchange_seq(mix):
        return lax.all_to_all(mix, "seq", split_axis=0, concat_axis=0, tiled=True)

    def mix_left(cols, b):
        out = left_stage(lefts[b], cols.reshape(p_count * j_dev, BLK))
        return out.reshape(p_count, j_dev, BLK)

    def exchange_all(cols):
        out = lax.all_to_all(cols, everyone, split_axis=0, concat_axis=0, tiled=True)
        return out.reshape(seq_count, n_blk, j_dev, BLK)

    mix = right_stage(x_own, gain_local[0], rights[0], seq_count, shared=shared)
    mix, left_own, sends, near_blocks = tie((mix, left_own, sends, [received[d] for d in near]))
    for d, block in zip(near, near_blocks):
        received[d] = block
    cols = exchange_seq(mix)
    lefts = by_block(left_own)
    for d in range(3, n_blk - 2):
        received[d] = along_z(sends[d], d)

    cols = mix_left(cols, 0)
    cols, received, *own = tie(
        (cols, received, gate_first[0], out_first[0], gate_second, out_second)
    )
    seq_out = exchange_all(cols)
    gate_firsts, out_firsts = (by_block(w) for w in own[:2])
    gate_seconds, out_seconds = (by_block(rows_second(w)) for w in own[2:])
    x_tok, normed = token_stage(received, gains[0], z_scalar)
    gate = gate_stage(normed, channel_map(gate_firsts[0], gate_seconds[0], n_blk))
    out_map = channel_map(out_firsts[0], out_seconds[0], n_blk)
    rows_one, packed, normed = out_stage(seq_out, gate, x_tok, out_map, gain=gains[1])

    packed, normed, head_own, gate_two, out_two, gate_sec, out_sec = tie(
        (packed, normed, head[0], gate_firsts[1], out_firsts[1], gate_seconds[1], out_seconds[1])
    )
    heads = [head_own, along_y(head_own, 1), None, along_y(head_own, 3)]
    chan_one = lax.all_to_all(packed, "tensor", split_axis=0, concat_axis=0, tiled=True)
    gate = gate_stage(normed, channel_map(gate_two, gate_sec, n_blk))
    out_map = channel_map(out_two, out_sec, n_blk)
    mix = right_stage(chan_one, gain_local[1], rights[1], seq_count)
    mix, gate, out_map, heads = tie((mix, gate, out_map, [heads[0], heads[1], heads[3]]))
    cols = mix_left(exchange_seq(mix), 1)
    cols, heads = tie((cols, heads))
    seq_out = exchange_all(cols)
    seq_out, far_head = tie((seq_out, along_y(heads[0], 2)))
    heads = [*heads[:2], far_head, heads[2]]
    rows_two, result = out_stage(seq_out, gate, packed, out_map)

    pair = jnp.stack([rows_one, rows_two])[:, None]
    pair = jnp.broadcast_to(pair, (2, n_blk) + rows_two.shape).reshape((-1,) + rows_two.shape)
    rows = lax.all_to_all(pair, ("section", "tensor"), split_axis=0, concat_axis=0, tiled=True)
    rows, result = tie((rows, result))
    chan_two = lax.all_to_all(result, "tensor", split_axis=0, concat_axis=0, tiled=True)

    rows = rows.reshape(-1, D)
    row_sets = [rows] + [along_x(rows, d) for d in range(1, x_count)]
    seq_index = lax.axis_index("seq").astype(jnp.int32)
    x_index, y_index = seq_index // y_count, seq_index % y_count
    vocab_dev = head.shape[2]
    labels = targets.reshape(2, x_count, y_count, -1)
    labels = lax.dynamic_index_in_dim(labels, y_index, 2, keepdims=False)
    labels = jnp.transpose(labels, (1, 0, 2)).reshape(-1, 1)
    places = [(x_index + x_count - d) % x_count for d in range(x_count)]
    for d in range(y_count):
        source = x_index * y_count + (y_index + y_count - d) % y_count
        places.append((source * n_blk + z_scalar[0]) * vocab_dev)
    parts = score_stage(row_sets, heads, labels, jnp.stack(places))
    parts, chan_two = tie((parts, chan_two))
    sums = gather_by_exchange(parts, everyone)

    got_one = lax.ppermute(chan_one, "section", [(1, 0)])
    got_two = lax.ppermute(chan_two, "section", [(0, 1)])
    scalar = section.astype(jnp.int32).reshape(1)
    block_out = result_stage(scalar, chan_one, got_one, got_two, chan_two, tokens)
    sums, block_out = tie((sums, block_out))
    aux_losses = loss_stage(sums, x_count, y_count).reshape(1, 2, -1)
    block_out = block_out.reshape(1, 2, rows_dev * tokens, BLK)
    return (block_out, aux_losses)


def solution(mesh):
    in_specs = (
        P(None, "seq", "tensor"),
        P("section", "tensor"),
        P("section", "seq", None, None),
        P("section", "seq", None, None),
        P("section", None, None, None),
        P("section", None, None, None),
        P("section", None, None, None),
        P("section", None, None, None),
        P("section", None, ("seq", "tensor")),
        P(),
    )
    out_specs = (P("section", None, "seq", "tensor"), P("section", None, None))
    return jax.shard_map(body, mesh=mesh, in_specs=in_specs, out_specs=out_specs, check_vma=False)
```

```python
import jax
import jax.numpy as jnp
from jax import lax
from jax.experimental import pallas as pl
from jax.experimental.pallas import tpu as pltpu
from jax.sharding import PartitionSpec as P

C1 = 32
C2 = 64
D = 2048
STRIDE = 128
EPS = 1e-05
BLK = 256
EXTRA = 16
PER = BLK // C2
VMEM_LIMIT = 48 * 1024 * 1024
F32 = jnp.float32
BF16 = jnp.bfloat16


def params():
    return pltpu.CompilerParams(vmem_limit_bytes=VMEM_LIMIT)


def whole(shape):
    return pl.BlockSpec(shape, lambda *_: (0,) * len(shape))


def scalar_spec():
    return pl.BlockSpec(memory_space=pltpu.SMEM)


def shape_of(shape, dtype=BF16):
    return jax.ShapeDtypeStruct(shape, dtype)


def dot(a, b):
    return jnp.dot(a, b, preferred_element_type=F32)


def gather_by_exchange(block, axis):
    count = lax.axis_size(axis)
    copies = jnp.broadcast_to(block[None], (count,) + block.shape)
    return lax.all_to_all(copies, axis, split_axis=0, concat_axis=0, tiled=True)


def squares_by_lane(x_blocks):
    ones = jnp.ones((8, BLK), BF16)
    dims = (((1,), (1,)), ((), ()))
    total = None
    for x in x_blocks:
        xf = x.astype(F32)
        square = xf * xf
        high = square.astype(BF16)
        low = (square - high.astype(F32)).astype(BF16)
        part = lax.dot_general(ones, high, dims, preferred_element_type=F32) + lax.dot_general(
            ones, low, dims, preferred_element_type=F32
        )
        total = part if total is None else total + part
    return total


def choose(mine_ref, own, other):
    return jnp.where(mine_ref[0] == 1, own.astype(F32), other.astype(F32))


def split3(value):
    high = value.astype(BF16).astype(F32)
    mid = (value - high).astype(BF16).astype(F32)
    return high, mid, value - high - mid


def split_stage(x_own, gains, tensor_index):
    rows, tokens, _ = x_own.shape

    def kernel(z_ref, gain_a_ref, gain_b_ref, x_ref, shared_ref, *send_refs):
        row = lax.broadcasted_iota(jnp.int32, (rows, tokens), 0)
        squares = jnp.zeros((rows, tokens), F32)
        for p in range(rows):
            squares = jnp.where(row == p, squares_by_lane([x_ref[p]]), squares)
        shared_ref[:rows] = squares
        shared_ref[rows:] = jnp.where(row == 0, gain_a_ref[...], gain_b_ref[...])
        for d in range(rows):
            send_refs[d][...] = x_ref[(z_ref[0] + d) % rows]

    outs = [shape_of((2 * rows, tokens), F32)] + [shape_of((tokens, BLK))] * rows
    return pl.pallas_call(
        kernel,
        in_specs=[scalar_spec()] + [whole((1, BLK))] * 2 + [whole(x_own.shape)],
        out_shape=outs,
        compiler_params=params(),
    )(tensor_index, *gains, x_own)


def right_stage(x_chan, gain_local, right, mine, groups, shared=None):
    rows = right[0].shape[0]
    tokens = right[0].shape[1]
    width = tokens // groups
    operands = [mine, *right, x_chan, gain_local] + ([] if shared is None else [shared])

    def kernel(mine_ref, own_ref, other_ref, x_ref, gain_ref, *refs):
        out_ref = refs[-1]
        if shared is not None:
            squares = refs[0][0, :rows]
            for z in range(1, shared.shape[0]):
                squares = squares + refs[0][z, :rows]
        for p in range(rows):
            if shared is None:
                extra = x_ref[p, tokens : tokens + EXTRA].astype(F32)
                total = extra[0:1] + extra[1:2] + extra[2:3]
            else:
                total = squares[p : p + 1]
            scale = lax.rsqrt(total / D + EPS)
            right_row = choose(mine_ref, own_ref[p], other_ref[p])
            scaled = (right_row * scale).astype(BF16)
            mix = dot(scaled, x_ref[p, :tokens]) * gain_ref[...]
            out_ref[:, p] = mix.astype(BF16).reshape(groups, width, BLK)

    return pl.pallas_call(
        kernel,
        in_specs=[scalar_spec()] + [whole(o.shape) for o in operands[1:]],
        out_shape=shape_of((groups, rows, width, BLK)),
        compiler_params=params(),
    )(*operands)


def left_stage(left, mine, mix):
    j_count, i_count, p_count = left[0].shape

    half = BLK // 2

    def kernel(mine_ref, own_ref, other_ref, mix_ref, out_ref, wide_ref, acc_ref):
        for h in range(2):
            wide_ref[h] = mix_ref[:, h * half : (h + 1) * half].astype(F32)
        for j in range(j_count):
            column = jnp.concatenate(
                [wide_ref[h, pl.ds(j, p_count, stride=j_count), :] for h in range(2)], axis=1
            ).astype(BF16)
            factor = choose(mine_ref, own_ref[j], other_ref[j]).astype(BF16)
            mixed = dot(factor, column)
            for h in range(2):
                acc_ref[h, pl.ds(j, i_count, stride=j_count), :] = mixed[:, h * half : (h + 1) * half]
        for h in range(2):
            out_ref[:, h * half : (h + 1) * half] = acc_ref[h].astype(BF16)

    return pl.pallas_call(
        kernel,
        in_specs=[scalar_spec()] + [whole(a.shape) for a in (*left, mix)],
        out_shape=shape_of((i_count * j_count, BLK)),
        scratch_shapes=[
            pltpu.VMEM((2, p_count * j_count, half), F32),
            pltpu.VMEM((2, i_count * j_count, half), F32),
        ],
        compiler_params=params(),
    )(mine, *left, mix)


def spread_first(mine_ref, first_refs, spread_ref):
    lane = lax.broadcasted_iota(jnp.int32, (BLK, PER * BLK), 1)
    wanted = (lane // BLK) * C2 + lane % C2
    pick = (wanted == lax.broadcasted_iota(jnp.int32, (BLK, PER * BLK), 0)).astype(BF16)
    for g in range(C1 // PER):
        group = [f[g * PER : (g + 1) * PER].reshape(BLK, C2) for f in first_refs]
        spread = lax.dot_general(
            choose(mine_ref, *group).astype(BF16),
            pick,
            (((0,), (0,)), ((), ())),
            preferred_element_type=F32,
        ).astype(BF16)
        for r in range(PER):
            spread_ref[g * PER + r] = spread[:, r * BLK : (r + 1) * BLK]


def map_rows(spread_ref, second, r):
    return (spread_ref[r].astype(F32) * second[r : r + 1]).astype(BF16)


def factor_specs():
    return (
        [scalar_spec()]
        + [whole((C1, C2, C2))] * 2
        + [pl.BlockSpec((C1, BLK), lambda n: (0, n))] * 2
    )


def channel_map(first, second, mine, n_blk):
    def kernel(mine_ref, first_a, first_b, second_a, second_b, out_ref, spread_ref):
        @pl.when(pl.program_id(0) == 0)
        def _():
            spread_first(mine_ref, (first_a, first_b), spread_ref)

        second_rows = choose(mine_ref, second_a[...], second_b[...])
        for r in range(C1):
            out_ref[0, r * C2 : (r + 1) * C2] = map_rows(spread_ref, second_rows, r)

    return pl.pallas_call(
        kernel,
        grid=(n_blk,),
        in_specs=factor_specs(),
        out_specs=pl.BlockSpec((1, D, BLK), lambda n: (n, 0, 0)),
        out_shape=shape_of((n_blk, D, BLK)),
        scratch_shapes=[pltpu.VMEM((C1, C2, BLK), BF16)],
        compiler_params=params(),
    )(mine, *first, *second)


def normalize(x_blocks, gain_ref, tokens, store):
    total = jnp.zeros((tokens, 1), F32)
    for x in x_blocks:
        xf = x.astype(F32)
        total = total + jnp.sum(xf * xf, axis=1, keepdims=True)
    scale = lax.rsqrt(total / D + EPS)
    for n, x in enumerate(x_blocks):
        store(n, (x.astype(F32) * scale * gain_ref[n]).astype(BF16))


def token_stage(received, gain, tensor_index):
    n_blk = len(received)
    tokens = received[0].shape[0]

    def kernel(z_ref, gain_ref, *refs):
        x_ref, normed_ref = refs[n_blk:]
        for d in range(n_blk):
            x_ref[(z_ref[0] + n_blk - d) % n_blk] = refs[d][...]

        def store(n, value):
            normed_ref[:, n * BLK : (n + 1) * BLK] = value

        normalize([x_ref[n] for n in range(n_blk)], gain_ref, tokens, store)

    return pl.pallas_call(
        kernel,
        in_specs=[scalar_spec(), whole(gain.shape)] + [whole((tokens, BLK))] * n_blk,
        out_shape=(shape_of((n_blk, tokens, BLK)), shape_of((tokens, D))),
        compiler_params=params(),
    )(tensor_index, gain, *received)


def gate_stage(normed, first, second, mine, n_blk):
    tokens = normed.shape[0]
    parts = 4
    span = D // parts

    def kernel(mine_ref, first_a, first_b, second_a, second_b, normed_ref, out_ref, *scratch):
        spread_ref, *map_refs = scratch

        @pl.when(pl.program_id(0) == 0)
        def _():
            spread_first(mine_ref, (first_a, first_b), spread_ref)

        second_rows = choose(mine_ref, second_a[...], second_b[...])
        pre = jnp.zeros((tokens, BLK), F32)
        for part in range(parts):
            for r in range(span // C2):
                rows = map_rows(spread_ref, second_rows, part * span // C2 + r)
                map_refs[part][r * C2 : (r + 1) * C2] = rows
            pre = pre + dot(normed_ref[:, part * span : (part + 1) * span], map_refs[part][...])
        out_ref[0] = jax.nn.sigmoid(pre.astype(BF16).astype(F32))

    return pl.pallas_call(
        kernel,
        grid=(n_blk,),
        in_specs=factor_specs() + [whole(normed.shape)],
        out_specs=pl.BlockSpec((1, tokens, BLK), lambda n: (n, 0, 0)),
        out_shape=shape_of((n_blk, tokens, BLK), F32),
        scratch_shapes=[pltpu.VMEM((C1, C2, BLK), BF16)] + [pltpu.VMEM((span, BLK), BF16)] * parts,
        compiler_params=params(),
    )(mine, *first, *second, normed)


def out_stage(seq_out, gate, x_tok, out_map, gain=None):
    groups, n_blk, width, _ = seq_out.shape
    tokens = groups * width
    height = tokens + (0 if gain is None else EXTRA)

    def kernel(seq_ref, gate_ref, x_ref, map_ref, *refs):
        n = pl.program_id(0)
        if gain is None:
            rows_ref, res_ref, gated_ref = refs
        else:
            gain_ref, rows_ref, res_ref, normed_ref, gated_ref = refs

        @pl.when(n == 0)
        def _():
            for z in range(n_blk):
                seq = seq_ref[:, z].reshape(tokens, BLK).astype(F32)
                gated_ref[:, z * BLK : (z + 1) * BLK] = (seq * gate_ref[z]).astype(BF16)

        mixed = dot(gated_ref[...], map_ref[0]).astype(BF16).astype(F32)
        res_ref[n, :tokens] = (x_ref[n, :tokens].astype(F32) + mixed).astype(BF16)

        @pl.when(n == n_blk - 1)
        def _():
            blocks = [res_ref[z, :tokens] for z in range(n_blk)]
            for z in range(n_blk):
                for q in range(tokens // STRIDE):
                    rows_ref[q : q + 1, z * BLK : (z + 1) * BLK] = blocks[z][
                        q * STRIDE : q * STRIDE + 1
                    ]
            if gain is None:
                return

            def store(z, value):
                normed_ref[:, z * BLK : (z + 1) * BLK] = value

            normalize(blocks, gain_ref, tokens, store)
            total = squares_by_lane(blocks)
            total = jnp.concatenate([total, total], axis=0)
            high, mid, low = split3(total)
            row = lax.broadcasted_iota(jnp.int32, (EXTRA, tokens), 0)
            rest = jnp.where(row == 1, mid, jnp.where(row == 2, low, 0.0))
            packed = jnp.where(row == 0, high, rest).astype(BF16)
            for z in range(n_blk):
                res_ref[z, tokens : tokens + EXTRA] = packed

    in_specs = [
        whole(seq_out.shape),
        whole(gate.shape),
        whole(x_tok.shape),
        pl.BlockSpec((1, D, BLK), lambda n: (n, 0, 0)),
    ]
    operands = [seq_out, gate, x_tok, out_map]
    out_shape = [shape_of((tokens // STRIDE, D)), shape_of((n_blk, height, BLK))]
    if gain is not None:
        operands.append(gain)
        in_specs.append(whole(gain.shape))
        out_shape.append(shape_of((tokens, D)))
    return pl.pallas_call(
        kernel,
        grid=(n_blk,),
        in_specs=in_specs,
        out_specs=[whole(s.shape) for s in out_shape],
        out_shape=out_shape,
        scratch_shapes=[pltpu.VMEM((tokens, D), BF16)],
        compiler_params=params(),
    )(*operands)


def score_stage(row_sets, heads, labels, places):
    x_count = len(row_sets)
    per_set = row_sets[0].shape[0]
    count = x_count * per_set
    width = heads[0].shape[1]

    def kernel(place_ref, label_ref, *refs):
        out_ref, rows_ref = refs[-2:]
        head_refs = refs[x_count : x_count + len(heads)]
        for d in range(x_count):
            rows_ref[place_ref[d]] = refs[d][...]
        rows = rows_ref[...].reshape(count, D)
        exp_sum = jnp.zeros((count, 1), F32)
        target = jnp.zeros((count, 1), F32)
        for d, head_ref in enumerate(head_refs):
            logits = dot(rows, head_ref[...])
            column = lax.broadcasted_iota(jnp.int32, (count, width), 1) + place_ref[x_count + d]
            exp_sum = exp_sum + jnp.sum(jnp.exp(logits), axis=1, keepdims=True)
            target = target + jnp.sum(
                jnp.where(column == label_ref[...], logits, 0.0), axis=1, keepdims=True
            )
        row = lax.broadcasted_iota(jnp.int32, (count, count), 0)
        lane = lax.broadcasted_iota(jnp.int32, (count, count), 1)
        out_ref[0:1] = jnp.sum(jnp.where(lane == row, exp_sum, 0.0), axis=0, keepdims=True)
        out_ref[1:2] = jnp.sum(jnp.where(lane == row, target, 0.0), axis=0, keepdims=True)

    return pl.pallas_call(
        kernel,
        in_specs=[scalar_spec(), whole(labels.shape)]
        + [whole(r.shape) for r in row_sets]
        + [whole(h.shape) for h in heads],
        out_shape=shape_of((2, count), F32),
        scratch_shapes=[pltpu.VMEM((x_count, per_set, D), BF16)],
        compiler_params=params(),
    )(places, labels, *row_sets, *heads)


def loss_stage(parts, x_count, y_count):
    count = parts.shape[-1]
    ring = count // (2 * x_count)

    def kernel(parts_ref, out_ref):
        by_place = parts_ref[...].reshape(x_count, y_count, -1, 2, count)
        total = jnp.sum(jnp.sum(by_place, axis=2), axis=0)
        losses = jnp.log(total[:, 0]) - total[:, 1]
        for m in range(2):
            for x in range(x_count):
                at = (x * 2 + m) * ring
                out_ref[m, x] = losses[:, at : at + ring]

    return pl.pallas_call(
        kernel,
        out_shape=shape_of((2, x_count, y_count, ring), F32),
        compiler_params=params(),
    )(parts)


def result_stage(section, chan_one, got_one, got_two, chan_two, tokens):
    rows = chan_one.shape[0]

    def kernel(section_ref, *refs):
        out_ref = refs[-1]

        @pl.when(section_ref[0] == 0)
        def _():
            out_ref[0] = refs[0][...]
            out_ref[1] = refs[1][...]

        @pl.when(section_ref[0] != 0)
        def _():
            out_ref[0] = refs[2][...]
            out_ref[1] = refs[3][...]

    return pl.pallas_call(
        kernel,
        grid=(rows,),
        in_specs=[scalar_spec()] + [pl.BlockSpec((1, tokens, BLK), lambda p: (p, 0, 0))] * 4,
        out_specs=pl.BlockSpec((2, 1, tokens, BLK), lambda p: (0, p, 0, 0)),
        out_shape=shape_of((2, rows, tokens, BLK)),
        compiler_params=params(),
    )(section, chan_one, got_one, got_two, chan_two)


def body(
    x_in,
    norm_gain,
    right_blocks,
    left_blocks,
    gate_first,
    gate_second,
    out_first,
    out_second,
    head,
    targets,
):
    section = lax.axis_index("section")
    first = section == 0
    tensor_index = lax.axis_index("tensor")
    z_scalar = tensor_index.astype(jnp.int32).reshape(1)
    seq_count = lax.axis_size("seq")
    y_count = 4
    x_count = seq_count // y_count
    n_blk = lax.axis_size("tensor")
    everyone = ("seq", "tensor")
    swap = [(0, 1), (1, 0)]
    rows_dev, tokens = right_blocks.shape[1], right_blocks.shape[2]
    j_dev = left_blocks.shape[1]
    p_count = left_blocks.shape[2]

    mine = [(section == b).astype(jnp.int32).reshape(1) for b in range(2)]

    def with_other(own):
        return own, lax.ppermute(own, "section", swap)

    def along_y(block, distance):
        route = [(i, i - i % y_count + (i + distance) % y_count) for i in range(seq_count)]
        return lax.ppermute(block, "seq", route)

    def along_z(block, distance):
        return lax.ppermute(block, "tensor", [(i, (i + distance) % n_blk) for i in range(n_blk)])

    def along_x(block, distance):
        route = [(i, (i + distance * y_count) % seq_count) for i in range(seq_count)]
        return lax.ppermute(block, "seq", route)

    def rows_second(factor):
        return jnp.transpose(factor[0], (2, 1, 0)).reshape(C1, D)

    tie = lax.optimization_barrier

    x_own = lax.dynamic_index_in_dim(x_in, section, 0, keepdims=False).reshape(
        rows_dev, tokens, BLK
    )
    gain_other = lax.ppermute(norm_gain, "section", swap)
    gain_local = [jnp.where(section == b, norm_gain, gain_other) for b in range(2)]

    shared, *sends = split_stage(x_own, gain_local, z_scalar)
    shared, right_own, left_own = tie((shared, right_blocks[0], left_blocks[0]))
    right = with_other(right_own)
    near = [1, 2, n_blk - 2, n_blk - 1]
    received = [sends[0]] + [None] * (n_blk - 1)
    for d in near:
        received[d] = along_z(sends[d], d)
    shared = gather_by_exchange(shared, "tensor")
    gains = [shared[:, rows_dev + b][:, None] for b in range(2)]

    def exchange_seq(mix):
        return lax.all_to_all(mix, "seq", split_axis=0, concat_axis=0, tiled=True)

    def mix_left(cols, b):
        out = left_stage(left, mine[b], cols.reshape(p_count * j_dev, BLK))
        return out.reshape(p_count, j_dev, BLK)

    def exchange_all(cols):
        out = lax.all_to_all(cols, everyone, split_axis=0, concat_axis=0, tiled=True)
        return out.reshape(seq_count, n_blk, j_dev, BLK)

    mix = right_stage(x_own, gain_local[0], right, mine[0], seq_count, shared=shared)
    mix, left_own, sends, near_blocks = tie((mix, left_own, sends, [received[d] for d in near]))
    for d, block in zip(near, near_blocks):
        received[d] = block
    cols = exchange_seq(mix)
    left = with_other(left_own)
    for d in range(3, n_blk - 2):
        received[d] = along_z(sends[d], d)

    cols = mix_left(cols, 0)
    cols, received, head_own, *own = tie(
        (cols, received, head[0], gate_first[0], out_first[0], gate_second, out_second)
    )
    seq_out = exchange_all(cols)
    gate_first_pair, out_first_pair = (with_other(w) for w in own[:2])
    gate_second_pair, out_second_pair = (with_other(rows_second(w)) for w in own[2:])
    near_heads = [along_y(head_own, d) for d in (1, 3)]
    x_tok, normed = token_stage(received, gains[0], z_scalar)
    gate = gate_stage(normed, gate_first_pair, gate_second_pair, mine[0], n_blk)
    out_map = channel_map(out_first_pair, out_second_pair, mine[0], n_blk)
    rows_one, packed, normed = out_stage(seq_out, gate, x_tok, out_map, gain=gains[1])

    packed, normed, head_own, near_heads, gate_first_pair, out_first_pair = tie(
        (packed, normed, head_own, near_heads, gate_first_pair, out_first_pair)
    )
    far_head = along_y(head_own, 2)
    chan_one = lax.all_to_all(packed, "tensor", split_axis=0, concat_axis=0, tiled=True)
    gate = gate_stage(normed, gate_first_pair, gate_second_pair, mine[1], n_blk)
    out_map = channel_map(out_first_pair, out_second_pair, mine[1], n_blk)
    mix = right_stage(chan_one, gain_local[1], right, mine[1], seq_count)
    mix, gate, out_map, far_head = tie((mix, gate, out_map, far_head))
    heads = [head_own, near_heads[0], far_head, near_heads[1]]
    seq_out = exchange_all(mix_left(exchange_seq(mix), 1))
    rows_two, result = out_stage(seq_out, gate, packed, out_map)

    pair = jnp.stack([rows_one, rows_two])[:, None]
    pair = jnp.broadcast_to(pair, (2, n_blk) + rows_two.shape).reshape((-1,) + rows_two.shape)
    rows = lax.all_to_all(pair, ("section", "tensor"), split_axis=0, concat_axis=0, tiled=True)
    rows, result = tie((rows, result))
    chan_two = lax.all_to_all(result, "tensor", split_axis=0, concat_axis=0, tiled=True)

    rows = rows.reshape(-1, D)
    row_sets = [rows] + [along_x(rows, d) for d in range(1, x_count)]
    seq_index = lax.axis_index("seq").astype(jnp.int32)
    x_index, y_index = seq_index // y_count, seq_index % y_count
    vocab_dev = head.shape[2]
    labels = targets.reshape(2, x_count, y_count, -1)
    labels = lax.dynamic_index_in_dim(labels, y_index, 2, keepdims=False)
    labels = jnp.transpose(labels, (1, 0, 2)).reshape(-1, 1)
    places = [(x_index + x_count - d) % x_count for d in range(x_count)]
    for d in range(y_count):
        source = x_index * y_count + (y_index + y_count - d) % y_count
        places.append((source * n_blk + z_scalar[0]) * vocab_dev)
    parts = score_stage(row_sets, heads, labels, jnp.stack(places))
    parts, chan_two = tie((parts, chan_two))
    sums = gather_by_exchange(parts, everyone)

    got_one = lax.ppermute(chan_one, "section", [(1, 0)])
    got_two = lax.ppermute(chan_two, "section", [(0, 1)])
    scalar = section.astype(jnp.int32).reshape(1)
    block_out = result_stage(scalar, chan_one, got_one, got_two, chan_two, tokens)
    sums, block_out = tie((sums, block_out))
    aux_losses = loss_stage(sums, x_count, y_count).reshape(1, 2, -1)
    block_out = block_out.reshape(1, 2, rows_dev * tokens, BLK)
    return (block_out, aux_losses)


def solution(mesh):
    in_specs = (
        P(None, "seq", "tensor"),
        P("section", "tensor"),
        P("section", "seq", None, None),
        P("section", "seq", None, None),
        P("section", None, None, None),
        P("section", None, None, None),
        P("section", None, None, None),
        P("section", None, None, None),
        P("section", None, ("seq", "tensor")),
        P(),
    )
    out_specs = (P("section", None, "seq", "tensor"), P("section", None, None))
    return jax.shard_map(body, mesh=mesh, in_specs=in_specs, out_specs=out_specs, check_vma=False)
```

```python
import jax
import jax.numpy as jnp
from jax import lax
from jax.experimental import pallas as pl
from jax.experimental.pallas import tpu as pltpu
from jax.sharding import PartitionSpec as P

C1 = 32
C2 = 64
D = 2048
STRIDE = 128
EPS = 1e-05
BLK = 256
EXTRA = 16
PER = BLK // C2
PARTS = 4
VMEM_LIMIT = 48 * 1024 * 1024
F32 = jnp.float32
BF16 = jnp.bfloat16


def params():
    return pltpu.CompilerParams(vmem_limit_bytes=VMEM_LIMIT)


def whole(shape):
    return pl.BlockSpec(shape, lambda *_: (0,) * len(shape))


def scalar_spec():
    return pl.BlockSpec(memory_space=pltpu.SMEM)


def shape_of(shape, dtype=BF16):
    return jax.ShapeDtypeStruct(shape, dtype)


def dot(a, b):
    return jnp.dot(a, b, preferred_element_type=F32)


def gather_by_exchange(block, axis):
    count = lax.axis_size(axis)
    copies = jnp.broadcast_to(block[None], (count,) + block.shape)
    return lax.all_to_all(copies, axis, split_axis=0, concat_axis=0, tiled=True)


def squares_by_lane(x_blocks):
    ones = jnp.ones((8, BLK), BF16)
    dims = (((1,), (1,)), ((), ()))
    total = None
    for x in x_blocks:
        xf = x.astype(F32)
        square = xf * xf
        high = square.astype(BF16)
        low = (square - high.astype(F32)).astype(BF16)
        part = lax.dot_general(ones, high, dims, preferred_element_type=F32) + lax.dot_general(
            ones, low, dims, preferred_element_type=F32
        )
        total = part if total is None else total + part
    return total


def choose(mine_ref, own, other):
    return jnp.where(mine_ref[0] == 1, own.astype(F32), other.astype(F32))


def split3(value):
    high = value.astype(BF16).astype(F32)
    mid = (value - high).astype(BF16).astype(F32)
    return high, mid, value - high - mid


def split_stage(x_own, gains, tensor_index):
    rows, tokens, _ = x_own.shape

    def kernel(z_ref, gain_a_ref, gain_b_ref, x_ref, shared_ref, *refs):
        send_refs, sems = refs[:rows], refs[rows]
        copies = [
            pltpu.make_async_copy(x_ref.at[(z_ref[0] + d) % rows], send_refs[d], sems.at[d])
            for d in range(rows)
        ]
        for copy in copies:
            copy.start()
        row = lax.broadcasted_iota(jnp.int32, (rows, tokens), 0)
        squares = jnp.zeros((rows, tokens), F32)
        for p in range(rows):
            squares = jnp.where(row == p, squares_by_lane([x_ref[p]]), squares)
        shared_ref[:rows] = squares
        shared_ref[rows:] = jnp.where(row == 0, gain_a_ref[...], gain_b_ref[...])
        for copy in copies:
            copy.wait()

    return pl.pallas_call(
        kernel,
        in_specs=[scalar_spec()] + [whole((1, BLK))] * 2 + [whole(x_own.shape)],
        out_specs=[whole((2 * rows, tokens))] + [pl.BlockSpec(memory_space=pltpu.HBM)] * rows,
        out_shape=[shape_of((2 * rows, tokens), F32)] + [shape_of((tokens, BLK))] * rows,
        scratch_shapes=[pltpu.SemaphoreType.DMA((rows,))],
        compiler_params=params(),
    )(tensor_index, *gains, x_own)


def right_stage(x_chan, gain_local, right, mine, groups, shared=None):
    rows = right[0].shape[0]
    tokens = right[0].shape[1]
    width = tokens // groups
    operands = [mine, *right, x_chan, gain_local] + ([] if shared is None else [shared])

    def kernel(mine_ref, own_ref, other_ref, x_ref, gain_ref, *refs):
        out_ref = refs[-1]
        if shared is not None:
            squares = refs[0][0, :rows]
            for z in range(1, shared.shape[0]):
                squares = squares + refs[0][z, :rows]
        for p in range(rows):
            if shared is None:
                extra = x_ref[p, tokens : tokens + EXTRA].astype(F32)
                total = extra[0:1] + extra[1:2] + extra[2:3]
            else:
                total = squares[p : p + 1]
            scale = lax.rsqrt(total / D + EPS)
            right_row = choose(mine_ref, own_ref[p], other_ref[p])
            scaled = (right_row * scale).astype(BF16)
            mix = dot(scaled, x_ref[p, :tokens]) * gain_ref[...]
            out_ref[:, p] = mix.astype(BF16).reshape(groups, width, BLK)

    return pl.pallas_call(
        kernel,
        in_specs=[scalar_spec()] + [whole(o.shape) for o in operands[1:]],
        out_shape=shape_of((groups, rows, width, BLK)),
        compiler_params=params(),
    )(*operands)


def left_stage(left, mine, mix):
    j_count, i_count, p_count = left[0].shape

    half = BLK // 2

    def kernel(mine_ref, own_ref, other_ref, mix_ref, out_ref, wide_ref, acc_ref):
        for h in range(2):
            wide_ref[h] = mix_ref[:, h * half : (h + 1) * half].astype(F32)
        for j in range(j_count):
            column = jnp.concatenate(
                [wide_ref[h, pl.ds(j, p_count, stride=j_count), :] for h in range(2)], axis=1
            ).astype(BF16)
            factor = choose(mine_ref, own_ref[j], other_ref[j]).astype(BF16)
            mixed = dot(factor, column)
            for h in range(2):
                acc_ref[h, pl.ds(j, i_count, stride=j_count), :] = mixed[:, h * half : (h + 1) * half]
        for h in range(2):
            out_ref[:, h * half : (h + 1) * half] = acc_ref[h].astype(BF16)

    return pl.pallas_call(
        kernel,
        in_specs=[scalar_spec()] + [whole(a.shape) for a in (*left, mix)],
        out_shape=shape_of((i_count * j_count, BLK)),
        scratch_shapes=[
            pltpu.VMEM((2, p_count * j_count, half), F32),
            pltpu.VMEM((2, i_count * j_count, half), F32),
        ],
        compiler_params=params(),
    )(mine, *left, mix)


def spread_first(mine_ref, first_refs, spread_ref):
    lane = lax.broadcasted_iota(jnp.int32, (BLK, PER * BLK), 1)
    wanted = (lane // BLK) * C2 + lane % C2
    pick = (wanted == lax.broadcasted_iota(jnp.int32, (BLK, PER * BLK), 0)).astype(BF16)
    for g in range(C1 // PER):
        group = [f[g * PER : (g + 1) * PER].reshape(BLK, C2) for f in first_refs]
        spread = lax.dot_general(
            choose(mine_ref, *group).astype(BF16),
            pick,
            (((0,), (0,)), ((), ())),
            preferred_element_type=F32,
        ).astype(BF16)
        for r in range(PER):
            spread_ref[g * PER + r] = spread[:, r * BLK : (r + 1) * BLK]


def map_rows(spread_ref, second, r):
    return (spread_ref[r].astype(F32) * second[r : r + 1]).astype(BF16)


def factor_specs():
    return (
        [scalar_spec()]
        + [whole((C1, C2, C2))] * 2
        + [pl.BlockSpec((C1, BLK), lambda n: (0, n))] * 2
    )


def mix_channels(values_ref, spread_ref, second, map_refs):
    span = D // len(map_refs)
    total = jnp.zeros((values_ref.shape[0], BLK), F32)
    for part, map_ref in enumerate(map_refs):
        for r in range(span // C2):
            map_ref[r * C2 : (r + 1) * C2] = map_rows(spread_ref, second, part * span // C2 + r)
        total = total + dot(values_ref[:, part * span : (part + 1) * span], map_ref[...])
    return total.astype(BF16)


def map_scratch():
    return [pltpu.VMEM((C1, C2, BLK), BF16)] + [pltpu.VMEM((D // PARTS, BLK), BF16)] * PARTS


def normalize(x_blocks, gain_ref, tokens, store):
    total = jnp.zeros((tokens, 1), F32)
    for x in x_blocks:
        xf = x.astype(F32)
        total = total + jnp.sum(xf * xf, axis=1, keepdims=True)
    scale = lax.rsqrt(total / D + EPS)
    for n, x in enumerate(x_blocks):
        store(n, (x.astype(F32) * scale * gain_ref[n]).astype(BF16))


def token_stage(received, gain, tensor_index):
    n_blk = len(received)
    tokens = received[0].shape[0]

    def kernel(z_ref, gain_ref, *refs):
        x_ref, normed_ref = refs[n_blk:]
        for d in range(n_blk):
            x_ref[(z_ref[0] + n_blk - d) % n_blk] = refs[d][...]

        def store(n, value):
            normed_ref[:, n * BLK : (n + 1) * BLK] = value

        normalize([x_ref[n] for n in range(n_blk)], gain_ref, tokens, store)

    return pl.pallas_call(
        kernel,
        in_specs=[scalar_spec(), whole(gain.shape)] + [whole((tokens, BLK))] * n_blk,
        out_shape=(shape_of((n_blk, tokens, BLK)), shape_of((tokens, D))),
        compiler_params=params(),
    )(tensor_index, gain, *received)


def gate_stage(normed, first, second, mine, n_blk):
    tokens = normed.shape[0]

    def kernel(mine_ref, first_a, first_b, second_a, second_b, normed_ref, out_ref, *scratch):
        spread_ref, *map_refs = scratch

        @pl.when(pl.program_id(0) == 0)
        def _():
            spread_first(mine_ref, (first_a, first_b), spread_ref)

        second_rows = choose(mine_ref, second_a[...], second_b[...])
        pre = mix_channels(normed_ref, spread_ref, second_rows, map_refs)
        out_ref[0] = jax.nn.sigmoid(pre.astype(F32))

    return pl.pallas_call(
        kernel,
        grid=(n_blk,),
        in_specs=factor_specs() + [whole(normed.shape)],
        out_specs=pl.BlockSpec((1, tokens, BLK), lambda n: (n, 0, 0)),
        out_shape=shape_of((n_blk, tokens, BLK), F32),
        scratch_shapes=map_scratch(),
        compiler_params=params(),
    )(mine, *first, *second, normed)


def out_stage(seq_out, gate, x_tok, first, second, mine, gain=None):
    groups, n_blk, width, _ = seq_out.shape
    tokens = groups * width
    height = tokens + (0 if gain is None else EXTRA)

    def kernel(mine_ref, first_a, first_b, second_a, second_b, seq_ref, gate_ref, x_ref, *refs):
        n = pl.program_id(0)
        gated_ref, spread_ref, *map_refs = refs[-2 - PARTS :]
        if gain is None:
            rows_ref, res_ref = refs[:2]
        else:
            gain_ref, rows_ref, res_ref, normed_ref = refs[:4]

        @pl.when(n == 0)
        def _():
            spread_first(mine_ref, (first_a, first_b), spread_ref)
            for z in range(n_blk):
                seq = seq_ref[:, z].reshape(tokens, BLK).astype(F32)
                gated_ref[:, z * BLK : (z + 1) * BLK] = (seq * gate_ref[z]).astype(BF16)

        second_rows = choose(mine_ref, second_a[...], second_b[...])
        mixed = mix_channels(gated_ref, spread_ref, second_rows, map_refs).astype(F32)
        res_ref[n, :tokens] = (x_ref[n, :tokens].astype(F32) + mixed).astype(BF16)

        @pl.when(n == n_blk - 1)
        def _():
            blocks = [res_ref[z, :tokens] for z in range(n_blk)]
            for z in range(n_blk):
                for q in range(tokens // STRIDE):
                    rows_ref[q : q + 1, z * BLK : (z + 1) * BLK] = blocks[z][
                        q * STRIDE : q * STRIDE + 1
                    ]
            if gain is None:
                return

            def store(z, value):
                normed_ref[:, z * BLK : (z + 1) * BLK] = value

            normalize(blocks, gain_ref, tokens, store)
            total = squares_by_lane(blocks)
            total = jnp.concatenate([total, total], axis=0)
            high, mid, low = split3(total)
            row = lax.broadcasted_iota(jnp.int32, (EXTRA, tokens), 0)
            rest = jnp.where(row == 1, mid, jnp.where(row == 2, low, 0.0))
            packed = jnp.where(row == 0, high, rest).astype(BF16)
            for z in range(n_blk):
                res_ref[z, tokens : tokens + EXTRA] = packed

    in_specs = factor_specs() + [whole(a.shape) for a in (seq_out, gate, x_tok)]
    operands = [mine, *first, *second, seq_out, gate, x_tok]
    out_shape = [shape_of((tokens // STRIDE, D)), shape_of((n_blk, height, BLK))]
    if gain is not None:
        operands.append(gain)
        in_specs.append(whole(gain.shape))
        out_shape.append(shape_of((tokens, D)))
    return pl.pallas_call(
        kernel,
        grid=(n_blk,),
        in_specs=in_specs,
        out_specs=[whole(s.shape) for s in out_shape],
        out_shape=out_shape,
        scratch_shapes=[pltpu.VMEM((tokens, D), BF16)] + map_scratch(),
        compiler_params=params(),
    )(*operands)


def score_stage(row_sets, heads, labels, places):
    x_count = len(row_sets)
    per_set = row_sets[0].shape[0]
    count = x_count * per_set
    width = heads[0].shape[1]

    def kernel(place_ref, label_ref, *refs):
        out_ref, rows_ref = refs[-2:]
        head_refs = refs[x_count : x_count + len(heads)]
        for d in range(x_count):
            rows_ref[place_ref[d]] = refs[d][...]
        rows = rows_ref[...].reshape(count, D)
        exp_sum = jnp.zeros((count, 1), F32)
        target = jnp.zeros((count, 1), F32)
        for d, head_ref in enumerate(head_refs):
            logits = dot(rows, head_ref[...])
            column = lax.broadcasted_iota(jnp.int32, (count, width), 1) + place_ref[x_count + d]
            exp_sum = exp_sum + jnp.sum(jnp.exp(logits), axis=1, keepdims=True)
            target = target + jnp.sum(
                jnp.where(column == label_ref[...], logits, 0.0), axis=1, keepdims=True
            )
        row = lax.broadcasted_iota(jnp.int32, (count, count), 0)
        lane = lax.broadcasted_iota(jnp.int32, (count, count), 1)
        out_ref[0:1] = jnp.sum(jnp.where(lane == row, exp_sum, 0.0), axis=0, keepdims=True)
        out_ref[1:2] = jnp.sum(jnp.where(lane == row, target, 0.0), axis=0, keepdims=True)

    return pl.pallas_call(
        kernel,
        in_specs=[scalar_spec(), whole(labels.shape)]
        + [whole(r.shape) for r in row_sets]
        + [whole(h.shape) for h in heads],
        out_shape=shape_of((2, count), F32),
        scratch_shapes=[pltpu.VMEM((x_count, per_set, D), BF16)],
        compiler_params=params(),
    )(places, labels, *row_sets, *heads)


def loss_stage(parts, x_count, y_count):
    count = parts.shape[-1]
    ring = count // (2 * x_count)

    def kernel(parts_ref, out_ref):
        by_place = parts_ref[...].reshape(x_count, y_count, -1, 2, count)
        total = jnp.sum(jnp.sum(by_place, axis=2), axis=0)
        losses = jnp.log(total[:, 0]) - total[:, 1]
        for m in range(2):
            for x in range(x_count):
                at = (x * 2 + m) * ring
                out_ref[m, x] = losses[:, at : at + ring]

    return pl.pallas_call(
        kernel,
        out_shape=shape_of((2, x_count, y_count, ring), F32),
        compiler_params=params(),
    )(parts)


def result_stage(section, chan_one, got_one, got_two, chan_two, tokens):
    rows = chan_one.shape[0]

    def kernel(section_ref, *refs):
        out_ref = refs[-1]

        @pl.when(section_ref[0] == 0)
        def _():
            out_ref[0] = refs[0][...]
            out_ref[1] = refs[1][...]

        @pl.when(section_ref[0] != 0)
        def _():
            out_ref[0] = refs[2][...]
            out_ref[1] = refs[3][...]

    return pl.pallas_call(
        kernel,
        grid=(rows,),
        in_specs=[scalar_spec()] + [pl.BlockSpec((1, tokens, BLK), lambda p: (p, 0, 0))] * 4,
        out_specs=pl.BlockSpec((2, 1, tokens, BLK), lambda p: (0, p, 0, 0)),
        out_shape=shape_of((2, rows, tokens, BLK)),
        compiler_params=params(),
    )(section, chan_one, got_one, got_two, chan_two)


def body(
    x_in,
    norm_gain,
    right_blocks,
    left_blocks,
    gate_first,
    gate_second,
    out_first,
    out_second,
    head,
    targets,
):
    section = lax.axis_index("section")
    first = section == 0
    tensor_index = lax.axis_index("tensor")
    z_scalar = tensor_index.astype(jnp.int32).reshape(1)
    seq_count = lax.axis_size("seq")
    y_count = 4
    x_count = seq_count // y_count
    n_blk = lax.axis_size("tensor")
    everyone = ("seq", "tensor")
    swap = [(0, 1), (1, 0)]
    rows_dev, tokens = right_blocks.shape[1], right_blocks.shape[2]
    j_dev = left_blocks.shape[1]
    p_count = left_blocks.shape[2]

    mine = [(section == b).astype(jnp.int32).reshape(1) for b in range(2)]

    def with_other(own):
        return own, lax.ppermute(own, "section", swap)

    def along_y(block, distance):
        route = [(i, i - i % y_count + (i + distance) % y_count) for i in range(seq_count)]
        return lax.ppermute(block, "seq", route)

    def along_z(block, distance):
        return lax.ppermute(block, "tensor", [(i, (i + distance) % n_blk) for i in range(n_blk)])

    def along_x(block, distance):
        route = [(i, (i + distance * y_count) % seq_count) for i in range(seq_count)]
        return lax.ppermute(block, "seq", route)

    def rows_second(factor):
        return jnp.transpose(factor[0], (2, 1, 0)).reshape(C1, D)

    tie = lax.optimization_barrier

    x_own = lax.dynamic_index_in_dim(x_in, section, 0, keepdims=False).reshape(
        rows_dev, tokens, BLK
    )
    gain_other = lax.ppermute(norm_gain, "section", swap)
    gain_local = [jnp.where(section == b, norm_gain, gain_other) for b in range(2)]

    shared, *sends = split_stage(x_own, gain_local, z_scalar)
    shared, right_own, left_own = tie((shared, right_blocks[0], left_blocks[0]))
    right = with_other(right_own)
    near = [1, 2, n_blk - 2, n_blk - 1]
    received = [sends[0]] + [None] * (n_blk - 1)
    for d in near:
        received[d] = along_z(sends[d], d)
    shared = gather_by_exchange(shared, "tensor")
    gains = [shared[:, rows_dev + b][:, None] for b in range(2)]

    def exchange_seq(mix):
        return lax.all_to_all(mix, "seq", split_axis=0, concat_axis=0, tiled=True)

    def mix_left(cols, b):
        out = left_stage(left, mine[b], cols.reshape(p_count * j_dev, BLK))
        return out.reshape(p_count, j_dev, BLK)

    def exchange_all(cols):
        out = lax.all_to_all(cols, everyone, split_axis=0, concat_axis=0, tiled=True)
        return out.reshape(seq_count, n_blk, j_dev, BLK)

    mix = right_stage(x_own, gain_local[0], right, mine[0], seq_count, shared=shared)
    mix, left_own, sends, near_blocks = tie((mix, left_own, sends, [received[d] for d in near]))
    for d, block in zip(near, near_blocks):
        received[d] = block
    cols = exchange_seq(mix)
    left = with_other(left_own)
    for d in range(3, n_blk - 2):
        received[d] = along_z(sends[d], d)

    cols = mix_left(cols, 0)
    cols, received, head_own, *own = tie(
        (cols, received, head[0], gate_first[0], out_first[0], gate_second, out_second)
    )
    seq_out = exchange_all(cols)
    gate_first_pair, out_first_pair = (with_other(w) for w in own[:2])
    gate_second_pair, out_second_pair = (with_other(rows_second(w)) for w in own[2:])
    near_heads = [along_y(head_own, d) for d in (1, 3)]
    x_tok, normed = token_stage(received, gains[0], z_scalar)
    gate = gate_stage(normed, gate_first_pair, gate_second_pair, mine[0], n_blk)
    rows_one, packed, normed = out_stage(
        seq_out, gate, x_tok, out_first_pair, out_second_pair, mine[0], gain=gains[1]
    )

    packed, normed, head_own, near_heads, gate_first_pair, out_first_pair = tie(
        (packed, normed, head_own, near_heads, gate_first_pair, out_first_pair)
    )
    far_head = along_y(head_own, 2)
    chan_one = lax.all_to_all(packed, "tensor", split_axis=0, concat_axis=0, tiled=True)
    gate = gate_stage(normed, gate_first_pair, gate_second_pair, mine[1], n_blk)
    mix = right_stage(chan_one, gain_local[1], right, mine[1], seq_count)
    mix, gate, far_head = tie((mix, gate, far_head))
    heads = [head_own, near_heads[0], far_head, near_heads[1]]
    seq_out = exchange_all(mix_left(exchange_seq(mix), 1))
    rows_two, result = out_stage(
        seq_out, gate, packed, out_first_pair, out_second_pair, mine[1]
    )

    pair = jnp.stack([rows_one, rows_two])[:, None]
    pair = jnp.broadcast_to(pair, (2, n_blk) + rows_two.shape).reshape((-1,) + rows_two.shape)
    rows = lax.all_to_all(pair, ("section", "tensor"), split_axis=0, concat_axis=0, tiled=True)
    rows, result = tie((rows, result))
    chan_two = lax.all_to_all(result, "tensor", split_axis=0, concat_axis=0, tiled=True)

    rows = rows.reshape(-1, D)
    row_sets = [rows] + [along_x(rows, d) for d in range(1, x_count)]
    seq_index = lax.axis_index("seq").astype(jnp.int32)
    x_index, y_index = seq_index // y_count, seq_index % y_count
    vocab_dev = head.shape[2]
    labels = targets.reshape(2, x_count, y_count, -1)
    labels = lax.dynamic_index_in_dim(labels, y_index, 2, keepdims=False)
    labels = jnp.transpose(labels, (1, 0, 2)).reshape(-1, 1)
    places = [(x_index + x_count - d) % x_count for d in range(x_count)]
    for d in range(y_count):
        source = x_index * y_count + (y_index + y_count - d) % y_count
        places.append((source * n_blk + z_scalar[0]) * vocab_dev)
    parts = score_stage(row_sets, heads, labels, jnp.stack(places))
    parts, chan_two = tie((parts, chan_two))
    sums = gather_by_exchange(parts, everyone)

    got_one = lax.ppermute(chan_one, "section", [(1, 0)])
    got_two = lax.ppermute(chan_two, "section", [(0, 1)])
    scalar = section.astype(jnp.int32).reshape(1)
    block_out = result_stage(scalar, chan_one, got_one, got_two, chan_two, tokens)
    sums, block_out = tie((sums, block_out))
    aux_losses = loss_stage(sums, x_count, y_count).reshape(1, 2, -1)
    block_out = block_out.reshape(1, 2, rows_dev * tokens, BLK)
    return (block_out, aux_losses)


def solution(mesh):
    in_specs = (
        P(None, "seq", "tensor"),
        P("section", "tensor"),
        P("section", "seq", None, None),
        P("section", "seq", None, None),
        P("section", None, None, None),
        P("section", None, None, None),
        P("section", None, None, None),
        P("section", None, None, None),
        P("section", None, ("seq", "tensor")),
        P(),
    )
    out_specs = (P("section", None, "seq", "tensor"), P("section", None, None))
    return jax.shard_map(body, mesh=mesh, in_specs=in_specs, out_specs=out_specs, check_vma=False)
```

```python
import jax
import jax.numpy as jnp
from jax import lax
from jax.experimental import pallas as pl
from jax.experimental.pallas import tpu as pltpu
from jax.sharding import PartitionSpec as P

C1 = 32
C2 = 64
D = 2048
STRIDE = 128
EPS = 1e-05
BLK = 256
EXTRA = 16
PER = BLK // C2
PARTS = 4
VMEM_LIMIT = 48 * 1024 * 1024
F32 = jnp.float32
BF16 = jnp.bfloat16


def params():
    return pltpu.CompilerParams(vmem_limit_bytes=VMEM_LIMIT)


def whole(shape):
    return pl.BlockSpec(shape, lambda *_: (0,) * len(shape))


def scalar_spec():
    return pl.BlockSpec(memory_space=pltpu.SMEM)


def shape_of(shape, dtype=BF16):
    return jax.ShapeDtypeStruct(shape, dtype)


def dot(a, b):
    return jnp.dot(a, b, preferred_element_type=F32)


def gather_by_exchange(block, axis):
    count = lax.axis_size(axis)
    copies = jnp.broadcast_to(block[None], (count,) + block.shape)
    return lax.all_to_all(copies, axis, split_axis=0, concat_axis=0, tiled=True)


def squares_by_lane(x_blocks):
    ones = jnp.ones((8, BLK), BF16)
    dims = (((1,), (1,)), ((), ()))
    total = None
    for x in x_blocks:
        xf = x.astype(F32)
        square = xf * xf
        high = square.astype(BF16)
        low = (square - high.astype(F32)).astype(BF16)
        part = lax.dot_general(ones, high, dims, preferred_element_type=F32) + lax.dot_general(
            ones, low, dims, preferred_element_type=F32
        )
        total = part if total is None else total + part
    return total


def choose(mine_ref, own, other):
    return jnp.where(mine_ref[0] == 1, own.astype(F32), other.astype(F32))


def split3(value):
    high = value.astype(BF16).astype(F32)
    mid = (value - high).astype(BF16).astype(F32)
    return high, mid, value - high - mid


def pack_stage(x_own, gains):
    rows, tokens, _ = x_own.shape

    def kernel(x_ref, gain_a_ref, gain_b_ref, out_ref):
        row = lax.broadcasted_iota(jnp.int32, (rows, tokens), 0)
        squares = jnp.zeros((rows, tokens), F32)
        for p in range(rows):
            squares = jnp.where(row == p, squares_by_lane([x_ref[p]]), squares)
        gain_rows = jnp.zeros((rows, BLK), F32)
        for b, gain_ref in enumerate((gain_a_ref, gain_b_ref)):
            for part, value in enumerate(split3(gain_ref[...])):
                gain_rows = jnp.where(row == b * 3 + part, value, gain_rows)
        planes = jnp.concatenate([*split3(squares), gain_rows], axis=0).astype(BF16)
        for p in range(rows):
            out_ref[p, :tokens] = x_ref[p]
            out_ref[p, tokens:] = planes

    return pl.pallas_call(
        kernel,
        out_shape=shape_of((rows, tokens + 4 * rows, BLK)),
        compiler_params=params(),
    )(x_own, *gains)


def right_stage(x_chan, gain_local, right, mine, groups, shared=None):
    rows = right[0].shape[0]
    tokens = right[0].shape[1]
    width = tokens // groups
    operands = [mine, *right, x_chan, gain_local] + ([] if shared is None else [shared])

    def kernel(mine_ref, own_ref, other_ref, x_ref, gain_ref, *refs):
        out_ref = refs[-1]
        if shared is not None:
            squares = jnp.zeros((rows, tokens), F32)
            for z in range(shared.shape[0]):
                planes = refs[0][z, tokens:].astype(F32)
                for part in range(3):
                    squares = squares + planes[part * rows : (part + 1) * rows]
        for p in range(rows):
            if shared is None:
                extra = x_ref[p, tokens : tokens + EXTRA].astype(F32)
                total = extra[0:1] + extra[1:2] + extra[2:3]
            else:
                total = squares[p : p + 1]
            scale = lax.rsqrt(total / D + EPS)
            right_row = choose(mine_ref, own_ref[p], other_ref[p])
            scaled = (right_row * scale).astype(BF16)
            mix = dot(scaled, x_ref[p, :tokens]) * gain_ref[...]
            out_ref[:, p] = mix.astype(BF16).reshape(groups, width, BLK)

    return pl.pallas_call(
        kernel,
        in_specs=[scalar_spec()] + [whole(o.shape) for o in operands[1:]],
        out_shape=shape_of((groups, rows, width, BLK)),
        compiler_params=params(),
    )(*operands)


def left_stage(left, mine, mix):
    j_count, i_count, p_count = left[0].shape

    half = BLK // 2

    def kernel(mine_ref, own_ref, other_ref, mix_ref, out_ref, wide_ref, acc_ref):
        for h in range(2):
            wide_ref[h] = mix_ref[:, h * half : (h + 1) * half].astype(F32)
        for j in range(j_count):
            column = jnp.concatenate(
                [wide_ref[h, pl.ds(j, p_count, stride=j_count), :] for h in range(2)], axis=1
            ).astype(BF16)
            factor = choose(mine_ref, own_ref[j], other_ref[j]).astype(BF16)
            mixed = dot(factor, column)
            for h in range(2):
                acc_ref[h, pl.ds(j, i_count, stride=j_count), :] = mixed[:, h * half : (h + 1) * half]
        for h in range(2):
            out_ref[:, h * half : (h + 1) * half] = acc_ref[h].astype(BF16)

    return pl.pallas_call(
        kernel,
        in_specs=[scalar_spec()] + [whole(a.shape) for a in (*left, mix)],
        out_shape=shape_of((i_count * j_count, BLK)),
        scratch_shapes=[
            pltpu.VMEM((2, p_count * j_count, half), F32),
            pltpu.VMEM((2, i_count * j_count, half), F32),
        ],
        compiler_params=params(),
    )(mine, *left, mix)


def spread_first(mine_ref, first_refs, spread_ref):
    lane = lax.broadcasted_iota(jnp.int32, (BLK, PER * BLK), 1)
    wanted = (lane // BLK) * C2 + lane % C2
    pick = (wanted == lax.broadcasted_iota(jnp.int32, (BLK, PER * BLK), 0)).astype(BF16)
    for g in range(C1 // PER):
        group = [f[g * PER : (g + 1) * PER].reshape(BLK, C2) for f in first_refs]
        spread = lax.dot_general(
            choose(mine_ref, *group).astype(BF16),
            pick,
            (((0,), (0,)), ((), ())),
            preferred_element_type=F32,
        ).astype(BF16)
        for r in range(PER):
            spread_ref[g * PER + r] = spread[:, r * BLK : (r + 1) * BLK]


def map_rows(spread_ref, second, r):
    return (spread_ref[r].astype(F32) * second[r : r + 1]).astype(BF16)


def factor_specs():
    return (
        [scalar_spec()]
        + [whole((C1, C2, C2))] * 2
        + [pl.BlockSpec((C1, BLK), lambda n: (0, n))] * 2
    )


def mix_channels(values_ref, spread_ref, second, map_refs):
    span = D // len(map_refs)
    total = jnp.zeros((values_ref.shape[0], BLK), F32)
    for part, map_ref in enumerate(map_refs):
        for r in range(span // C2):
            map_ref[r * C2 : (r + 1) * C2] = map_rows(spread_ref, second, part * span // C2 + r)
        total = total + dot(values_ref[:, part * span : (part + 1) * span], map_ref[...])
    return total.astype(BF16)


def map_scratch():
    return [pltpu.VMEM((C1, C2, BLK), BF16)] + [pltpu.VMEM((D // PARTS, BLK), BF16)] * PARTS


def normalize(x_blocks, gain_ref, tokens, store):
    total = jnp.zeros((tokens, 1), F32)
    for x in x_blocks:
        xf = x.astype(F32)
        total = total + jnp.sum(xf * xf, axis=1, keepdims=True)
    scale = lax.rsqrt(total / D + EPS)
    for n, x in enumerate(x_blocks):
        store(n, (x.astype(F32) * scale * gain_ref[n]).astype(BF16))


def token_stage(x_tok, gain, tokens):
    n_blk = x_tok.shape[0]

    def kernel(gain_ref, x_ref, normed_ref):
        def store(n, value):
            normed_ref[:, n * BLK : (n + 1) * BLK] = value

        normalize([x_ref[n, :tokens] for n in range(n_blk)], gain_ref, tokens, store)

    return pl.pallas_call(
        kernel,
        out_shape=shape_of((tokens, D)),
        compiler_params=params(),
    )(gain, x_tok)


def gate_stage(normed, first, second, mine, n_blk):
    tokens = normed.shape[0]

    def kernel(mine_ref, first_a, first_b, second_a, second_b, normed_ref, out_ref, *scratch):
        spread_ref, *map_refs = scratch

        @pl.when(pl.program_id(0) == 0)
        def _():
            spread_first(mine_ref, (first_a, first_b), spread_ref)

        second_rows = choose(mine_ref, second_a[...], second_b[...])
        pre = mix_channels(normed_ref, spread_ref, second_rows, map_refs)
        out_ref[0] = jax.nn.sigmoid(pre.astype(F32))

    return pl.pallas_call(
        kernel,
        grid=(n_blk,),
        in_specs=factor_specs() + [whole(normed.shape)],
        out_specs=pl.BlockSpec((1, tokens, BLK), lambda n: (n, 0, 0)),
        out_shape=shape_of((n_blk, tokens, BLK), F32),
        scratch_shapes=map_scratch(),
        compiler_params=params(),
    )(mine, *first, *second, normed)


def out_stage(seq_out, gate, x_tok, first, second, mine, gain=None):
    groups, n_blk, width, _ = seq_out.shape
    tokens = groups * width
    height = tokens + (0 if gain is None else EXTRA)

    def kernel(mine_ref, first_a, first_b, second_a, second_b, seq_ref, gate_ref, x_ref, *refs):
        n = pl.program_id(0)
        gated_ref, spread_ref, *map_refs = refs[-2 - PARTS :]
        if gain is None:
            rows_ref, res_ref = refs[:2]
        else:
            gain_ref, rows_ref, res_ref, normed_ref = refs[:4]

        @pl.when(n == 0)
        def _():
            spread_first(mine_ref, (first_a, first_b), spread_ref)
            for z in range(n_blk):
                seq = seq_ref[:, z].reshape(tokens, BLK).astype(F32)
                gated_ref[:, z * BLK : (z + 1) * BLK] = (seq * gate_ref[z]).astype(BF16)

        second_rows = choose(mine_ref, second_a[...], second_b[...])
        mixed = mix_channels(gated_ref, spread_ref, second_rows, map_refs).astype(F32)
        res_ref[n, :tokens] = (x_ref[n, :tokens].astype(F32) + mixed).astype(BF16)

        @pl.when(n == n_blk - 1)
        def _():
            blocks = [res_ref[z, :tokens] for z in range(n_blk)]
            for z in range(n_blk):
                for q in range(tokens // STRIDE):
                    rows_ref[q : q + 1, z * BLK : (z + 1) * BLK] = blocks[z][
                        q * STRIDE : q * STRIDE + 1
                    ]
            if gain is None:
                return

            def store(z, value):
                normed_ref[:, z * BLK : (z + 1) * BLK] = value

            normalize(blocks, gain_ref, tokens, store)
            total = squares_by_lane(blocks)
            total = jnp.concatenate([total, total], axis=0)
            high, mid, low = split3(total)
            row = lax.broadcasted_iota(jnp.int32, (EXTRA, tokens), 0)
            rest = jnp.where(row == 1, mid, jnp.where(row == 2, low, 0.0))
            packed = jnp.where(row == 0, high, rest).astype(BF16)
            for z in range(n_blk):
                res_ref[z, tokens : tokens + EXTRA] = packed

    in_specs = factor_specs() + [whole(a.shape) for a in (seq_out, gate, x_tok)]
    operands = [mine, *first, *second, seq_out, gate, x_tok]
    out_shape = [shape_of((tokens // STRIDE, D)), shape_of((n_blk, height, BLK))]
    if gain is not None:
        operands.append(gain)
        in_specs.append(whole(gain.shape))
        out_shape.append(shape_of((tokens, D)))
    return pl.pallas_call(
        kernel,
        grid=(n_blk,),
        in_specs=in_specs,
        out_specs=[whole(s.shape) for s in out_shape],
        out_shape=out_shape,
        scratch_shapes=[pltpu.VMEM((tokens, D), BF16)] + map_scratch(),
        compiler_params=params(),
    )(*operands)


def score_stage(row_sets, heads, labels, places):
    x_count = len(row_sets)
    per_set = row_sets[0].shape[0]
    count = x_count * per_set
    width = heads[0].shape[1]

    def kernel(place_ref, label_ref, *refs):
        out_ref, rows_ref = refs[-2:]
        head_refs = refs[x_count : x_count + len(heads)]
        for d in range(x_count):
            rows_ref[place_ref[d]] = refs[d][...]
        rows = rows_ref[...].reshape(count, D)
        exp_sum = jnp.zeros((count, 1), F32)
        target = jnp.zeros((count, 1), F32)
        for d, head_ref in enumerate(head_refs):
            logits = dot(rows, head_ref[...])
            column = lax.broadcasted_iota(jnp.int32, (count, width), 1) + place_ref[x_count + d]
            exp_sum = exp_sum + jnp.sum(jnp.exp(logits), axis=1, keepdims=True)
            target = target + jnp.sum(
                jnp.where(column == label_ref[...], logits, 0.0), axis=1, keepdims=True
            )
        row = lax.broadcasted_iota(jnp.int32, (count, count), 0)
        lane = lax.broadcasted_iota(jnp.int32, (count, count), 1)
        out_ref[0:1] = jnp.sum(jnp.where(lane == row, exp_sum, 0.0), axis=0, keepdims=True)
        out_ref[1:2] = jnp.sum(jnp.where(lane == row, target, 0.0), axis=0, keepdims=True)

    return pl.pallas_call(
        kernel,
        in_specs=[scalar_spec(), whole(labels.shape)]
        + [whole(r.shape) for r in row_sets]
        + [whole(h.shape) for h in heads],
        out_shape=shape_of((2, count), F32),
        scratch_shapes=[pltpu.VMEM((x_count, per_set, D), BF16)],
        compiler_params=params(),
    )(places, labels, *row_sets, *heads)


def loss_stage(parts, x_count, y_count):
    count = parts.shape[-1]
    ring = count // (2 * x_count)

    def kernel(parts_ref, out_ref):
        by_place = parts_ref[...].reshape(x_count, y_count, -1, 2, count)
        total = jnp.sum(jnp.sum(by_place, axis=2), axis=0)
        losses = jnp.log(total[:, 0]) - total[:, 1]
        for m in range(2):
            for x in range(x_count):
                at = (x * 2 + m) * ring
                out_ref[m, x] = losses[:, at : at + ring]

    return pl.pallas_call(
        kernel,
        out_shape=shape_of((2, x_count, y_count, ring), F32),
        compiler_params=params(),
    )(parts)


def result_stage(section, chan_one, got_one, got_two, chan_two, tokens):
    rows = chan_one.shape[0]

    def kernel(section_ref, *refs):
        out_ref = refs[-1]

        @pl.when(section_ref[0] == 0)
        def _():
            out_ref[0] = refs[0][...]
            out_ref[1] = refs[1][...]

        @pl.when(section_ref[0] != 0)
        def _():
            out_ref[0] = refs[2][...]
            out_ref[1] = refs[3][...]

    return pl.pallas_call(
        kernel,
        grid=(rows,),
        in_specs=[scalar_spec()] + [pl.BlockSpec((1, tokens, BLK), lambda p: (p, 0, 0))] * 4,
        out_specs=pl.BlockSpec((2, 1, tokens, BLK), lambda p: (0, p, 0, 0)),
        out_shape=shape_of((2, rows, tokens, BLK)),
        compiler_params=params(),
    )(section, chan_one, got_one, got_two, chan_two)


def body(
    x_in,
    norm_gain,
    right_blocks,
    left_blocks,
    gate_first,
    gate_second,
    out_first,
    out_second,
    head,
    targets,
):
    section = lax.axis_index("section")
    first = section == 0
    tensor_index = lax.axis_index("tensor")
    z_scalar = tensor_index.astype(jnp.int32).reshape(1)
    seq_count = lax.axis_size("seq")
    y_count = 4
    x_count = seq_count // y_count
    n_blk = lax.axis_size("tensor")
    everyone = ("seq", "tensor")
    swap = [(0, 1), (1, 0)]
    rows_dev, tokens = right_blocks.shape[1], right_blocks.shape[2]
    j_dev = left_blocks.shape[1]
    p_count = left_blocks.shape[2]

    mine = [(section == b).astype(jnp.int32).reshape(1) for b in range(2)]

    def with_other(own):
        return own, lax.ppermute(own, "section", swap)

    def along_y(block, distance):
        route = [(i, i - i % y_count + (i + distance) % y_count) for i in range(seq_count)]
        return lax.ppermute(block, "seq", route)

    def along_x(block, distance):
        route = [(i, (i + distance * y_count) % seq_count) for i in range(seq_count)]
        return lax.ppermute(block, "seq", route)

    def rows_second(factor):
        return jnp.transpose(factor[0], (2, 1, 0)).reshape(C1, D)

    tie = lax.optimization_barrier

    x_own = lax.dynamic_index_in_dim(x_in, section, 0, keepdims=False).reshape(
        rows_dev, tokens, BLK
    )
    gain_other = lax.ppermute(norm_gain, "section", swap)
    gain_local = [jnp.where(section == b, norm_gain, gain_other) for b in range(2)]

    packed = pack_stage(x_own, gain_local)
    packed, right_own, left_own, gate_own, out_own, gate_sec, out_sec, head_own = tie(
        (
            packed,
            right_blocks[0],
            left_blocks[0],
            gate_first[0],
            out_first[0],
            gate_second,
            out_second,
            head[0],
        )
    )
    right, left, gate_first_pair, out_first_pair = (
        with_other(w) for w in (right_own, left_own, gate_own, out_own)
    )
    gate_second_pair, out_second_pair = (with_other(rows_second(w)) for w in (gate_sec, out_sec))
    left, head_own = tie((left, head_own))
    near_heads = [along_y(head_own, d) for d in (1, 3)]
    x_tok = lax.all_to_all(packed, "tensor", split_axis=0, concat_axis=0, tiled=True)
    gain_rows = x_tok[:, tokens + 3 * rows_dev :][:, :6].astype(F32)
    gain_rows = jnp.sum(gain_rows.reshape(n_blk, 2, 3, BLK), axis=2)
    gains = [gain_rows[:, b : b + 1] for b in range(2)]

    def exchange_seq(mix):
        return lax.all_to_all(mix, "seq", split_axis=0, concat_axis=0, tiled=True)

    def mix_left(cols, b):
        out = left_stage(left, mine[b], cols.reshape(p_count * j_dev, BLK))
        return out.reshape(p_count, j_dev, BLK)

    def exchange_all(cols):
        out = lax.all_to_all(cols, everyone, split_axis=0, concat_axis=0, tiled=True)
        return out.reshape(seq_count, n_blk, j_dev, BLK)

    mix = right_stage(x_own, gain_local[0], right, mine[0], seq_count, shared=x_tok)
    mix, near_heads, left, gate_first_pair, out_first_pair, gate_second_pair, out_second_pair = tie(
        (mix, near_heads, left, gate_first_pair, out_first_pair, gate_second_pair, out_second_pair)
    )
    cols = exchange_seq(mix)

    seq_out = exchange_all(mix_left(cols, 0))
    normed = token_stage(x_tok, gains[0], tokens)
    gate = gate_stage(normed, gate_first_pair, gate_second_pair, mine[0], n_blk)
    rows_one, packed, normed = out_stage(
        seq_out, gate, x_tok, out_first_pair, out_second_pair, mine[0], gain=gains[1]
    )

    packed, normed, head_own, gate_first_pair, out_first_pair = tie(
        (packed, normed, head_own, gate_first_pair, out_first_pair)
    )
    far_head = along_y(head_own, 2)
    chan_one = lax.all_to_all(packed, "tensor", split_axis=0, concat_axis=0, tiled=True)
    gate = gate_stage(normed, gate_first_pair, gate_second_pair, mine[1], n_blk)
    mix = right_stage(chan_one, gain_local[1], right, mine[1], seq_count)
    mix, gate, far_head = tie((mix, gate, far_head))
    heads = [head_own, near_heads[0], far_head, near_heads[1]]
    seq_out = exchange_all(mix_left(exchange_seq(mix), 1))
    rows_two, result = out_stage(
        seq_out, gate, packed, out_first_pair, out_second_pair, mine[1]
    )

    pair = jnp.stack([rows_one, rows_two])[:, None]
    pair = jnp.broadcast_to(pair, (2, n_blk) + rows_two.shape).reshape((-1,) + rows_two.shape)
    rows = lax.all_to_all(pair, ("section", "tensor"), split_axis=0, concat_axis=0, tiled=True)
    rows, result = tie((rows, result))
    chan_two = lax.all_to_all(result, "tensor", split_axis=0, concat_axis=0, tiled=True)

    rows = rows.reshape(-1, D)
    row_sets = [rows] + [along_x(rows, d) for d in range(1, x_count)]
    seq_index = lax.axis_index("seq").astype(jnp.int32)
    x_index, y_index = seq_index // y_count, seq_index % y_count
    vocab_dev = head.shape[2]
    labels = targets.reshape(2, x_count, y_count, -1)
    labels = lax.dynamic_index_in_dim(labels, y_index, 2, keepdims=False)
    labels = jnp.transpose(labels, (1, 0, 2)).reshape(-1, 1)
    places = [(x_index + x_count - d) % x_count for d in range(x_count)]
    for d in range(y_count):
        source = x_index * y_count + (y_index + y_count - d) % y_count
        places.append((source * n_blk + z_scalar[0]) * vocab_dev)
    parts = score_stage(row_sets, heads, labels, jnp.stack(places))
    parts, chan_two = tie((parts, chan_two))
    sums = gather_by_exchange(parts, everyone)

    got_one = lax.ppermute(chan_one, "section", [(1, 0)])
    got_two = lax.ppermute(chan_two, "section", [(0, 1)])
    scalar = section.astype(jnp.int32).reshape(1)
    block_out = result_stage(scalar, chan_one, got_one, got_two, chan_two, tokens)
    sums, block_out = tie((sums, block_out))
    aux_losses = loss_stage(sums, x_count, y_count).reshape(1, 2, -1)
    block_out = block_out.reshape(1, 2, rows_dev * tokens, BLK)
    return (block_out, aux_losses)


def solution(mesh):
    in_specs = (
        P(None, "seq", "tensor"),
        P("section", "tensor"),
        P("section", "seq", None, None),
        P("section", "seq", None, None),
        P("section", None, None, None),
        P("section", None, None, None),
        P("section", None, None, None),
        P("section", None, None, None),
        P("section", None, ("seq", "tensor")),
        P(),
    )
    out_specs = (P("section", None, "seq", "tensor"), P("section", None, None))
    return jax.shard_map(body, mesh=mesh, in_specs=in_specs, out_specs=out_specs, check_vma=False)
```

```python
import jax
import jax.numpy as jnp
from jax import lax
from jax.experimental import pallas as pl
from jax.experimental.pallas import tpu as pltpu
from jax.sharding import PartitionSpec as P

C1 = 32
C2 = 64
D = 2048
STRIDE = 128
EPS = 1e-05
BLK = 256
EXTRA = 16
PER = BLK // C2
VMEM_LIMIT = 48 * 1024 * 1024
F32 = jnp.float32
BF16 = jnp.bfloat16


def params():
    return pltpu.CompilerParams(vmem_limit_bytes=VMEM_LIMIT)


def whole(shape):
    return pl.BlockSpec(shape, lambda *_: (0,) * len(shape))


def scalar_spec():
    return pl.BlockSpec(memory_space=pltpu.SMEM)


def shape_of(shape, dtype=BF16):
    return jax.ShapeDtypeStruct(shape, dtype)


def dot(a, b):
    return jnp.dot(a, b, preferred_element_type=F32)


def gather_by_exchange(block, axis):
    count = lax.axis_size(axis)
    copies = jnp.broadcast_to(block[None], (count,) + block.shape)
    return lax.all_to_all(copies, axis, split_axis=0, concat_axis=0, tiled=True)


def squares_by_lane(x_blocks):
    ones = jnp.ones((8, BLK), BF16)
    dims = (((1,), (1,)), ((), ()))
    total = None
    for x in x_blocks:
        xf = x.astype(F32)
        square = xf * xf
        high = square.astype(BF16)
        low = (square - high.astype(F32)).astype(BF16)
        part = lax.dot_general(ones, high, dims, preferred_element_type=F32) + lax.dot_general(
            ones, low, dims, preferred_element_type=F32
        )
        total = part if total is None else total + part
    return total


def split3(value):
    high = value.astype(BF16).astype(F32)
    mid = (value - high).astype(BF16).astype(F32)
    return high, mid, value - high - mid


def pack_stage(x_own, gains):
    rows, tokens, _ = x_own.shape

    def kernel(x_ref, gain_a_ref, gain_b_ref, out_ref):
        row = lax.broadcasted_iota(jnp.int32, (rows, tokens), 0)
        squares = jnp.zeros((rows, tokens), F32)
        for p in range(rows):
            squares = jnp.where(row == p, squares_by_lane([x_ref[p]]), squares)
        gain_rows = jnp.zeros((rows, BLK), F32)
        for b, gain_ref in enumerate((gain_a_ref, gain_b_ref)):
            for part, value in enumerate(split3(gain_ref[...])):
                gain_rows = jnp.where(row == b * 3 + part, value, gain_rows)
        planes = jnp.concatenate([*split3(squares), gain_rows], axis=0).astype(BF16)
        for p in range(rows):
            out_ref[p, :tokens] = x_ref[p]
            out_ref[p, tokens:] = planes

    return pl.pallas_call(
        kernel,
        out_shape=shape_of((rows, tokens + 4 * rows, BLK)),
        compiler_params=params(),
    )(x_own, *gains)


def right_stage(x_chan, gain_local, right, groups, shared=None):
    rows = right.shape[0]
    tokens = right.shape[1]
    width = tokens // groups
    operands = [x_chan, gain_local, right] + ([] if shared is None else [shared])

    def kernel(x_ref, gain_ref, right_ref, *refs):
        out_ref = refs[-1]
        if shared is not None:
            squares = jnp.zeros((rows, tokens), F32)
            for z in range(shared.shape[0]):
                planes = refs[0][z, tokens:].astype(F32)
                for part in range(3):
                    squares = squares + planes[part * rows : (part + 1) * rows]
        for p in range(rows):
            if shared is None:
                extra = x_ref[p, tokens : tokens + EXTRA].astype(F32)
                total = extra[0:1] + extra[1:2] + extra[2:3]
            else:
                total = squares[p : p + 1]
            scale = lax.rsqrt(total / D + EPS)
            scaled = (right_ref[p].astype(F32) * scale).astype(BF16)
            mix = dot(scaled, x_ref[p, :tokens]) * gain_ref[...]
            out_ref[:, p] = mix.astype(BF16).reshape(groups, width, BLK)

    return pl.pallas_call(
        kernel,
        out_shape=shape_of((groups, rows, width, BLK)),
        compiler_params=params(),
    )(*operands)


def left_stage(left, mix):
    j_count, i_count, p_count = left.shape

    half = BLK // 2

    def kernel(left_ref, mix_ref, out_ref, wide_ref, acc_ref):
        for h in range(2):
            wide_ref[h] = mix_ref[:, h * half : (h + 1) * half].astype(F32)
        for j in range(j_count):
            column = jnp.concatenate(
                [wide_ref[h, pl.ds(j, p_count, stride=j_count), :] for h in range(2)], axis=1
            ).astype(BF16)
            mixed = dot(left_ref[j], column)
            for h in range(2):
                acc_ref[h, pl.ds(j, i_count, stride=j_count), :] = mixed[:, h * half : (h + 1) * half]
        for h in range(2):
            out_ref[:, h * half : (h + 1) * half] = acc_ref[h].astype(BF16)

    return pl.pallas_call(
        kernel,
        out_shape=shape_of((i_count * j_count, BLK)),
        scratch_shapes=[
            pltpu.VMEM((2, p_count * j_count, half), F32),
            pltpu.VMEM((2, i_count * j_count, half), F32),
        ],
        compiler_params=params(),
    )(left, mix)


def channel_map(first, second_rows, n_blk):
    def kernel(first_ref, second_ref, out_ref, spread_ref):
        @pl.when(pl.program_id(0) == 0)
        def _():
            lane = lax.broadcasted_iota(jnp.int32, (BLK, PER * BLK), 1)
            wanted = (lane // BLK) * C2 + lane % C2
            pick = (wanted == lax.broadcasted_iota(jnp.int32, (BLK, PER * BLK), 0)).astype(BF16)
            for g in range(C1 // PER):
                spread = lax.dot_general(
                    first_ref[g * PER : (g + 1) * PER].reshape(BLK, C2),
                    pick,
                    (((0,), (0,)), ((), ())),
                    preferred_element_type=F32,
                ).astype(BF16)
                for r in range(PER):
                    spread_ref[g * PER + r] = spread[:, r * BLK : (r + 1) * BLK]

        for r in range(C1):
            row = second_ref[r : r + 1].astype(F32)
            out_ref[0, r * C2 : (r + 1) * C2] = (spread_ref[r].astype(F32) * row).astype(BF16)

    return pl.pallas_call(
        kernel,
        grid=(n_blk,),
        in_specs=[whole((C1, C2, C2)), pl.BlockSpec((C1, BLK), lambda n: (0, n))],
        out_specs=pl.BlockSpec((1, D, BLK), lambda n: (n, 0, 0)),
        out_shape=shape_of((n_blk, D, BLK)),
        scratch_shapes=[pltpu.VMEM((C1, C2, BLK), BF16)],
        compiler_params=params(),
    )(first, second_rows)


def normalize(x_blocks, gain_ref, tokens, store):
    total = jnp.zeros((tokens, 1), F32)
    for x in x_blocks:
        xf = x.astype(F32)
        total = total + jnp.sum(xf * xf, axis=1, keepdims=True)
    scale = lax.rsqrt(total / D + EPS)
    for n, x in enumerate(x_blocks):
        store(n, (x.astype(F32) * scale * gain_ref[n]).astype(BF16))


def token_stage(x_tok, gain, tokens):
    n_blk = x_tok.shape[0]

    def kernel(gain_ref, x_ref, normed_ref):
        def store(n, value):
            normed_ref[:, n * BLK : (n + 1) * BLK] = value

        normalize([x_ref[n, :tokens] for n in range(n_blk)], gain_ref, tokens, store)

    return pl.pallas_call(
        kernel,
        out_shape=shape_of((tokens, D)),
        compiler_params=params(),
    )(gain, x_tok)


def gate_stage(normed, gate_map):
    tokens = normed.shape[0]
    n_blk = gate_map.shape[0]

    def kernel(normed_ref, map_ref, out_ref):
        pre = dot(normed_ref[...], map_ref[0]).astype(BF16)
        out_ref[0] = jax.nn.sigmoid(pre.astype(F32))

    return pl.pallas_call(
        kernel,
        grid=(n_blk,),
        in_specs=[whole(normed.shape), pl.BlockSpec((1, D, BLK), lambda n: (n, 0, 0))],
        out_specs=pl.BlockSpec((1, tokens, BLK), lambda n: (n, 0, 0)),
        out_shape=shape_of((n_blk, tokens, BLK), F32),
        compiler_params=params(),
    )(normed, gate_map)


def out_stage(seq_out, gate, x_tok, out_map, with_squares):
    groups, n_blk, width, _ = seq_out.shape
    tokens = groups * width
    height = tokens + (EXTRA if with_squares else 0)

    def kernel(seq_ref, gate_ref, x_ref, map_ref, *refs):
        n = pl.program_id(0)
        rows_ref, res_ref, gated_ref = refs

        @pl.when(n == 0)
        def _():
            for z in range(n_blk):
                seq = seq_ref[:, z].reshape(tokens, BLK).astype(F32)
                gated_ref[:, z * BLK : (z + 1) * BLK] = (seq * gate_ref[z]).astype(BF16)

        mixed = dot(gated_ref[...], map_ref[0]).astype(BF16).astype(F32)
        res_ref[n, :tokens] = (x_ref[n, :tokens].astype(F32) + mixed).astype(BF16)

        @pl.when(n == n_blk - 1)
        def _():
            blocks = [res_ref[z, :tokens] for z in range(n_blk)]
            for z in range(n_blk):
                for q in range(tokens // STRIDE):
                    rows_ref[q : q + 1, z * BLK : (z + 1) * BLK] = blocks[z][
                        q * STRIDE : q * STRIDE + 1
                    ]
            if not with_squares:
                return
            total = squares_by_lane(blocks)
            total = jnp.concatenate([total, total], axis=0)
            high, mid, low = split3(total)
            row = lax.broadcasted_iota(jnp.int32, (EXTRA, tokens), 0)
            rest = jnp.where(row == 1, mid, jnp.where(row == 2, low, 0.0))
            packed = jnp.where(row == 0, high, rest).astype(BF16)
            for z in range(n_blk):
                res_ref[z, tokens : tokens + EXTRA] = packed

    in_specs = [
        whole(seq_out.shape),
        whole(gate.shape),
        whole(x_tok.shape),
        pl.BlockSpec((1, D, BLK), lambda n: (n, 0, 0)),
    ]
    operands = [seq_out, gate, x_tok, out_map]
    out_shape = [shape_of((tokens // STRIDE, D)), shape_of((n_blk, height, BLK))]
    return pl.pallas_call(
        kernel,
        grid=(n_blk,),
        in_specs=in_specs,
        out_specs=[whole(s.shape) for s in out_shape],
        out_shape=out_shape,
        scratch_shapes=[pltpu.VMEM((tokens, D), BF16)],
        compiler_params=params(),
    )(*operands)


def score_stage(row_sets, heads, labels, places):
    x_count = len(row_sets)
    per_set = row_sets[0].shape[0]
    count = x_count * per_set
    width = heads[0].shape[1]

    def kernel(place_ref, label_ref, *refs):
        out_ref, rows_ref = refs[-2:]
        head_refs = refs[x_count : x_count + len(heads)]
        for d in range(x_count):
            rows_ref[place_ref[d]] = refs[d][...]
        rows = rows_ref[...].reshape(count, D)
        exp_sum = jnp.zeros((count, 1), F32)
        target = jnp.zeros((count, 1), F32)
        for d, head_ref in enumerate(head_refs):
            logits = dot(rows, head_ref[...])
            column = lax.broadcasted_iota(jnp.int32, (count, width), 1) + place_ref[x_count + d]
            exp_sum = exp_sum + jnp.sum(jnp.exp(logits), axis=1, keepdims=True)
            target = target + jnp.sum(
                jnp.where(column == label_ref[...], logits, 0.0), axis=1, keepdims=True
            )
        row = lax.broadcasted_iota(jnp.int32, (count, count), 0)
        lane = lax.broadcasted_iota(jnp.int32, (count, count), 1)
        out_ref[0:1] = jnp.sum(jnp.where(lane == row, exp_sum, 0.0), axis=0, keepdims=True)
        out_ref[1:2] = jnp.sum(jnp.where(lane == row, target, 0.0), axis=0, keepdims=True)

    return pl.pallas_call(
        kernel,
        in_specs=[scalar_spec(), whole(labels.shape)]
        + [whole(r.shape) for r in row_sets]
        + [whole(h.shape) for h in heads],
        out_shape=shape_of((2, count), F32),
        scratch_shapes=[pltpu.VMEM((x_count, per_set, D), BF16)],
        compiler_params=params(),
    )(places, labels, *row_sets, *heads)


def loss_stage(parts, x_count, y_count):
    count = parts.shape[-1]
    ring = count // (2 * x_count)

    def kernel(parts_ref, out_ref):
        by_place = parts_ref[...].reshape(x_count, y_count, -1, 2, count)
        total = jnp.sum(jnp.sum(by_place, axis=2), axis=0)
        losses = jnp.log(total[:, 0]) - total[:, 1]
        for m in range(2):
            for x in range(x_count):
                at = (x * 2 + m) * ring
                out_ref[m, x] = losses[:, at : at + ring]

    return pl.pallas_call(
        kernel,
        out_shape=shape_of((2, x_count, y_count, ring), F32),
        compiler_params=params(),
    )(parts)


def result_stage(section, chan_one, got_one, got_two, chan_two, tokens):
    rows = chan_one.shape[0]

    def kernel(section_ref, *refs):
        out_ref = refs[-1]

        @pl.when(section_ref[0] == 0)
        def _():
            out_ref[0] = refs[0][...]
            out_ref[1] = refs[1][...]

        @pl.when(section_ref[0] != 0)
        def _():
            out_ref[0] = refs[2][...]
            out_ref[1] = refs[3][...]

    return pl.pallas_call(
        kernel,
        grid=(rows,),
        in_specs=[scalar_spec()] + [pl.BlockSpec((1, tokens, BLK), lambda p: (p, 0, 0))] * 4,
        out_specs=pl.BlockSpec((2, 1, tokens, BLK), lambda p: (0, p, 0, 0)),
        out_shape=shape_of((2, rows, tokens, BLK)),
        compiler_params=params(),
    )(section, chan_one, got_one, got_two, chan_two)


def body(
    x_in,
    norm_gain,
    right_blocks,
    left_blocks,
    gate_first,
    gate_second,
    out_first,
    out_second,
    head,
    targets,
):
    section = lax.axis_index("section")
    first = section == 0
    tensor_index = lax.axis_index("tensor")
    z_scalar = tensor_index.astype(jnp.int32).reshape(1)
    seq_count = lax.axis_size("seq")
    y_count = 4
    x_count = seq_count // y_count
    n_blk = lax.axis_size("tensor")
    everyone = ("seq", "tensor")
    swap = [(0, 1), (1, 0)]
    rows_dev, tokens = right_blocks.shape[1], right_blocks.shape[2]
    j_dev = left_blocks.shape[1]
    p_count = left_blocks.shape[2]

    def by_block(own):
        other = lax.ppermute(own, "section", swap)
        return jnp.where(first, own, other), jnp.where(first, other, own)

    def along_y(block, distance):
        route = [(i, i - i % y_count + (i + distance) % y_count) for i in range(seq_count)]
        return lax.ppermute(block, "seq", route)

    def along_x(block, distance):
        route = [(i, (i + distance * y_count) % seq_count) for i in range(seq_count)]
        return lax.ppermute(block, "seq", route)

    def rows_second(factor):
        return jnp.transpose(factor[0], (2, 1, 0)).reshape(C1, D)

    tie = lax.optimization_barrier

    x_own = lax.dynamic_index_in_dim(x_in, section, 0, keepdims=False).reshape(
        rows_dev, tokens, BLK
    )
    gain_local = by_block(norm_gain)

    packed = pack_stage(x_own, gain_local)
    packed, *own = tie(
        (
            packed,
            right_blocks[0],
            left_blocks[0],
            gate_first[0],
            out_first[0],
            gate_second,
            out_second,
            head[0],
        )
    )
    rights, lefts, gate_firsts, out_firsts = (by_block(w) for w in own[:4])
    gate_seconds, out_seconds = (by_block(rows_second(w)) for w in own[4:6])
    lefts, head_own = tie((lefts, own[6]))
    heads = [head_own, along_y(head_own, 1), None, along_y(head_own, 3)]
    x_tok = lax.all_to_all(packed, "tensor", split_axis=0, concat_axis=0, tiled=True)
    gain_rows = x_tok[:, tokens + 3 * rows_dev :][:, :6].astype(F32)
    gain_rows = jnp.sum(gain_rows.reshape(n_blk, 2, 3, BLK), axis=2)
    gains = [gain_rows[:, b : b + 1] for b in range(2)]

    def exchange_seq(mix):
        return lax.all_to_all(mix, "seq", split_axis=0, concat_axis=0, tiled=True)

    def mix_left(cols, b):
        out = left_stage(lefts[b], cols.reshape(p_count * j_dev, BLK))
        return out.reshape(p_count, j_dev, BLK)

    def exchange_all(cols):
        out = lax.all_to_all(cols, everyone, split_axis=0, concat_axis=0, tiled=True)
        return out.reshape(seq_count, n_blk, j_dev, BLK)

    mix = right_stage(x_own, gain_local[0], rights[0], seq_count, shared=x_tok)
    mix, heads[1], heads[3], lefts, gate_firsts, out_firsts, gate_seconds, out_seconds = tie(
        (mix, heads[1], heads[3], lefts, gate_firsts, out_firsts, gate_seconds, out_seconds)
    )
    cols = exchange_seq(mix)

    cols = mix_left(cols, 0)
    cols, gate_firsts, out_firsts, gate_seconds, out_seconds = tie(
        (cols, gate_firsts, out_firsts, gate_seconds, out_seconds)
    )
    seq_out = exchange_all(cols)
    normed = token_stage(x_tok, gains[0], tokens)
    gate = gate_stage(normed, channel_map(gate_firsts[0], gate_seconds[0], n_blk))
    out_map = channel_map(out_firsts[0], out_seconds[0], n_blk)
    rows_one, packed = out_stage(seq_out, gate, x_tok, out_map, True)

    packed, heads[0], gate_two, out_two, gate_sec, out_sec = tie(
        (packed, heads[0], gate_firsts[1], out_firsts[1], gate_seconds[1], out_seconds[1])
    )
    heads[2] = along_y(heads[0], 2)
    chan_one = lax.all_to_all(packed, "tensor", split_axis=0, concat_axis=0, tiled=True)
    normed = token_stage(packed, gains[1], tokens)
    gate = gate_stage(normed, channel_map(gate_two, gate_sec, n_blk))
    out_map = channel_map(out_two, out_sec, n_blk)
    mix = right_stage(chan_one, gain_local[1], rights[1], seq_count)
    mix, gate, out_map, heads[2] = tie((mix, gate, out_map, heads[2]))
    seq_out = exchange_all(mix_left(exchange_seq(mix), 1))
    rows_two, result = out_stage(seq_out, gate, packed, out_map, False)

    pair = jnp.stack([rows_one, rows_two])[:, None]
    pair = jnp.broadcast_to(pair, (2, n_blk) + rows_two.shape).reshape((-1,) + rows_two.shape)
    rows = lax.all_to_all(pair, ("section", "tensor"), split_axis=0, concat_axis=0, tiled=True)
    rows, result = tie((rows, result))
    chan_two = lax.all_to_all(result, "tensor", split_axis=0, concat_axis=0, tiled=True)

    rows = rows.reshape(-1, D)
    row_sets = [rows] + [along_x(rows, d) for d in range(1, x_count)]
    seq_index = lax.axis_index("seq").astype(jnp.int32)
    x_index, y_index = seq_index // y_count, seq_index % y_count
    vocab_dev = head.shape[2]
    labels = targets.reshape(2, x_count, y_count, -1)
    labels = lax.dynamic_index_in_dim(labels, y_index, 2, keepdims=False)
    labels = jnp.transpose(labels, (1, 0, 2)).reshape(-1, 1)
    places = [(x_index + x_count - d) % x_count for d in range(x_count)]
    for d in range(y_count):
        source = x_index * y_count + (y_index + y_count - d) % y_count
        places.append((source * n_blk + z_scalar[0]) * vocab_dev)
    parts = score_stage(row_sets, heads, labels, jnp.stack(places))
    parts = jnp.broadcast_to(parts[None], (p_count,) + parts.shape)
    parts, chan_two = tie((parts, chan_two))
    sums = lax.all_to_all(parts, everyone, split_axis=0, concat_axis=0, tiled=True)

    got_one = lax.ppermute(chan_one, "section", [(1, 0)])
    got_two = lax.ppermute(chan_two, "section", [(0, 1)])
    scalar = section.astype(jnp.int32).reshape(1)
    block_out = result_stage(scalar, chan_one, got_one, got_two, chan_two, tokens)
    sums, block_out = tie((sums, block_out))
    aux_losses = loss_stage(sums, x_count, y_count).reshape(1, 2, -1)
    block_out = block_out.reshape(1, 2, rows_dev * tokens, BLK)
    return (block_out, aux_losses)


def solution(mesh):
    in_specs = (
        P(None, "seq", "tensor"),
        P("section", "tensor"),
        P("section", "seq", None, None),
        P("section", "seq", None, None),
        P("section", None, None, None),
        P("section", None, None, None),
        P("section", None, None, None),
        P("section", None, None, None),
        P("section", None, ("seq", "tensor")),
        P(),
    )
    out_specs = (P("section", None, "seq", "tensor"), P("section", None, None))
    return jax.shard_map(body, mesh=mesh, in_specs=in_specs, out_specs=out_specs, check_vma=False)
```
